32 devices in a mesh: groups: 2 (over x), ctx: 16 (over z, y, core).
Axes of the slice: x: 2, y: 2, z: 4, core: 2. Of those that a mesh axis runs over, the one named last changes fastest.
Arguments:
- tokens: bfloat16 [4096, 2880], P(('groups', 'ctx')), parts along dimension 0, may hold values from -6 to 6
- lengths: int32 [8], P('groups'), parts along dimension 0, may hold values from 1 to 1536, 2048 in all
- attn_gain: float32 [2880], replicated, may hold values from 0.1 to 1.9
- w_query: bfloat16 [2880, 2048], P('ctx'), may hold values from -2 to 2
- w_key: bfloat16 [2880, 256], replicated, may hold values from -1 to 1
- w_value: bfloat16 [2880, 256], replicated, may hold values from -0.109375 to 0.109375
- sinks: float32 [32], replicated, may hold values from -2 to 4
- w_out: bfloat16 [2048, 2880], P('ctx'), may hold values from -0.5 to 0.5
- moe_gain: float32 [2880], replicated, may hold values from 0.1 to 1.9
- routes: int32 [4096, 4], P(('groups', 'ctx')), parts along dimension 0, may hold values from 0 to 7, all different within a row; in each aligned block of 128 rows (0 to 127, 128 to 255, ...) at most 68 rows name the same one
- route_weights: float32 [4096, 4], P(('groups', 'ctx')), parts along dimension 0, may hold values from 0.05 to 1
- w_gate: bfloat16 [16, 2880, 768], P('ctx'), may hold values from -0.109375 to 0.109375
- w_up: bfloat16 [16, 2880, 768], P('ctx'), may hold values from -0.109375 to 0.109375
- w_down: bfloat16 [16, 768, 2880], P('ctx'), may hold values from -0.15625 to 0.15625
Outputs:
- result: bfloat16 [4096, 2880], P(('groups', 'ctx')), parts along dimension 0
The draws below stay inside these ranges and needn't reach their ends.
There are 2 independent parts, one for each index of `groups`. The reference program is written for one: setup_inputs(seed, part) draws one part's arguments, and reference() takes and returns one part's arrays. A program takes and returns all parts, laid end to end along the dimension named above; an argument that names none is the same for every part. Nothing has to cross between parts.
Inputs may be any that keep to these rules, and one draw needn't show every extreme that they name: lengths of the 4 requests packed in order into the 2048 tokens; they sum to 2048. `routes`: each token names 4 different experts; among the 128 tokens of one index of ctx no expert is named by more than 68 tokens, a bound that some block reaches.
All inputs are finite; a program needn't handle non-finite values.
Results may differ from the reference program's by a relative error of at most 0.014.
Values may be sent and summed in bfloat16 or wider, within the bound.
A program may use at most 128 MiB of HBM per device.

```python
import math
import jax
import jax.numpy as jnp
import numpy as np
from jax import lax

D = 2880
HEADS = 32
KV = 4
HD = 64
FF = 1536
SPLITS = 2
TOP = 4
DOCS = 4
TOK_DEV = 128
SEQ = 2048
SLABS = 16
EXPERTS = 8
FF_SLAB = 768
CAP = 68
N_CTX = 16


def key_matrix(base_key):
    source = jax.random.normal(jax.random.fold_in(base_key, 11), (D, KV * HD), jnp.float32)
    return jnp.clip(source, -4.0, 4.0) / math.sqrt(D)


def draw_w_key(key, part):
    return key_matrix(key).astype(jnp.bfloat16)


def draw_w_query(key, part):
    source = jax.random.normal(jax.random.fold_in(key, 12), (D, HEADS * HD), jnp.float32)
    query_mat = jnp.clip(source, -4.0, 4.0) / math.sqrt(D)
    return query_mat.astype(jnp.bfloat16)


def steps_of(own_key, extent, pieces, least, high):
    level = 1.0
    for axis_at, blocks in pieces:
        draws = jax.random.uniform(jax.random.fold_in(jax.random.fold_in(own_key, 6), axis_at), (blocks,), jnp.float32, least / len(pieces), high / len(pieces))
        level = level * jnp.repeat(jnp.exp(draws), extent[axis_at] // blocks).reshape((-1,) + (1,) * (len(extent) - 1 - axis_at))
    return level


def length_profile(amount, total, bound, slope):
    portions = [(1 << 20) // math.isqrt(standing ** slope) + 1 for standing in range(2, amount + 1)]
    spare, holding = total - bound - (amount - 1), [1] * (amount - 1)
    while spare > 0:
        movable = [i for i in range(amount - 1) if holding[i] < bound]
        pool, left = sum([portions[i] for i in movable]), spare
        for i in movable:
            addition = min(bound - holding[i], max(1, left * portions[i] // pool), spare)
            holding[i] = holding[i] + addition
            spare = spare - addition
    return np.array([bound] + holding)


def ragged_sizes(own_key, number_of, total, bound, lean):
    if number_of == 2:
        one = jax.random.randint(own_key, (), max(1, total - bound), min(bound, total - 1) + 1)
        return jnp.stack([one, total - one])
    sizes = jnp.asarray(length_profile(number_of, total, bound, lean), jnp.int32)
    couples = (number_of - 1) // 2
    source_of, taker = sizes[1:1 + 2 * couples:2], sizes[2:2 + 2 * couples:2]
    margin = jnp.minimum(source_of - 1, bound - taker)
    moved = jax.random.randint(jax.random.fold_in(own_key, 1), (couples,), 0, 1 << 20) % (margin + 1)
    sizes = sizes.at[1:1 + 2 * couples:2].set(source_of - moved).at[2:2 + 2 * couples:2].set(taker + moved)
    return sizes[jax.random.permutation(jax.random.fold_in(own_key, 2), number_of)]


def assign_block(key, own, number, rows, number_of, top, reach, slope):
    sequence = jax.random.permutation(key, number_of)
    packed, common = portions_of(number_of, rows * top, reach, slope, True), portions_of(number_of, rows * top, reach, slope, False)
    places = jnp.arange(number_of)

    def named(sizes, turn):
        used = int((sizes > 0).sum())
        fixed = max(1, used // 4)
        shifted = fixed + (places - fixed + turn * (used - fixed)) % max(1, number_of - fixed)
        return jnp.zeros((number_of,), jnp.int32).at[sequence[jnp.where(places < fixed, places, shifted)]].set(jnp.asarray(sizes, jnp.int32))

    sizes = jnp.where(number % 4 == 0, named(packed, number // 4), named(common, number - number // 4 - 1))
    mixed = jax.random.permutation(jax.random.fold_in(own, 3), number_of)
    giver, receiver = mixed[0:number_of // 2 * 2:2], mixed[1:number_of // 2 * 2:2]
    room = jnp.minimum(sizes[giver] - 1, reach - sizes[receiver]) // 2
    room = jnp.where((giver == sequence[0]) | (receiver == sequence[0]) | (sizes[receiver] == 0), 0, jnp.maximum(room, 0))
    shifted = jax.random.randint(jax.random.fold_in(own, 4), (number_of // 2,), 0, 1 << 20) % (room + 1)
    sizes = sizes.at[giver].add(-shifted).at[receiver].add(shifted)
    labels = jnp.searchsorted(jnp.cumsum(sizes), jnp.arange(rows * top), side="right").astype(jnp.int32)
    table = labels.reshape(top, rows).T
    table = table[jax.random.permutation(jax.random.fold_in(own, 1), rows)]
    turn = jax.random.randint(jax.random.fold_in(own, 2), (rows, 1), 0, top)
    return jnp.take_along_axis(table, (jnp.arange(top)[None, :] + turn) % top, axis=1)


def portions_of(count, total, limit, skew, full):
    loads = [(1 << 20) // math.isqrt(standing ** skew) + 1 for standing in range(1, count + 1)]
    largest = limit if full else min(limit, max(-(-total // count), total * loads[0] // sum(loads)))
    least = 1 if total - largest >= count - 1 else 0
    counts, surplus = [largest] + [least] * (count - 1), total - largest - least * (count - 1)
    while surplus > 0:
        movable = [i for i in range(1, count) if counts[i] < largest] or [i for i in range(1, count) if counts[i] < limit]
        pool, left = sum([loads[i] for i in movable]), surplus
        for i in movable:
            extra = min(limit - counts[i], max(1, left * loads[i] // pool), surplus)
            counts[i] = counts[i] + extra
            surplus = surplus - extra
    return np.array(counts)


def bell_draw(own_key, shape, width, most, split=(), held_as=jnp.bfloat16):
    drawn = width * jax.random.normal(own_key, shape, jnp.float32)
    if split:
        drawn = drawn * steps_of(own_key, shape, split, -0.22, 0.18)
    return jnp.clip(drawn, -most, most).astype(held_as)


def setup_inputs(seed: int = 0, part: int = 0) -> dict:
    streams_of = jax.random.split(jax.random.key(seed), 15)
    part_keys = jax.random.split(jax.random.fold_in(streams_of[14], part), 15)
    tokens = bell_draw(part_keys[0], (SEQ, D), 1.0, 6.0, ((0, 16),))
    lengths = ragged_sizes(part_keys[1], DOCS, SEQ, 3 * SEQ // 4, 2).astype(jnp.int32)
    attn_gain = jnp.clip(1.0 + 0.18 * jax.random.normal(streams_of[2], (D,), jnp.float32), 0.1, 1.9)
    w_query = draw_w_query(jax.random.fold_in(streams_of[14], 71), part)
    w_key = draw_w_key(jax.random.fold_in(streams_of[14], 71), part)
    w_value = bell_draw(streams_of[5], (D, KV * HD), D ** -0.5, 0.109375)
    sinks = jnp.clip(jax.random.uniform(streams_of[6], (HEADS,), jnp.float32, -2.0, 4.0), -2.0, 4.0)
    w_out = bell_draw(streams_of[7], (HEADS * HD, D), (HEADS * HD // 16) ** -0.5, 0.5, ((0, 16),))
    moe_gain = jnp.clip(1.0 + 0.18 * jax.random.normal(streams_of[8], (D,), jnp.float32), 0.1, 1.9)
    routes_keys = jax.random.split(jax.random.fold_in(part_keys[9], 1), SEQ // TOK_DEV)
    routes_turns = jax.random.permutation(jax.random.fold_in(part_keys[9], 3), SEQ // TOK_DEV)
    routes = jax.vmap(lambda own, number: assign_block(jax.random.fold_in(part_keys[9], 2), own, number, TOK_DEV, EXPERTS, TOP, CAP, 1))(routes_keys, routes_turns).reshape((SEQ, TOP))
    route_weights = jnp.clip(jnp.exp(math.log(1.0) - 2.9957323 * jax.random.uniform(part_keys[10], (SEQ, TOP), jnp.float32) ** steps_of(part_keys[10], (SEQ, TOP), ((0, 16),), -0.2, 0.2)), 0.05, 1.0)
    w_gate = bell_draw(streams_of[11], (SLABS, D, FF_SLAB), D ** -0.5, 0.109375, ((0, 16),))
    w_up = bell_draw(streams_of[12], (SLABS, D, FF_SLAB), D ** -0.5, 0.109375, ((0, 16),))
    w_down = bell_draw(streams_of[13], (SLABS, FF_SLAB, D), FF ** -0.5, 0.15625, ((0, 16),))
    return dict(tokens=tokens, lengths=lengths, attn_gain=attn_gain, w_query=w_query, w_key=w_key, w_value=w_value, sinks=sinks, w_out=w_out, moe_gain=moe_gain, routes=routes, route_weights=route_weights, w_gate=w_gate, w_up=w_up, w_down=w_down)


EPS = 1e-05
THETA = 150000.0
ALPHA = 1.702
SCALE = 0.125
NEGATIVE = -1e+30

def rms_scale(values, gain_vec):
    wide = values.astype(jnp.float32)
    inverse = lax.rsqrt(lax.optimization_barrier(jnp.mean(wide * wide, axis=-1, keepdims=True)) + EPS)
    return (wide * inverse * gain_vec.astype(jnp.float32)).astype(jnp.bfloat16)

def rotate(values, positions):
    half_size = values.shape[-1] // 2
    freqs = THETA ** (-jnp.arange(half_size, dtype=jnp.float32) / half_size)
    angles = positions.astype(jnp.float32)[:, None] * freqs[None, :]
    cosine = jnp.cos(angles)[:, None, :]
    sine = jnp.sin(angles)[:, None, :]
    first = values[..., :half_size]
    second = values[..., half_size:]
    return jnp.concatenate([first * cosine - second * sine, second * cosine + first * sine], axis=-1)

def segment_of(positions, doc_ends):
    return lax.optimization_barrier(jnp.sum((positions[:, None] >= doc_ends[None, :]).astype(jnp.int32), axis=1)).astype(jnp.int32)

def expert_rows(inputs, gate_mat, up_mat, down_mat):
    gate_val = jnp.dot(inputs, gate_mat, preferred_element_type=jnp.float32)
    up_val = jnp.dot(inputs, up_mat, preferred_element_type=jnp.float32)
    hidden = ((up_val + 1.0) * gate_val * jax.nn.sigmoid(ALPHA * gate_val)).astype(jnp.bfloat16)
    return jnp.dot(hidden, down_mat, preferred_element_type=jnp.float32).astype(jnp.bfloat16)

def reference(tokens, lengths, attn_gain, w_query, w_key, w_value, sinks, w_out, moe_gain, routes, route_weights, w_gate, w_up, w_down):
    seq_len = tokens.shape[0]
    group_size = HEADS // KV
    positions = jnp.arange(seq_len, dtype=jnp.int32)
    doc_ends = jnp.cumsum(lengths).astype(jnp.int32)
    segment = segment_of(positions, doc_ends)
    normed = rms_scale(tokens, attn_gain)
    raw_query = jnp.dot(normed, w_query, preferred_element_type=jnp.float32).reshape(seq_len, HEADS, HD)
    raw_key = jnp.dot(normed, w_key, preferred_element_type=jnp.float32).reshape(seq_len, KV, HD)
    val_rot = jnp.dot(normed, w_value, preferred_element_type=jnp.float32).astype(jnp.bfloat16).reshape(seq_len, KV, HD)
    queries = rotate(raw_query, positions).astype(jnp.bfloat16)
    key_rot = rotate(raw_key, positions).astype(jnp.bfloat16)
    allowed = (segment[:, None] == segment[None, :]) & (positions[None, :] <= positions[:, None])

    def one_head(head_id):
        q_head = lax.dynamic_index_in_dim(queries, head_id, 1, keepdims=False)
        k_head = lax.dynamic_index_in_dim(key_rot, head_id // group_size, 1, keepdims=False)
        v_head = lax.dynamic_index_in_dim(val_rot, head_id // group_size, 1, keepdims=False)
        sink_val = lax.dynamic_index_in_dim(sinks, head_id, 0, keepdims=False)
        scores = jnp.dot(q_head, k_head.T, preferred_element_type=jnp.float32) * SCALE
        scores = jnp.where(allowed, scores, NEGATIVE)
        top_val = jnp.maximum(lax.optimization_barrier(jnp.max(scores, axis=1)), sink_val)
        weights = jnp.exp(scores - top_val[:, None])
        denom = lax.optimization_barrier(jnp.sum(weights, axis=1)) + jnp.exp(sink_val - top_val)
        probs = (weights / denom[:, None]).astype(jnp.bfloat16)
        return jnp.dot(probs, v_head, preferred_element_type=jnp.float32).astype(jnp.bfloat16)
    per_head = lax.map(one_head, jnp.arange(HEADS, dtype=jnp.int32))
    attended = jnp.transpose(per_head, (1, 0, 2)).reshape(seq_len, HEADS * HD)
    mixed = (tokens.astype(jnp.float32) + jnp.dot(attended, w_out, preferred_element_type=jnp.float32)).astype(jnp.bfloat16)
    expert_in = rms_scale(mixed, moe_gain)
    block_routes = routes.reshape(N_CTX, TOK_DEV * TOP)
    onehot = (block_routes[..., None] == jnp.arange(EXPERTS, dtype=jnp.int32)[None, None, :]).astype(jnp.int32)
    slots = lax.optimization_barrier(jnp.sum((jnp.cumsum(onehot, axis=1).astype(jnp.int32) - 1) * onehot, axis=2)).astype(jnp.int32)
    block_ids = jnp.arange(N_CTX, dtype=jnp.int32)[:, None]
    row_index = (block_ids * CAP + slots).reshape(-1)
    token_ids = (block_ids * TOK_DEV + jnp.arange(TOK_DEV * TOP, dtype=jnp.int32)[None, :] // TOP).reshape(-1)
    expert_ids = block_routes.reshape(-1)
    buffer = jnp.zeros((EXPERTS, N_CTX * CAP, D), jnp.bfloat16).at[expert_ids, row_index].set(expert_in[token_ids])

    def slab_out(slab_id):
        rows_in = lax.dynamic_index_in_dim(buffer, slab_id // SPLITS, 0, keepdims=False)
        return expert_rows(rows_in, w_gate[slab_id], w_up[slab_id], w_down[slab_id])
    partials = lax.map(slab_out, jnp.arange(SLABS, dtype=jnp.int32))
    summed = lax.optimization_barrier(jnp.sum(partials.reshape(EXPERTS, SPLITS, N_CTX * CAP, D).astype(jnp.float32), axis=1)).astype(jnp.bfloat16)
    summed = lax.optimization_barrier(summed).astype(jnp.float32)
    picked = summed[expert_ids, row_index].reshape(seq_len, TOP, D)
    expert_sum = lax.optimization_barrier(jnp.sum(picked * route_weights[..., None], axis=1))
    return (mixed.astype(jnp.float32) + expert_sum).astype(jnp.bfloat16)
```

```python
import functools

import jax
import jax.numpy as jnp
import numpy as np
from jax import lax
from jax.experimental import pallas as pl
from jax.experimental.pallas import tpu as pltpu
from jax.sharding import PartitionSpec as P

HD = 64
EPS = 1e-05
THETA = 150000.0
ALPHA = 1.702
SCALE = 0.125
NEGATIVE = -1e30
MESH = pl.DeviceIdType.MESH
VMEM = pl.BlockSpec(memory_space=pltpu.VMEM)
LIMIT = 63 * 1024 * 1024


def rms_scale(values, gain_vec):
    wide = values.astype(jnp.float32)
    inverse = lax.rsqrt(jnp.mean(wide * wide, axis=-1, keepdims=True) + EPS)
    return (wide * inverse * gain_vec).astype(jnp.bfloat16)


class Ring:
    def __init__(self, chips):
        self.chips = chips
        self.me = lax.axis_index("ctx")
        self.core = lax.rem(self.me, 2)
        chip = self.me // 2
        self.fold = chips == 8
        if self.fold:
            z, y = chip // 2, lax.rem(chip, 2)
            self.pos = z + y * (chips - 1 - 2 * z)
        else:
            self.pos = chip
        self.way = 1 - 2 * self.core
        self.partner = {"ctx": self.me + self.way}
        self.next = {"ctx": self.owner(-1)}
        self.prev = {"ctx": self.owner(1)}
        group = lax.axis_index("groups")
        self.parity = lax.rem(group, 2)
        self.peer = {"groups": group + 1 - 2 * self.parity}

    def index(self, pos, core):
        pos = lax.rem(pos + 2 * self.chips, self.chips)
        if self.fold:
            y = pos // (self.chips // 2)
            z = pos + y * (self.chips - 1 - 2 * pos)
            chip = z * 2 + y
        else:
            chip = pos
        return chip * 2 + core

    def owner(self, step):
        return self.index(self.pos - self.way * step, self.core)

    def partner_owner(self, step):
        return self.index(self.pos + self.way * step, 1 - self.core)

    def barrier(self, with_peer=False):
        sem = pltpu.get_barrier_semaphore()
        others = [self.next, self.prev, self.partner] + ([self.peer] if with_peer else [])
        for other in others:
            pl.semaphore_signal(sem, inc=1, device_id=other, device_id_type=MESH)
        pl.semaphore_wait(sem, len(others))


def gather_ring(ring, pieces, sems, setup, work):
    ring_send, ring_recv, part_send, part_recv, peer_send, peer_recv = sems
    chips = ring.chips
    ringed = [i for i, piece in enumerate(pieces) if piece[3] != "peer"]
    peered = [i for i, piece in enumerate(pieces) if piece[3] == "peer"]
    shared = [i for i, piece in enumerate(pieces) if piece[3] == "both"]
    lag = 2 if peered else 1

    def copy(i, step, target, send, recv, own=False):
        source, slots, view, _ = pieces[i]
        dst = view(slots.at[ring.owner(step)])
        return pltpu.make_async_remote_copy(
            src_ref=view(source) if own else dst,
            dst_ref=dst,
            send_sem=send,
            recv_sem=recv,
            device_id=target,
            device_id_type=MESH,
        )

    def onward(i, step, own=False):
        return copy(
            i, step, ring.next, ring_send.at[i, step], ring_recv.at[i, step + 1], own
        )

    def across(i, step, own=False):
        return copy(i, step, ring.partner, part_send.at[i, step], part_recv.at[i, step], own)

    def aside(i, step):
        return copy(i, step, ring.peer, peer_send.at[step], peer_recv.at[step])

    def arrived(i, sem, who):
        ref = pieces[i][2](pieces[i][1].at[who])
        pltpu.make_async_copy(ref, ref, sem).wait()

    ring.barrier(bool(peered))
    for i in ringed:
        onward(i, 0, True).start()
    for i in range(len(pieces)):
        across(i, 0, True).start()
    filled = []
    for source, slots, _, _ in pieces:
        if not any(slots is other for other in filled):
            slots[ring.me] = source[...]
            filled.append(slots)
    setup()

    def turn(t, carry):
        @pl.when(t < chips)
        def _():
            for i in ringed:
                arrived(i, ring_recv.at[i, t], ring.owner(t))

                @pl.when(t < chips - 1)
                def _():
                    onward(i, t).start()

                if i in shared:
                    aside(i, t).start()
                across(i, t).start()

        if peered:

            @pl.when((t > 1) & (t <= chips))
            def _():
                for i in peered:
                    arrived(i, peer_recv.at[t - 1], ring.owner(t - 1))
                    across(i, t - 1).start()

        @pl.when(t >= lag)
        def _():
            s = t - lag
            for i in range(len(pieces)):
                arrived(i, part_recv.at[i, s], ring.partner_owner(s))
            work(s)

        return carry

    lax.fori_loop(1, chips + lag, turn, 0)

    def drain(s, carry):
        for i in range(len(pieces)):
            across(i, s).wait_send()
        for i in ringed:

            @pl.when(s < chips - 1)
            def _():
                onward(i, s).wait_send()

        for i in shared:

            @pl.when(s > 0)
            def _():
                aside(i, s).wait_send()

        return carry

    lax.fori_loop(0, chips, drain, 0)


def ring_sems(count, chips):
    return [pltpu.SemaphoreType.DMA((count, chips))] * 4


def gather_sems(count, chips):
    return ring_sems(count, chips) + [pltpu.SemaphoreType.DMA((chips,))] * 2


def whole(ref):
    return ref


def cols(start, size):
    return lambda ref: ref.at[:, pl.ds(start, size)]


def rows(start, size):
    return lambda ref: ref.at[pl.ds(start, size), :]


def thirds(ring, source, slots):
    width = source.shape[1]
    third = width // 3 // 128 * 128
    mine = pl.multiple_of(ring.parity * third, 128)
    other = pl.multiple_of((1 - ring.parity) * third, 128)
    return [
        (source, slots, cols(mine, third), "both"),
        (source, slots, cols(2 * third, width - 2 * third), "ring"),
        (source, slots, cols(other, third), "peer"),
    ]


def query_kernel(chips, lhs, kv, meta, weight, out, kv_all, meta_all, slots, *sems):
    ring = Ring(chips)
    pieces = [(kv, kv_all, whole, "ring"), (meta, meta_all, whole, "ring")]
    pieces += thirds(ring, weight, slots)

    def setup():
        out[...] = jnp.zeros_like(out)

    def work(s):
        for who in (ring.owner(s), ring.partner_owner(s)):
            out[...] += jnp.dot(lhs[who], slots[who], preferred_element_type=jnp.float32)

    gather_ring(ring, pieces, sems, setup, work)


def attend_kernel(
    chips, raw, kv_all, cosine, sine, sinks, start, weight, tokens, gain,
    mixed_out, expert_in, out, slots, bias, query, key, value, attended, *sems
):
    ring = Ring(chips)
    blocks, tok_rows, width = attended.shape
    per_block = width // HD
    kv_heads, seq, _ = key.shape
    group = query.shape[0] // kv_heads
    pieces = thirds(ring, weight, slots)

    def setup():
        key_pos = lax.broadcasted_iota(jnp.int32, (tok_rows, seq), 1)
        row_pos = lax.broadcasted_iota(jnp.int32, (tok_rows, seq), 0) + ring.me * tok_rows
        allowed = (key_pos <= row_pos) & (key_pos >= start[...])
        bias[...] = jnp.where(allowed, 0.0, NEGATIVE)
        lane = lax.broadcasted_iota(jnp.int32, (tok_rows, 2 * HD), 1)
        first = lax.rem(lane, HD) < HD // 2

        def turn_pair(j, carry):
            pair = raw[:, pl.ds(pl.multiple_of(j * 2 * HD, 2 * HD), 2 * HD)]
            other = jnp.where(
                first, pltpu.roll(pair, 2 * HD - HD // 2, 1), pltpu.roll(pair, HD // 2, 1)
            )
            turned = ((pair * cosine[...] + other * sine[...]) * SCALE).astype(jnp.bfloat16)
            query[2 * j] = turned[:, :HD]
            query[2 * j + 1] = turned[:, HD:]
            return carry

        lax.fori_loop(0, query.shape[0] // 2, turn_pair, 0)

        def unpack(d, carry):
            at = pl.ds(pl.multiple_of(d * tok_rows, tok_rows), tok_rows)
            block = kv_all[d]
            for g in range(kv_heads):
                key[g, at, :] = block[:, g * HD : (g + 1) * HD]
                value[g, at, :] = block[:, (kv_heads + g) * HD : (kv_heads + g + 1) * HD]
            return carry

        lax.fori_loop(0, blocks, unpack, 0)

    def attend(who):
        heads = []
        for j in range(per_block):
            head = who * per_block + j
            kv_head = head // group
            scores = (
                lax.dot_general(
                    query[head],
                    key[kv_head],
                    (((1,), (1,)), ((), ())),
                    preferred_element_type=jnp.float32,
                )
                + bias[...]
            )
            sink = sinks[head]
            top = jnp.maximum(jnp.max(scores, axis=1, keepdims=True), sink)
            weights = jnp.exp(scores - top)
            total = jnp.sum(weights, axis=1, keepdims=True) + jnp.exp(sink - top)
            mixed = jnp.dot(
                weights.astype(jnp.bfloat16), value[kv_head], preferred_element_type=jnp.float32
            )
            heads.append(mixed / total)
        joined = heads[0] if per_block == 1 else jnp.concatenate(heads, axis=1)
        attended[who] = joined.astype(jnp.bfloat16)

    def work(s):
        attend(ring.owner(s))
        attend(ring.partner_owner(s))

    gather_ring(ring, pieces, sems, setup, work)
    out[...] = tokens[...].astype(jnp.float32)

    def project(d, carry):
        out[...] += jnp.dot(attended[d], slots[d], preferred_element_type=jnp.float32)
        return carry

    lax.fori_loop(0, blocks, project, 0)
    mixed_out[...] = out[...].astype(jnp.bfloat16)
    expert_in[...] = rms_scale(mixed_out[...], gain[...])


def expert_kernel(
    chips, rows_in, select, w_gate, w_up, w_down,
    out, slots, packed, gate, up, down, load_sem, *sems
):
    ring = Ring(chips)
    half = rows_in.shape[0] // 2
    padded = select.shape[1]
    pieces = [
        (rows_in, slots, rows(0, half), "ring"),
        (rows_in, slots, rows(half, half), "ring"),
    ]
    loads = [
        pltpu.make_async_copy(source, target, load_sem.at[i])
        for i, (source, target) in enumerate(((w_gate, gate), (w_up, up), (w_down, down)))
    ]
    for load in loads:
        load.start()

    def work(s):
        whose = [
            ring.owner(s - 1), ring.partner_owner(s - 1), ring.owner(s), ring.partner_owner(s)
        ]

        @pl.when(s == 1)
        def _():
            for load in loads:
                load.wait()

        @pl.when(lax.rem(s, 2) == 1)
        def _():
            for j, who in enumerate(whose):
                packed[j * padded : (j + 1) * padded, :] = jnp.dot(
                    select[who], slots[who], preferred_element_type=jnp.float32
                ).astype(jnp.bfloat16)
            gate_val = jnp.dot(packed[...], gate[...], preferred_element_type=jnp.float32)
            up_val = jnp.dot(packed[...], up[...], preferred_element_type=jnp.float32)
            hidden = (up_val + 1.0) * gate_val * jax.nn.sigmoid(ALPHA * gate_val)
            partial = lax.dot_general(
                hidden.astype(jnp.bfloat16),
                down[...],
                (((1,), (1,)), ((), ())),
                preferred_element_type=jnp.float32,
            ).astype(jnp.bfloat16)
            for j, who in enumerate(whose):
                out[who] = partial[j * padded : (j + 1) * padded, :]

    gather_ring(ring, pieces, sems, lambda: None, work)


def combine_kernel(
    chips, partial, select, weights, mixed, out, cross_out, cross_in, ring_out, ring_in,
    ring_send, ring_recv, part_send, part_recv,
):
    ring = Ring(chips)
    tok_rows = mixed.shape[0]
    half = tok_rows // 2
    ring.barrier()

    def share(who, h):
        at = pl.ds(h * half, half)
        spread = jnp.dot(select[who, at, :], partial[who], preferred_element_type=jnp.float32)
        return spread * weights[who, at, :]

    def crossing(s, h):
        at = pl.ds(h * half, half)
        return pltpu.make_async_remote_copy(
            src_ref=cross_out.at[s, at, :],
            dst_ref=cross_in.at[s, at, :],
            send_sem=part_send.at[h, s],
            recv_sem=part_recv.at[h, s],
            device_id=ring.partner,
            device_id_type=MESH,
        )

    def onward(s, h):
        at = pl.ds(h * half, half)
        return pltpu.make_async_remote_copy(
            src_ref=ring_out.at[s, at, :],
            dst_ref=ring_in.at[s, at, :],
            send_sem=ring_send.at[h, s],
            recv_sem=ring_recv.at[h, s],
            device_id=ring.next,
            device_id_type=MESH,
        )

    def give(s):
        who = ring.partner_owner(s + 1)
        for h in range(2):
            at = pl.ds(h * half, half)
            cross_out[s, at, :] = share(who, h).astype(jnp.bfloat16)
            crossing(s, h).start()

    def own(s, h):
        total = share(ring.owner(s + 1), h)
        crossing(s, h).wait_recv()
        return total + cross_in[s, pl.ds(h * half, half), :].astype(jnp.float32)

    give(0)
    for h in range(2):
        ring_out[0, pl.ds(h * half, half), :] = own(0, h).astype(jnp.bfloat16)
        onward(0, h).start()
    give(1)

    def step(s, carry):
        for h in range(2):
            at = pl.ds(h * half, half)
            total = own(s, h)
            onward(s - 1, h).wait_recv()
            total = total + ring_in[s - 1, at, :].astype(jnp.float32)
            ring_out[s, at, :] = total.astype(jnp.bfloat16)
            onward(s, h).start()
        give(s + 1)
        return carry

    lax.fori_loop(1, chips - 1, step, 0)
    last = chips - 1
    for h in range(2):
        at = pl.ds(h * half, half)
        total = own(last, h)
        onward(last - 1, h).wait_recv()
        total = total + ring_in[last - 1, at, :].astype(jnp.float32)
        out[at, :] = (mixed[at, :].astype(jnp.float32) + total).astype(jnp.bfloat16)

    def drain(s, carry):
        for h in range(2):
            crossing(s, h).wait_send()

            @pl.when(s < chips - 1)
            def _():
                onward(s, h).wait_send()

        return carry

    lax.fori_loop(0, chips, drain, 0)


LOG2E = 1.4426950408889634
ANY = pl.BlockSpec(memory_space=pl.ANY)
SMEM = pl.BlockSpec(memory_space=pltpu.SMEM)


class Copies:
    def __init__(self):
        self.made = []

    def send(self, make, pred=None):
        self.made.append((make, pred))
        if pred is None:
            make().start()
        else:
            pl.when(pred)(lambda: make().start())

    def drain(self):
        for make, pred in self.made:
            if pred is None:
                make().wait_send()
            else:
                pl.when(pred)(lambda make=make: make().wait_send())


def remote(src, dst, send_sem, recv_sem, where):
    return pltpu.make_async_remote_copy(
        src_ref=src, dst_ref=dst, send_sem=send_sem, recv_sem=recv_sem,
        device_id=where, device_id_type=MESH,
    )


def landed(ref, sem):
    pltpu.make_async_copy(ref, ref, sem).wait()


def spans(width, size):
    return [(at, min(size, width - at)) for at in range(0, width, size)]


def front_kernel(
    planes, tokens, lengths, attn_gain, w_query, w_key, w_value, sinks, w_out, moe_gain,
    cosine, sine, meta, mixed_out, expert_in, meta_all,
    normed, wq, wkv, kv_own, kv_all, lhs, raw, qx, kx, vx, bias, top, acc, attended, wo,
    part, held, k_out, k_in, y_out, y_in,
    load_sem, wq_recv, wq_plane, wq_send, norm_recv, norm_send, kv_recv, kv_send,
    meta_recv, meta_send, wo_recv, wo_plane, wo_send, k_recv, k_send, y_recv, y_send,
):
    f32, bf16 = jnp.float32, jnp.bfloat16
    x, c = lax.axis_index("groups"), lax.axis_index("ctx")
    z, y, k, d = c // 4, lax.rem(c // 2, 2), lax.rem(c, 2), lax.rem(c, 4)
    total = 4 * planes
    rows, width = tokens.shape
    wq_rows, qcols = wq.shape[1], wq.shape[2]
    heads = qx.shape[0]
    plane_rows = 4 * rows
    partner, across = {"ctx": c + 1 - 2 * k}, {"ctx": c + 2 - 4 * y}
    peer = {"groups": 1 - x}
    copies = Copies()

    loads = [
        pltpu.make_async_copy(w_key, wkv.at[0], load_sem.at[0]),
        pltpu.make_async_copy(w_value, wkv.at[1], load_sem.at[1]),
        pltpu.make_async_copy(w_query.at[:, pl.ds(d * qcols, qcols)], wq.at[c], wq_recv.at[c]),
    ]
    for load in loads:
        load.start()

    barrier = pltpu.get_barrier_semaphore()
    for r in range(1, total):
        pl.semaphore_signal(
            barrier, inc=1, device_id={"ctx": lax.rem(c + r, total)}, device_id_type=MESH
        )
    pl.semaphore_signal(barrier, inc=1, device_id=peer, device_id_type=MESH)
    normed[d] = rms_scale(tokens[...], attn_gain[...])
    meta_all[c] = meta[...]
    pl.semaphore_wait(barrier, total)

    for r in (2, 3, 1):
        other = jnp.bitwise_xor(d, r)
        copies.send(
            lambda r=r, other=other: remote(
                w_query.at[:, pl.ds(other * qcols, qcols)], wq.at[c],
                wq_plane.at[r], wq_recv.at[c], {"ctx": 4 * z + other},
            )
        )
    copies.send(
        lambda: remote(normed.at[d], normed.at[d], norm_send.at[0], norm_recv.at[d], across)
    )
    copies.send(
        lambda: remote(normed.at[d], normed.at[d], norm_send.at[1], norm_recv.at[d], partner)
    )

    def wq_relay(who, right, left, side):
        landed(wq.at[who], wq_recv.at[who])
        for i, (where, pred) in enumerate(
            (({"ctx": c + 4}, right), ({"ctx": c - 4}, left), (peer, side))
        ):
            if pred is not None:
                copies_start(
                    lambda i=i, where=where: remote(
                        wq.at[who], wq.at[who], wq_send.at[i, who], wq_recv.at[who], where
                    ),
                    pred,
                )

    def copies_start(make, pred):
        pl.when(pred)(lambda: make().start())

    upper, lower = z < planes - 1, z > 0
    always = z >= 0
    wq_relay(4 * z + 2 * y + x, upper, lower, None)

    for load in loads[:2]:
        load.wait()
    own = normed[d]
    lane = lax.broadcasted_iota(jnp.int32, (rows, 2 * HD), 1)
    first = lax.rem(lane, HD) < HD // 2
    mine = pl.ds(pl.multiple_of(d * rows, rows), rows)
    turn_cos, turn_sin = cosine[mine, :], sine[mine, :]

    def turned(pair, cos, sin, low):
        other = jnp.where(
            low, pltpu.roll(pair, 2 * HD - HD // 2, 1), pltpu.roll(pair, HD // 2, 1)
        )
        return pair * cos + other * sin

    raw_key = jnp.dot(own, wkv[0], preferred_element_type=f32)
    raw_value = jnp.dot(own, wkv[1], preferred_element_type=f32)
    for j in range(2):
        at = slice(j * 2 * HD, (j + 1) * 2 * HD)
        keys = turned(raw_key[:, at], turn_cos, turn_sin, first)
        values = raw_value[:, at]
        kv_own[2 * j] = jnp.where(lane < HD, keys, pltpu.roll(values, HD, 1)).astype(bf16)
        kv_own[2 * j + 1] = jnp.where(lane < HD, pltpu.roll(keys, HD, 1), values).astype(bf16)
    kv_all[c] = kv_own[d]

    def kv_copy(dz, other):
        return lambda: remote(
            kv_own.at[other], kv_all.at[c], kv_send.at[dz, other], kv_recv.at[c],
            {"ctx": 4 * (z + dz) + other},
        )

    wq_relay(4 * z + 2 * (1 - y) + x, upper, lower, None)
    for dz in range(planes):
        for other in range(4):
            pred = (z + dz < planes) if dz else (d != other)
            copies.send(kv_copy(dz, other), pred)
    for r in range(1, total):
        copies.send(
            lambda r=r: remote(
                meta, meta_all.at[c], meta_send.at[r], meta_recv.at[c],
                {"ctx": lax.rem(c + r, total)},
            )
        )

    def wo_rows(i):
        return pl.ds(pl.multiple_of(i * rows, rows), rows)

    wo_spans = spans(width, 1024)

    def wo_hand(n):
        at, size = wo_spans[n]
        return remote(
            w_out.at[:, pl.ds(at, size)], wo.at[wo_rows(d), pl.ds(at, size)],
            wo_plane.at[n], wo_recv.at[d, n], {"ctx": 5 * z},
        )

    def wo_keep(n):
        at, size = wo_spans[n]
        return pltpu.make_async_copy(
            w_out.at[:, pl.ds(at, size)], wo.at[wo_rows(d), pl.ds(at, size)], wo_recv.at[d, n]
        )

    for s in range(1, planes):
        for j in range(2):

            @pl.when(z >= s)
            def _(s=s, j=j):
                wq_relay(4 * (z - s) + 2 * j + x, upper, None, always)

            @pl.when(z + s < planes)
            def _(s=s, j=j):
                wq_relay(4 * (z + s) + 2 * j + x, None, lower, always)

        if s == 1:
            beyond = 4 * z + jnp.bitwise_xor(d, 2)
            opposite = jnp.bitwise_xor(d, 2)
            landed(normed.at[opposite], norm_recv.at[opposite])
            copies.send(
                lambda: remote(
                    normed.at[opposite], normed.at[opposite],
                    norm_send.at[2], norm_recv.at[opposite], partner,
                )
            )
            for n in range(len(wo_spans)):
                pl.when(d == z)(lambda n=n: wo_keep(n).start())
                copies.send(lambda n=n: wo_hand(n), d != z)

    for r in (1, 3):
        other = jnp.bitwise_xor(d, r)
        landed(normed.at[other], norm_recv.at[other])
    for t in range(4):
        block = normed[t]
        for j in range(total):
            lhs[j, t * rows : (t + 1) * rows, :] = block[:, j * wq_rows : (j + 1) * wq_rows]

    def wo_relay(n, j):
        at, size = wo_spans[n]
        i = 2 * j + x
        piece = wo.at[wo_rows(i), pl.ds(at, size)]
        landed(piece, wo_recv.at[i, n])
        for way, (where, pred) in enumerate(wo_ways()):
            copies_start(
                lambda way=way, where=where: remote(
                    piece, piece, wo_send.at[way, i, n], wo_recv.at[i, n], where
                ),
                pred,
            )

    def wo_ways():
        return (
            ({"ctx": c + 4}, upper & (z >= d)),
            ({"ctx": c - 4}, lower & (z <= d)),
            (peer, z != d),
        )

    def wo_stage(stage):
        for n in range(len(wo_spans)):
            for j in range(2):
                jj = jnp.bitwise_xor(j, y)
                if n == stage:
                    pl.when(z == d)(lambda n=n, jj=jj: wo_relay(n, jj))
                if n + 2 == stage:
                    pl.when(z != d)(lambda n=n, jj=jj: wo_relay(n, jj))

    raw[...] = jnp.zeros_like(raw)

    def query_rows(plane):
        for i in range(4):
            who = 4 * plane + i
            raw[...] += jnp.dot(lhs[who], wq[who], preferred_element_type=f32)

    query_rows_wait = lambda plane, i: landed(wq.at[4 * plane + i], wq_recv.at[4 * plane + i])
    for i in range(2):
        query_rows_wait(z, 2 * i + 1 - x)
    query_rows(z)
    for s in range(1, planes):
        for step in (-s, s):

            @pl.when((z + step >= 0) & (z + step < planes))
            def _(step=step):
                for i in range(2):
                    query_rows_wait(z + step, 2 * i + 1 - x)
                query_rows(z + step)

    wo_stage(0)

    ends = [lengths[0]]
    for i in range(1, lengths.shape[0]):
        ends.append(ends[-1] + lengths[i])

    def segment(start, shape):
        place = start + lax.broadcasted_iota(jnp.int32, shape, 0)
        found = jnp.zeros(shape, jnp.int32)
        for end in ends:
            found += (place >= end).astype(jnp.int32)
        return found

    wide = (plane_rows, 2 * HD)
    wide_lane = lax.broadcasted_iota(jnp.int32, wide, 1)
    mark = jnp.where(
        (wide_lane - HD == segment(z * plane_rows, wide)) & (wide_lane >= HD), 1.0, 0.0
    )
    wide_first = lax.rem(wide_lane, HD) < HD // 2

    for j in range(heads // 2):
        pair = turned(
            raw[:, j * 2 * HD : (j + 1) * 2 * HD], cosine[...], sine[...], wide_first
        ) * (SCALE * LOG2E)
        qx[2 * j] = jnp.where(wide_lane < HD, pair, mark).astype(bf16)
        qx[2 * j + 1] = jnp.where(wide_lane < HD, pltpu.roll(pair, HD, 1), mark).astype(bf16)

    def unpack(i, carry):
        @pl.when(i != c)
        def _():
            landed(kv_all.at[i], kv_recv.at[i])

        both = kv_all[i].astype(f32)
        apart = jnp.where(
            (lane - HD == segment(i * rows, lane.shape)) | (lane >= HD + len(ends)), 0.0, NEGATIVE
        )
        at = pl.ds(pl.multiple_of(i * rows, rows), rows)
        kx[at, :] = jnp.where(lane < HD, both, apart).astype(bf16)
        ones = jnp.where(lane == HD, 1.0, 0.0)
        vx[at, :] = jnp.where(lane < HD, pltpu.roll(both, HD, 1), ones).astype(bf16)
        return carry

    lax.fori_loop(0, 4 * (z + 1), unpack, 0)
    square = (plane_rows, plane_rows)
    bias[...] = jnp.where(
        lax.broadcasted_iota(jnp.int32, square, 1) <= lax.broadcasted_iota(jnp.int32, square, 0),
        0.0, NEGATIVE,
    )

    def attend(h):
        top[...] = jnp.full(top.shape, sinks[d * heads + h] * LOG2E, f32)
        acc[...] = jnp.where(wide_lane == HD, 1.0, 0.0)

        def block(b, last):
            at = pl.ds(pl.multiple_of(b * plane_rows, plane_rows), plane_rows)
            scores = lax.dot_general(
                qx[h], kx[at, :], (((1,), (1,)), ((), ())), preferred_element_type=f32
            )
            if last:
                scores += bias[...]
            old = top[...]
            new = jnp.maximum(old, jnp.max(scores, axis=1, keepdims=True))
            weights = jnp.exp2(scores - new).astype(bf16)
            acc[...] = acc[...] * jnp.exp2(old - new) + jnp.dot(
                weights, vx[at, :], preferred_element_type=f32
            )
            top[...] = new

        def body(b, carry):
            block(b, False)
            return carry

        lax.fori_loop(0, z, body, 0)
        block(z, True)
        found = acc[...]
        return found / found[:, HD : HD + 1]

    def pair_of_heads(j, carry):
        for stage in range(1, heads // 2):
            pl.when(j == stage)(lambda stage=stage: wo_stage(stage))
        even = attend(2 * j)
        part[:, : 2 * HD] = even
        odd = attend(2 * j + 1)
        both = jnp.where(wide_lane < HD, part[:, : 2 * HD], pltpu.roll(odd, HD, 1))
        attended[j] = both.astype(bf16)
        return carry

    lax.fori_loop(0, heads // 2, pair_of_heads, 0)
    wo_stage(4)

    lhs_out = jnp.concatenate([attended[j] for j in range(heads // 2)], axis=1)
    give, keep = 1 - k, k

    def k_copy(n):
        at, size = wo_spans[n]
        return remote(
            k_out.at[:, :, pl.ds(at, size)], k_in.at[:, :, pl.ds(at, size)],
            k_send.at[n], k_recv.at[n], partner,
        )

    def y_copy(n):
        at, size = wo_spans[n]
        return remote(
            y_out.at[:, pl.ds(at, size)], y_in.at[:, pl.ds(at, size)],
            y_send.at[n], y_recv.at[n], across,
        )

    def project(n):
        at, size = wo_spans[n]
        cols = pl.ds(at, size)
        for j in range(2):
            i = 2 * j + 1 - x
            landed(wo.at[wo_rows(i), cols], wo_recv.at[i, n])
        part[:, :size] = jnp.dot(lhs_out, wo[:, cols], preferred_element_type=f32)
        for j in range(2):
            k_out[j, :, cols] = part[wo_rows(2 * j + give), :size].astype(bf16)
            held[j, :, cols] = part[wo_rows(2 * j + keep), :size]
        copies.send(lambda: k_copy(n))

    def fold(n):
        at, size = wo_spans[n]
        cols = pl.ds(at, size)
        k_copy(n).wait_recv()
        y_out[:, cols] = (held[1 - y, :, cols] + k_in[1 - y, :, cols].astype(f32)).astype(bf16)
        copies.send(lambda: y_copy(n))

    def finish(n):
        at, size = wo_spans[n]
        cols = pl.ds(at, size)
        mine = held[y, :, cols] + k_in[y, :, cols].astype(f32) + tokens[:, cols].astype(f32)
        y_copy(n).wait_recv()
        mixed_out[:, cols] = (mine + y_in[:, cols].astype(f32)).astype(bf16)

    count = len(wo_spans)
    for n in range(count):
        if n == count - 1:
            wo_stage(5)
        project(n)
        if n:
            fold(n - 1)
    fold(count - 1)
    for n in range(count):
        finish(n)
    expert_in[...] = rms_scale(mixed_out[...], moe_gain[...])

    def meta_arrived(i, carry):
        @pl.when(i != c)
        def _():
            landed(meta_all.at[i], meta_recv.at[i])

        return carry

    lax.fori_loop(0, total, meta_arrived, 0)
    copies.drain()

    def wq_drain(who, ways):
        for i, pred in enumerate(ways):
            pl.when(pred)(
                lambda i=i: remote(
                    wq.at[who], wq.at[who], wq_send.at[i, who], wq_recv.at[who], partner
                ).wait_send()
            )

    never = z < 0
    for j in range(2):
        wq_drain(4 * z + 2 * j + x, (upper, lower))
    for s in range(1, planes):
        for j in range(2):
            pl.when(z >= s)(
                lambda s=s, j=j: wq_drain(4 * (z - s) + 2 * j + x, (upper, never, always))
            )
            pl.when(z + s < planes)(
                lambda s=s, j=j: wq_drain(4 * (z + s) + 2 * j + x, (never, lower, always))
            )
    for n, (at, size) in enumerate(wo_spans):
        for j in range(2):
            i = 2 * j + x
            piece = wo.at[wo_rows(i), pl.ds(at, size)]
            for way, (where, pred) in enumerate(wo_ways()):
                pl.when(pred)(
                    lambda way=way, where=where: remote(
                        piece, piece, wo_send.at[way, i, n], wo_recv.at[i, n], where
                    ).wait_send()
                )


def front(tokens, lengths, attn_gain, w_query, w_key, w_value, sinks, w_out, moe_gain, meta):
    bf16, f32 = jnp.bfloat16, jnp.float32
    rows, width = tokens.shape
    devices = lax.axis_size("ctx")
    planes = devices // 4
    seq = devices * rows
    quarter = w_query.shape[1] // 4
    heads = quarter // HD
    count = len(spans(width, 1024))
    place = np.arange(seq, dtype=np.float32)
    freqs = np.float32(THETA) ** (-np.arange(HD // 2, dtype=np.float32) / np.float32(HD // 2))
    angles = place[:, None] * freqs[None, :].astype(np.float32)
    cos, sin = np.cos(angles).astype(np.float32), np.sin(angles).astype(np.float32)
    plane = lax.axis_index("ctx") // 4
    cosine = lax.dynamic_slice_in_dim(jnp.asarray(np.tile(cos, (1, 4))), plane * 4 * rows, 4 * rows)
    sine = lax.dynamic_slice_in_dim(
        jnp.asarray(np.tile(np.concatenate([-sin, sin], axis=1), (1, 2))), plane * 4 * rows, 4 * rows
    )
    dma = pltpu.SemaphoreType.DMA
    vmem = pltpu.VMEM
    return pl.pallas_call(
        functools.partial(front_kernel, planes),
        out_shape=[
            jax.ShapeDtypeStruct((rows, width), bf16),
            jax.ShapeDtypeStruct((rows, width), bf16),
            jax.ShapeDtypeStruct((devices,) + meta.shape, f32),
        ],
        in_specs=[VMEM, SMEM, VMEM, ANY, ANY, ANY, SMEM, ANY, VMEM, VMEM, VMEM, VMEM],
        out_specs=[VMEM] * 3,
        scratch_shapes=[
            vmem((4, rows, width), bf16),
            vmem((devices, w_query.shape[0], quarter), bf16),
            vmem((2,) + w_key.shape, bf16),
            vmem((4, rows, 2 * HD), bf16),
            vmem((devices, rows, 2 * HD), bf16),
            vmem((devices, 4 * rows, w_query.shape[0]), bf16),
            vmem((4 * rows, quarter), f32),
            vmem((heads, 4 * rows, 2 * HD), bf16),
            vmem((seq, 2 * HD), bf16),
            vmem((seq, 2 * HD), bf16),
            vmem((4 * rows, 4 * rows), f32),
            vmem((4 * rows, 1), f32),
            vmem((4 * rows, 2 * HD), f32),
            vmem((heads // 2, 4 * rows, 2 * HD), bf16),
            vmem((4 * rows, width), bf16),
            vmem((4 * rows, 1024), f32),
            vmem((2, rows, width), f32),
            vmem((2, rows, width), bf16),
            vmem((2, rows, width), bf16),
            vmem((rows, width), bf16),
            vmem((rows, width), bf16),
            dma((2,)),
            dma((devices,)), dma((4,)), dma((3, devices)),
            dma((4,)), dma((3,)),
            dma((devices,)), dma((planes, 4)),
            dma((devices,)), dma((devices,)),
            dma((4, count)), dma((count,)), dma((3, 4, count)),
            dma((count,)), dma((count,)), dma((count,)), dma((count,)),
        ],
        compiler_params=pltpu.CompilerParams(
            collective_id=4, has_side_effects=True, vmem_limit_bytes=LIMIT
        ),
    )(
        tokens, lengths, attn_gain[None, :], w_query, w_key, w_value, sinks, w_out,
        moe_gain[None, :], cosine, sine, meta,
    )


def call(kernel, chips, out_shape, scratch, identity, *args, smem=(), hbm=()):
    single = not isinstance(out_shape, (list, tuple))
    return pl.pallas_call(
        functools.partial(kernel, chips),
        out_shape=out_shape,
        in_specs=[
            pl.BlockSpec(memory_space=pltpu.SMEM)
            if i in smem
            else pl.BlockSpec(memory_space=pl.ANY)
            if i in hbm
            else VMEM
            for i in range(len(args))
        ],
        out_specs=VMEM if single else [VMEM] * len(out_shape),
        scratch_shapes=scratch,
        compiler_params=pltpu.CompilerParams(
            collective_id=identity, has_side_effects=True, vmem_limit_bytes=LIMIT
        ),
    )(*args)


def ring_front(
    tokens, lengths, attn_gain, w_query, w_key, w_value, sinks, w_out, moe_gain, meta
):
    bf16, f32 = jnp.bfloat16, jnp.float32
    tok_rows, width = tokens.shape
    devices = lax.axis_size("ctx")
    chips = devices // 2
    me = lax.axis_index("ctx")
    q_cols = w_query.shape[1]
    num_heads = q_cols // HD
    kv_cols = w_key.shape[1]
    kv_heads = kv_cols // HD
    positions = me * tok_rows + jnp.arange(tok_rows, dtype=jnp.int32)
    freqs = THETA ** (-jnp.arange(HD // 2, dtype=f32) / (HD // 2))
    angles = positions.astype(f32)[:, None] * freqs[None, :]
    cosine, sine = jnp.cos(angles)[:, None, :], jnp.sin(angles)[:, None, :]

    def rotate(values):
        first, second = values[..., : HD // 2], values[..., HD // 2 :]
        return jnp.concatenate(
            [first * cosine - second * sine, second * cosine + first * sine], axis=-1
        ).astype(bf16)

    normed = rms_scale(tokens, attn_gain)
    raw_key = jnp.dot(normed, w_key, preferred_element_type=f32)
    value = jnp.dot(normed, w_value, preferred_element_type=f32).astype(bf16)
    key = rotate(raw_key.reshape(tok_rows, kv_heads, HD)).reshape(tok_rows, kv_cols)
    kv = jnp.concatenate([key, value], axis=1)
    lhs = normed.reshape(tok_rows, devices, width // devices).transpose(1, 0, 2)
    raw_query, kv_all, meta_all = call(
        query_kernel,
        chips,
        [
            jax.ShapeDtypeStruct((tok_rows, q_cols), f32),
            jax.ShapeDtypeStruct((devices,) + kv.shape, bf16),
            jax.ShapeDtypeStruct((devices,) + meta.shape, f32),
        ],
        [pltpu.VMEM((devices,) + w_query.shape, bf16)] + gather_sems(5, chips),
        0,
        lhs, kv, meta, w_query,
    )
    cosine_pair = jnp.tile(cosine[:, 0, :], (1, 4))
    sine_pair = jnp.tile(jnp.concatenate([-sine[:, 0, :], sine[:, 0, :]], axis=1), (1, 2))
    doc_ends = jnp.dot(jnp.tril(jnp.ones((lengths.size,) * 2, jnp.int32)), lengths)
    start = jnp.max(
        jnp.where(positions[:, None] >= doc_ends[None, :], doc_ends[None, :], 0), axis=1
    )[:, None]
    mixed, expert_in = call(
        attend_kernel,
        chips,
        [jax.ShapeDtypeStruct((tok_rows, width), bf16)] * 2,
        [
            pltpu.VMEM((tok_rows, width), f32),
            pltpu.VMEM((devices,) + w_out.shape, bf16),
            pltpu.VMEM((tok_rows, devices * tok_rows), f32),
            pltpu.VMEM((num_heads, tok_rows, HD), bf16),
            pltpu.VMEM((kv_heads, devices * tok_rows, HD), bf16),
            pltpu.VMEM((kv_heads, devices * tok_rows, HD), bf16),
            pltpu.VMEM((devices, tok_rows, w_out.shape[0]), bf16),
        ]
        + gather_sems(3, chips),
        1,
        raw_query, kv_all, cosine_pair, sine_pair, sinks, start, w_out, tokens, moe_gain[None, :],
        smem=(4,),
    )
    return mixed, expert_in, meta_all


def per_device(
    tokens, lengths, attn_gain, w_query, w_key, w_value, sinks, w_out, moe_gain, routes,
    route_weights, w_gate, w_up, w_down,
):
    bf16, f32 = jnp.bfloat16, jnp.float32
    tok_rows, width = tokens.shape
    devices = lax.axis_size("ctx")
    chips = devices // 2
    me = lax.axis_index("ctx")
    experts = chips
    capacity = tok_rows * 4 * 17 // (16 * experts)
    padded = -(-capacity // 16) * 16

    member = routes[:, :, None] == jnp.arange(experts, dtype=jnp.int32)[None, None, :]
    named = jnp.any(member, axis=1)
    lower = jnp.tril(jnp.ones((tok_rows, tok_rows), bf16))
    slot = jnp.dot(lower, named.astype(bf16), preferred_element_type=f32) - 1.0
    slot = jnp.where(named, slot, -1.0)
    routed_weight = jnp.sum(jnp.where(member, route_weights[:, :, None], 0.0), axis=1)
    meta = jnp.concatenate([slot, routed_weight], axis=1).T

    square = lax.axis_size("groups") == 2 and devices == 16
    mixed, expert_in, meta_all = (front if square else ring_front)(
        tokens, lengths, attn_gain, w_query, w_key, w_value, sinks, w_out, moe_gain, meta
    )
    expert = me // 2
    slot_all = lax.dynamic_index_in_dim(meta_all, expert, 1, keepdims=False)
    weight_all = lax.dynamic_index_in_dim(meta_all, experts + expert, 1, keepdims=False)
    places = jnp.arange(padded, dtype=jnp.int32).astype(f32)
    select = (slot_all[:, None, :] == places[None, :, None]).astype(bf16)
    select_back = (slot_all[:, :, None] == places[None, None, :]).astype(bf16)
    partial = call(
        expert_kernel,
        chips,
        jax.ShapeDtypeStruct((devices, padded, width), bf16),
        [
            pltpu.VMEM((devices, tok_rows, width), bf16),
            pltpu.VMEM((4 * padded, width), bf16),
            pltpu.VMEM(w_gate.shape[1:], bf16),
            pltpu.VMEM(w_up.shape[1:], bf16),
            pltpu.VMEM(w_down.shape[:0:-1], bf16),
            pltpu.SemaphoreType.DMA((3,)),
        ]
        + gather_sems(2, chips),
        2,
        expert_in, select, w_gate[0], w_up[0], w_down[0].T,
        hbm=(2, 3, 4),
    )
    return call(
        combine_kernel,
        chips,
        jax.ShapeDtypeStruct((tok_rows, width), bf16),
        [pltpu.VMEM((chips, tok_rows, width), bf16)] * 2
        + [pltpu.VMEM((chips - 1, tok_rows, width), bf16)] * 2
        + ring_sems(2, chips),
        3,
        partial, select_back, weight_all[:, :, None], mixed,
    )


def solution(mesh):
    placed = (
        P(("groups", "ctx"), None),
        P("groups"),
        P(),
        P("ctx", None),
        P(),
        P(),
        P(),
        P("ctx", None),
        P(),
        P(("groups", "ctx"), None),
        P(("groups", "ctx"), None),
        P("ctx", None, None),
        P("ctx", None, None),
        P("ctx", None, None),
    )
    return jax.shard_map(
        per_device,
        mesh=mesh,
        in_specs=placed,
        out_specs=P(("groups", "ctx"), None),
        check_vma=False,
    )
```

```python
import functools

import jax
import jax.numpy as jnp
import numpy as np
from jax import lax
from jax.experimental import pallas as pl
from jax.experimental.pallas import tpu as pltpu
from jax.sharding import PartitionSpec as P

HD = 64
EPS = 1e-05
THETA = 150000.0
ALPHA = 1.702
SCALE = 0.125
NEGATIVE = -1e30
MESH = pl.DeviceIdType.MESH
VMEM = pl.BlockSpec(memory_space=pltpu.VMEM)
LIMIT = 63 * 1024 * 1024


def rms_scale(values, gain_vec):
    wide = values.astype(jnp.float32)
    inverse = lax.rsqrt(jnp.mean(wide * wide, axis=-1, keepdims=True) + EPS)
    return (wide * inverse * gain_vec).astype(jnp.bfloat16)


class Ring:
    def __init__(self, chips):
        self.chips = chips
        self.me = lax.axis_index("ctx")
        self.core = lax.rem(self.me, 2)
        chip = self.me // 2
        self.fold = chips == 8
        if self.fold:
            z, y = chip // 2, lax.rem(chip, 2)
            self.pos = z + y * (chips - 1 - 2 * z)
        else:
            self.pos = chip
        self.way = 1 - 2 * self.core
        self.partner = {"ctx": self.me + self.way}
        self.next = {"ctx": self.owner(-1)}
        self.prev = {"ctx": self.owner(1)}
        group = lax.axis_index("groups")
        self.parity = lax.rem(group, 2)
        self.peer = {"groups": group + 1 - 2 * self.parity}

    def index(self, pos, core):
        pos = lax.rem(pos + 2 * self.chips, self.chips)
        if self.fold:
            y = pos // (self.chips // 2)
            z = pos + y * (self.chips - 1 - 2 * pos)
            chip = z * 2 + y
        else:
            chip = pos
        return chip * 2 + core

    def owner(self, step):
        return self.index(self.pos - self.way * step, self.core)

    def partner_owner(self, step):
        return self.index(self.pos + self.way * step, 1 - self.core)

    def barrier(self, with_peer=False):
        sem = pltpu.get_barrier_semaphore()
        others = [self.next, self.prev, self.partner] + ([self.peer] if with_peer else [])
        for other in others:
            pl.semaphore_signal(sem, inc=1, device_id=other, device_id_type=MESH)
        pl.semaphore_wait(sem, len(others))


def gather_ring(ring, pieces, sems, setup, work):
    ring_send, ring_recv, part_send, part_recv, peer_send, peer_recv = sems
    chips = ring.chips
    ringed = [i for i, piece in enumerate(pieces) if piece[3] != "peer"]
    peered = [i for i, piece in enumerate(pieces) if piece[3] == "peer"]
    shared = [i for i, piece in enumerate(pieces) if piece[3] == "both"]
    lag = 2 if peered else 1

    def copy(i, step, target, send, recv, own=False):
        source, slots, view, _ = pieces[i]
        dst = view(slots.at[ring.owner(step)])
        return pltpu.make_async_remote_copy(
            src_ref=view(source) if own else dst,
            dst_ref=dst,
            send_sem=send,
            recv_sem=recv,
            device_id=target,
            device_id_type=MESH,
        )

    def onward(i, step, own=False):
        return copy(
            i, step, ring.next, ring_send.at[i, step], ring_recv.at[i, step + 1], own
        )

    def across(i, step, own=False):
        return copy(i, step, ring.partner, part_send.at[i, step], part_recv.at[i, step], own)

    def aside(i, step):
        return copy(i, step, ring.peer, peer_send.at[step], peer_recv.at[step])

    def arrived(i, sem, who):
        ref = pieces[i][2](pieces[i][1].at[who])
        pltpu.make_async_copy(ref, ref, sem).wait()

    ring.barrier(bool(peered))
    for i in ringed:
        onward(i, 0, True).start()
    for i in range(len(pieces)):
        across(i, 0, True).start()
    filled = []
    for source, slots, _, _ in pieces:
        if not any(slots is other for other in filled):
            slots[ring.me] = source[...]
            filled.append(slots)
    setup()

    def turn(t, carry):
        @pl.when(t < chips)
        def _():
            for i in ringed:
                arrived(i, ring_recv.at[i, t], ring.owner(t))

                @pl.when(t < chips - 1)
                def _():
                    onward(i, t).start()

                if i in shared:
                    aside(i, t).start()
                across(i, t).start()

        if peered:

            @pl.when((t > 1) & (t <= chips))
            def _():
                for i in peered:
                    arrived(i, peer_recv.at[t - 1], ring.owner(t - 1))
                    across(i, t - 1).start()

        @pl.when(t >= lag)
        def _():
            s = t - lag
            for i in range(len(pieces)):
                arrived(i, part_recv.at[i, s], ring.partner_owner(s))
            work(s)

        return carry

    lax.fori_loop(1, chips + lag, turn, 0)

    def drain(s, carry):
        for i in range(len(pieces)):
            across(i, s).wait_send()
        for i in ringed:

            @pl.when(s < chips - 1)
            def _():
                onward(i, s).wait_send()

        for i in shared:

            @pl.when(s > 0)
            def _():
                aside(i, s).wait_send()

        return carry

    lax.fori_loop(0, chips, drain, 0)


def ring_sems(count, chips):
    return [pltpu.SemaphoreType.DMA((count, chips))] * 4


def gather_sems(count, chips):
    return ring_sems(count, chips) + [pltpu.SemaphoreType.DMA((chips,))] * 2


def whole(ref):
    return ref


def cols(start, size):
    return lambda ref: ref.at[:, pl.ds(start, size)]


def rows(start, size):
    return lambda ref: ref.at[pl.ds(start, size), :]


def thirds(ring, source, slots):
    width = source.shape[1]
    third = width // 3 // 128 * 128
    mine = pl.multiple_of(ring.parity * third, 128)
    other = pl.multiple_of((1 - ring.parity) * third, 128)
    return [
        (source, slots, cols(mine, third), "both"),
        (source, slots, cols(2 * third, width - 2 * third), "ring"),
        (source, slots, cols(other, third), "peer"),
    ]


def query_kernel(chips, lhs, kv, meta, weight, out, kv_all, meta_all, slots, *sems):
    ring = Ring(chips)
    pieces = [(kv, kv_all, whole, "ring"), (meta, meta_all, whole, "ring")]
    pieces += thirds(ring, weight, slots)

    def setup():
        out[...] = jnp.zeros_like(out)

    def work(s):
        for who in (ring.owner(s), ring.partner_owner(s)):
            out[...] += jnp.dot(lhs[who], slots[who], preferred_element_type=jnp.float32)

    gather_ring(ring, pieces, sems, setup, work)


def attend_kernel(
    chips, raw, kv_all, cosine, sine, sinks, start, weight, tokens, gain,
    mixed_out, expert_in, out, slots, bias, query, key, value, attended, *sems
):
    ring = Ring(chips)
    blocks, tok_rows, width = attended.shape
    per_block = width // HD
    kv_heads, seq, _ = key.shape
    group = query.shape[0] // kv_heads
    pieces = thirds(ring, weight, slots)

    def setup():
        key_pos = lax.broadcasted_iota(jnp.int32, (tok_rows, seq), 1)
        row_pos = lax.broadcasted_iota(jnp.int32, (tok_rows, seq), 0) + ring.me * tok_rows
        allowed = (key_pos <= row_pos) & (key_pos >= start[...])
        bias[...] = jnp.where(allowed, 0.0, NEGATIVE)
        lane = lax.broadcasted_iota(jnp.int32, (tok_rows, 2 * HD), 1)
        first = lax.rem(lane, HD) < HD // 2

        def turn_pair(j, carry):
            pair = raw[:, pl.ds(pl.multiple_of(j * 2 * HD, 2 * HD), 2 * HD)]
            other = jnp.where(
                first, pltpu.roll(pair, 2 * HD - HD // 2, 1), pltpu.roll(pair, HD // 2, 1)
            )
            turned = ((pair * cosine[...] + other * sine[...]) * SCALE).astype(jnp.bfloat16)
            query[2 * j] = turned[:, :HD]
            query[2 * j + 1] = turned[:, HD:]
            return carry

        lax.fori_loop(0, query.shape[0] // 2, turn_pair, 0)

        def unpack(d, carry):
            at = pl.ds(pl.multiple_of(d * tok_rows, tok_rows), tok_rows)
            block = kv_all[d]
            for g in range(kv_heads):
                key[g, at, :] = block[:, g * HD : (g + 1) * HD]
                value[g, at, :] = block[:, (kv_heads + g) * HD : (kv_heads + g + 1) * HD]
            return carry

        lax.fori_loop(0, blocks, unpack, 0)

    def attend(who):
        heads = []
        for j in range(per_block):
            head = who * per_block + j
            kv_head = head // group
            scores = (
                lax.dot_general(
                    query[head],
                    key[kv_head],
                    (((1,), (1,)), ((), ())),
                    preferred_element_type=jnp.float32,
                )
                + bias[...]
            )
            sink = sinks[head]
            top = jnp.maximum(jnp.max(scores, axis=1, keepdims=True), sink)
            weights = jnp.exp(scores - top)
            total = jnp.sum(weights, axis=1, keepdims=True) + jnp.exp(sink - top)
            mixed = jnp.dot(
                weights.astype(jnp.bfloat16), value[kv_head], preferred_element_type=jnp.float32
            )
            heads.append(mixed / total)
        joined = heads[0] if per_block == 1 else jnp.concatenate(heads, axis=1)
        attended[who] = joined.astype(jnp.bfloat16)

    def work(s):
        attend(ring.owner(s))
        attend(ring.partner_owner(s))

    gather_ring(ring, pieces, sems, setup, work)
    out[...] = tokens[...].astype(jnp.float32)

    def project(d, carry):
        out[...] += jnp.dot(attended[d], slots[d], preferred_element_type=jnp.float32)
        return carry

    lax.fori_loop(0, blocks, project, 0)
    mixed_out[...] = out[...].astype(jnp.bfloat16)
    expert_in[...] = rms_scale(mixed_out[...], gain[...])


def expert_kernel(
    chips, rows_in, select, w_gate, w_up, w_down,
    out, slots, packed, gate, up, down, load_sem, *sems
):
    ring = Ring(chips)
    half = rows_in.shape[0] // 2
    padded = select.shape[1]
    pieces = [
        (rows_in, slots, rows(0, half), "ring"),
        (rows_in, slots, rows(half, half), "ring"),
    ]
    loads = [
        pltpu.make_async_copy(source, target, load_sem.at[i])
        for i, (source, target) in enumerate(((w_gate, gate), (w_up, up), (w_down, down)))
    ]
    for load in loads:
        load.start()

    def work(s):
        whose = [
            ring.owner(s - 1), ring.partner_owner(s - 1), ring.owner(s), ring.partner_owner(s)
        ]

        @pl.when(s == 1)
        def _():
            for load in loads:
                load.wait()

        @pl.when(lax.rem(s, 2) == 1)
        def _():
            for j, who in enumerate(whose):
                packed[j * padded : (j + 1) * padded, :] = jnp.dot(
                    select[who], slots[who], preferred_element_type=jnp.float32
                ).astype(jnp.bfloat16)
            gate_val = jnp.dot(packed[...], gate[...], preferred_element_type=jnp.float32)
            up_val = jnp.dot(packed[...], up[...], preferred_element_type=jnp.float32)
            hidden = (up_val + 1.0) * gate_val * jax.nn.sigmoid(ALPHA * gate_val)
            partial = lax.dot_general(
                hidden.astype(jnp.bfloat16),
                down[...],
                (((1,), (1,)), ((), ())),
                preferred_element_type=jnp.float32,
            ).astype(jnp.bfloat16)
            for j, who in enumerate(whose):
                out[who] = partial[j * padded : (j + 1) * padded, :]

    gather_ring(ring, pieces, sems, lambda: None, work)


def combine_kernel(
    chips, partial, select, weights, mixed, out, cross_out, cross_in, ring_out, ring_in,
    ring_send, ring_recv, part_send, part_recv,
):
    ring = Ring(chips)
    tok_rows = mixed.shape[0]
    half = tok_rows // 2
    ring.barrier()

    def share(who, h):
        at = pl.ds(h * half, half)
        spread = jnp.dot(select[who, at, :], partial[who], preferred_element_type=jnp.float32)
        return spread * weights[who, at, :]

    def crossing(s, h):
        at = pl.ds(h * half, half)
        return pltpu.make_async_remote_copy(
            src_ref=cross_out.at[s, at, :],
            dst_ref=cross_in.at[s, at, :],
            send_sem=part_send.at[h, s],
            recv_sem=part_recv.at[h, s],
            device_id=ring.partner,
            device_id_type=MESH,
        )

    def onward(s, h):
        at = pl.ds(h * half, half)
        return pltpu.make_async_remote_copy(
            src_ref=ring_out.at[s, at, :],
            dst_ref=ring_in.at[s, at, :],
            send_sem=ring_send.at[h, s],
            recv_sem=ring_recv.at[h, s],
            device_id=ring.next,
            device_id_type=MESH,
        )

    def give(s):
        who = ring.partner_owner(s + 1)
        for h in range(2):
            at = pl.ds(h * half, half)
            cross_out[s, at, :] = share(who, h).astype(jnp.bfloat16)
            crossing(s, h).start()

    def own(s, h):
        total = share(ring.owner(s + 1), h)
        crossing(s, h).wait_recv()
        return total + cross_in[s, pl.ds(h * half, half), :].astype(jnp.float32)

    give(0)
    for h in range(2):
        ring_out[0, pl.ds(h * half, half), :] = own(0, h).astype(jnp.bfloat16)
        onward(0, h).start()
    give(1)

    def step(s, carry):
        for h in range(2):
            at = pl.ds(h * half, half)
            total = own(s, h)
            onward(s - 1, h).wait_recv()
            total = total + ring_in[s - 1, at, :].astype(jnp.float32)
            ring_out[s, at, :] = total.astype(jnp.bfloat16)
            onward(s, h).start()
        give(s + 1)
        return carry

    lax.fori_loop(1, chips - 1, step, 0)
    last = chips - 1
    for h in range(2):
        at = pl.ds(h * half, half)
        total = own(last, h)
        onward(last - 1, h).wait_recv()
        total = total + ring_in[last - 1, at, :].astype(jnp.float32)
        out[at, :] = (mixed[at, :].astype(jnp.float32) + total).astype(jnp.bfloat16)

    def drain(s, carry):
        for h in range(2):
            crossing(s, h).wait_send()

            @pl.when(s < chips - 1)
            def _():
                onward(s, h).wait_send()

        return carry

    lax.fori_loop(0, chips, drain, 0)


LOG2E = 1.4426950408889634
ANY = pl.BlockSpec(memory_space=pl.ANY)
SMEM = pl.BlockSpec(memory_space=pltpu.SMEM)


class Copies:
    def __init__(self):
        self.made = []

    def send(self, make, pred=None):
        self.made.append((make, pred))
        if pred is None:
            make().start()
        else:
            pl.when(pred)(lambda: make().start())

    def drain(self):
        for make, pred in self.made:
            if pred is None:
                make().wait_send()
            else:
                pl.when(pred)(lambda make=make: make().wait_send())


def remote(src, dst, send_sem, recv_sem, where):
    return pltpu.make_async_remote_copy(
        src_ref=src, dst_ref=dst, send_sem=send_sem, recv_sem=recv_sem,
        device_id=where, device_id_type=MESH,
    )


def landed(ref, sem):
    pltpu.make_async_copy(ref, ref, sem).wait()


def spans(width, size):
    return [(at, min(size, width - at)) for at in range(0, width, size)]


def front_kernel(
    planes, tokens_t, lengths, attn_gain, w_query, w_key, w_value, sinks, w_out, moe_gain,
    angles, routes, weights_in, mixed_out, expert_in, meta_all,
    tokens, table, meta, normed, wq, wkv, kv_own, kv_all, lhs, raw, qx, kx, vx, bias, top, acc, attended, wo,
    part, held, k_out, k_in, y_out, y_in,
    load_sem, wq_recv, wq_plane, wq_send, norm_recv, norm_send, kv_recv, kv_send,
    meta_recv, meta_send, wo_recv, wo_plane, wo_send, k_recv, k_send, y_recv, y_send,
):
    f32, bf16 = jnp.float32, jnp.bfloat16
    x, c = lax.axis_index("groups"), lax.axis_index("ctx")
    z, y, k, d = c // 4, lax.rem(c // 2, 2), lax.rem(c, 2), lax.rem(c, 4)
    total = 4 * planes
    width, rows = tokens_t.shape
    wq_rows, qcols = wq.shape[1], wq.shape[2]
    heads = qx.shape[0]
    plane_rows = 4 * rows
    partner, across = {"ctx": c + 1 - 2 * k}, {"ctx": c + 2 - 4 * y}
    peer = {"groups": 1 - x}
    copies = Copies()

    loads = [
        pltpu.make_async_copy(w_key, wkv.at[0], load_sem.at[0]),
        pltpu.make_async_copy(w_value, wkv.at[1], load_sem.at[1]),
        pltpu.make_async_copy(
            angles.at[:, pl.ds(z * plane_rows, plane_rows), :], table, load_sem.at[2]
        ),
        pltpu.make_async_copy(w_query.at[:, pl.ds(d * qcols, qcols)], wq.at[c], wq_recv.at[c]),
    ]
    cosine, sine = table.at[0], table.at[1]
    for load in loads:
        load.start()

    barrier = pltpu.get_barrier_semaphore()
    for r in range(1, total):
        pl.semaphore_signal(
            barrier, inc=1, device_id={"ctx": lax.rem(c + r, total)}, device_id_type=MESH
        )
    pl.semaphore_signal(barrier, inc=1, device_id=peer, device_id_type=MESH)
    pl.semaphore_wait(barrier, total)

    for r in (2, 3, 1):
        other = jnp.bitwise_xor(d, r)
        copies.send(
            lambda r=r, other=other: remote(
                w_query.at[:, pl.ds(other * qcols, qcols)], wq.at[c],
                wq_plane.at[r], wq_recv.at[c], {"ctx": 4 * z + other},
            )
        )
    tokens[...] = tokens_t[...].T
    normed[d] = rms_scale(tokens[...], attn_gain[...][None, :])
    copies.send(
        lambda: remote(normed.at[d], normed.at[d], norm_send.at[0], norm_recv.at[d], across)
    )
    copies.send(
        lambda: remote(normed.at[d], normed.at[d], norm_send.at[1], norm_recv.at[d], partner)
    )

    def wq_relay(who, right, left, side):
        landed(wq.at[who], wq_recv.at[who])
        for i, (where, pred) in enumerate(
            (({"ctx": c + 4}, right), ({"ctx": c - 4}, left), (peer, side))
        ):
            if pred is not None:
                copies_start(
                    lambda i=i, where=where: remote(
                        wq.at[who], wq.at[who], wq_send.at[i, who], wq_recv.at[who], where
                    ),
                    pred,
                )

    def copies_start(make, pred):
        pl.when(pred)(lambda: make().start())

    upper, lower = z < planes - 1, z > 0
    always = z >= 0
    wq_relay(4 * z + 2 * y + x, upper, lower, None)

    for load in loads[:3]:
        load.wait()
    own = normed[d]
    lane = lax.broadcasted_iota(jnp.int32, (rows, 2 * HD), 1)
    first = lax.rem(lane, HD) < HD // 2
    mine = pl.ds(pl.multiple_of(d * rows, rows), rows)
    turn_cos, turn_sin = cosine[mine, :], sine[mine, :]

    def turned(pair, cos, sin, low):
        other = jnp.where(
            low, pltpu.roll(pair, 2 * HD - HD // 2, 1), pltpu.roll(pair, HD // 2, 1)
        )
        return pair * cos + other * sin

    raw_key = jnp.dot(own, wkv[0], preferred_element_type=f32)
    raw_value = jnp.dot(own, wkv[1], preferred_element_type=f32)
    for j in range(2):
        at = slice(j * 2 * HD, (j + 1) * 2 * HD)
        keys = turned(raw_key[:, at], turn_cos, turn_sin, first)
        values = raw_value[:, at]
        kv_own[2 * j] = jnp.where(lane < HD, keys, pltpu.roll(values, HD, 1)).astype(bf16)
        kv_own[2 * j + 1] = jnp.where(lane < HD, pltpu.roll(keys, HD, 1), values).astype(bf16)
    kv_all[c] = kv_own[d]

    def kv_copy(dz, other):
        return lambda: remote(
            kv_own.at[other], kv_all.at[c], kv_send.at[dz, other], kv_recv.at[c],
            {"ctx": 4 * (z + dz) + other},
        )

    wq_relay(4 * z + 2 * (1 - y) + x, upper, lower, None)
    for dz in range(planes):
        for other in range(4):
            pred = (z + dz < planes) if dz else (d != other)
            copies.send(kv_copy(dz, other), pred)
    experts = meta.shape[0] // 2
    expert = lax.broadcasted_iota(jnp.int32, (experts, rows), 0)
    named, chosen = jnp.zeros((experts, rows), f32), jnp.zeros((experts, rows), f32)
    for t in range(routes.shape[0]):
        same = routes[t : t + 1, :] == expert
        named += jnp.where(same, 1.0, 0.0)
        chosen += jnp.where(same, weights_in[t : t + 1, :], 0.0)
    tri = (rows, rows)
    upto = lax.broadcasted_iota(jnp.int32, tri, 0) <= lax.broadcasted_iota(jnp.int32, tri, 1)
    place = jnp.dot(
        named.astype(bf16), jnp.where(upto, 1.0, 0.0).astype(bf16), preferred_element_type=f32
    )
    meta[:experts, :] = jnp.where(named > 0.5, place - 1.0, -1.0)
    meta[experts:, :] = chosen
    meta_all[c] = meta[...]
    for r in range(1, total):
        copies.send(
            lambda r=r: remote(
                meta, meta_all.at[c], meta_send.at[r], meta_recv.at[c],
                {"ctx": lax.rem(c + r, total)},
            )
        )

    def wo_rows(i):
        return pl.ds(pl.multiple_of(i * rows, rows), rows)

    wo_spans = spans(width, 1024)

    def wo_hand(n):
        at, size = wo_spans[n]
        return remote(
            w_out.at[pl.ds(at, size), :], wo.at[pl.ds(at, size), wo_rows(d)],
            wo_plane.at[n], wo_recv.at[d, n], {"ctx": 5 * z},
        )

    def wo_keep(n):
        at, size = wo_spans[n]
        return pltpu.make_async_copy(
            w_out.at[pl.ds(at, size), :], wo.at[pl.ds(at, size), wo_rows(d)], wo_recv.at[d, n]
        )

    for s in range(1, planes):
        for j in range(2):

            @pl.when(z >= s)
            def _(s=s, j=j):
                wq_relay(4 * (z - s) + 2 * j + x, upper, None, always)

            @pl.when(z + s < planes)
            def _(s=s, j=j):
                wq_relay(4 * (z + s) + 2 * j + x, None, lower, always)

        if s == 1:
            for n in range(len(wo_spans)):
                pl.when(d == z)(lambda n=n: wo_keep(n).start())
                copies.send(lambda n=n: wo_hand(n), d != z)
            opposite = jnp.bitwise_xor(d, 2)
            landed(normed.at[opposite], norm_recv.at[opposite])
            copies.send(
                lambda: remote(
                    normed.at[opposite], normed.at[opposite],
                    norm_send.at[2], norm_recv.at[opposite], partner,
                )
            )

    def wo_relay(n, j):
        at, size = wo_spans[n]
        i = 2 * j + x
        piece = wo.at[pl.ds(at, size), wo_rows(i)]
        landed(piece, wo_recv.at[i, n])
        for way, (where, pred) in enumerate(wo_ways()):
            copies_start(
                lambda way=way, where=where: remote(
                    piece, piece, wo_send.at[way, i, n], wo_recv.at[i, n], where
                ),
                pred,
            )

    def wo_ways():
        return (
            ({"ctx": c + 4}, upper & (z >= d)),
            ({"ctx": c - 4}, lower & (z <= d)),
            (peer, z != d),
        )

    def wo_stage(stage):
        for n in range(len(wo_spans)):
            for j in range(2):
                jj = jnp.bitwise_xor(j, y)
                away = stage - n
                if stage == 0:
                    pl.when(z == d)(lambda n=n, jj=jj: wo_relay(n, jj))
                elif 0 < away < planes:
                    pl.when(jnp.abs(z - d) == away)(lambda n=n, jj=jj: wo_relay(n, jj))

    for r in (1, 3):
        other = jnp.bitwise_xor(d, r)
        landed(normed.at[other], norm_recv.at[other])
    for t in range(4):
        block = normed[t]
        for j in range(total):
            lhs[j, t * rows : (t + 1) * rows, :] = block[:, j * wq_rows : (j + 1) * wq_rows]

    wo_stage(0)
    raw[...] = jnp.zeros_like(raw)

    def query_rows(plane):
        for i in range(4):
            who = 4 * plane + i
            raw[...] += jnp.dot(lhs[who], wq[who], preferred_element_type=f32)

    query_rows_wait = lambda plane, i: landed(wq.at[4 * plane + i], wq_recv.at[4 * plane + i])
    for i in range(2):
        query_rows_wait(z, 2 * i + 1 - x)
    query_rows(z)
    for s in range(1, planes):
        for step in (-s, s):

            @pl.when((z + step >= 0) & (z + step < planes))
            def _(step=step):
                for i in range(2):
                    query_rows_wait(z + step, 2 * i + 1 - x)
                query_rows(z + step)

    ends = [lengths[0]]
    for i in range(1, lengths.shape[0]):
        ends.append(ends[-1] + lengths[i])

    def segment(start, shape):
        place = start + lax.broadcasted_iota(jnp.int32, shape, 0)
        found = jnp.zeros(shape, jnp.int32)
        for end in ends:
            found += (place >= end).astype(jnp.int32)
        return found

    wide = (plane_rows, 2 * HD)
    wide_lane = lax.broadcasted_iota(jnp.int32, wide, 1)
    mark = jnp.where(
        (wide_lane - HD == segment(z * plane_rows, wide)) & (wide_lane >= HD), 1.0, 0.0
    )
    wide_first = lax.rem(wide_lane, HD) < HD // 2

    for j in range(heads // 2):
        pair = turned(
            raw[:, j * 2 * HD : (j + 1) * 2 * HD], cosine[...], sine[...], wide_first
        ) * (SCALE * LOG2E)
        qx[2 * j] = jnp.where(wide_lane < HD, pair, mark).astype(bf16)
        qx[2 * j + 1] = jnp.where(wide_lane < HD, pltpu.roll(pair, HD, 1), mark).astype(bf16)

    def unpack(i, carry):
        @pl.when(i != c)
        def _():
            landed(kv_all.at[i], kv_recv.at[i])

        both = kv_all[i].astype(f32)
        apart = jnp.where(
            (lane - HD == segment(i * rows, lane.shape)) | (lane >= HD + len(ends)), 0.0, NEGATIVE
        )
        at = pl.ds(pl.multiple_of(i * rows, rows), rows)
        kx[at, :] = jnp.where(lane < HD, both, apart).astype(bf16)
        ones = jnp.where(lane == HD, 1.0, 0.0)
        vx[at, :] = jnp.where(lane < HD, pltpu.roll(both, HD, 1), ones).astype(bf16)
        return carry

    lax.fori_loop(0, 4 * (z + 1), unpack, 0)
    square = (plane_rows, plane_rows)
    bias[...] = jnp.where(
        lax.broadcasted_iota(jnp.int32, square, 1) <= lax.broadcasted_iota(jnp.int32, square, 0),
        0.0, NEGATIVE,
    )

    wo_stage(1)

    def attend(h):
        top[...] = jnp.full(top.shape, sinks[d * heads + h] * LOG2E, f32)
        acc[...] = jnp.where(wide_lane == HD, 1.0, 0.0)

        def block(b, last):
            at = pl.ds(pl.multiple_of(b * plane_rows, plane_rows), plane_rows)
            scores = lax.dot_general(
                qx[h], kx[at, :], (((1,), (1,)), ((), ())), preferred_element_type=f32
            )
            if last:
                scores += bias[...]
            old = top[...]
            new = jnp.maximum(old, jnp.max(scores, axis=1, keepdims=True))
            weights = jnp.exp2(scores - new).astype(bf16)
            acc[...] = acc[...] * jnp.exp2(old - new) + jnp.dot(
                weights, vx[at, :], preferred_element_type=f32
            )
            top[...] = new

        def body(b, carry):
            block(b, False)
            return carry

        lax.fori_loop(0, z, body, 0)
        block(z, True)
        found = acc[...]
        return found / found[:, HD : HD + 1]

    def pair_of_heads(j, carry):
        for stage in range(1, heads // 2):
            pl.when(j == stage)(lambda stage=stage: wo_stage(stage + 1))
        even = attend(2 * j)
        part[:, : 2 * HD] = even
        odd = attend(2 * j + 1)
        both = jnp.where(wide_lane < HD, part[:, : 2 * HD], pltpu.roll(odd, HD, 1))
        attended[j] = both.astype(bf16)
        return carry

    lax.fori_loop(0, heads // 2, pair_of_heads, 0)
    wo_stage(5)

    lhs_out = jnp.concatenate([attended[j] for j in range(heads // 2)], axis=1)
    give, keep = 1 - k, k

    def k_copy(n):
        at, size = wo_spans[n]
        return remote(
            k_out.at[:, :, pl.ds(at, size)], k_in.at[:, :, pl.ds(at, size)],
            k_send.at[n], k_recv.at[n], partner,
        )

    def y_copy(n):
        at, size = wo_spans[n]
        return remote(
            y_out.at[:, pl.ds(at, size)], y_in.at[:, pl.ds(at, size)],
            y_send.at[n], y_recv.at[n], across,
        )

    def project(n):
        at, size = wo_spans[n]
        cols = pl.ds(at, size)
        for j in range(2):
            i = 2 * j + 1 - x
            landed(wo.at[cols, wo_rows(i)], wo_recv.at[i, n])
        part[:, :size] = lax.dot_general(
            lhs_out, wo[cols, :], (((1,), (1,)), ((), ())), preferred_element_type=f32
        )
        for j in range(2):
            k_out[j, :, cols] = part[wo_rows(2 * j + give), :size].astype(bf16)
            held[j, :, cols] = part[wo_rows(2 * j + keep), :size]
        copies.send(lambda: k_copy(n))

    def fold(n):
        at, size = wo_spans[n]
        cols = pl.ds(at, size)
        k_copy(n).wait_recv()
        y_out[:, cols] = (held[1 - y, :, cols] + k_in[1 - y, :, cols].astype(f32)).astype(bf16)
        copies.send(lambda: y_copy(n))

    def finish(n):
        at, size = wo_spans[n]
        cols = pl.ds(at, size)
        mine = held[y, :, cols] + k_in[y, :, cols].astype(f32) + tokens[:, cols].astype(f32)
        y_copy(n).wait_recv()
        mixed_out[:, cols] = (mine + y_in[:, cols].astype(f32)).astype(bf16)

    count = len(wo_spans)
    for n in range(count):
        project(n)
        if n:
            fold(n - 1)
    fold(count - 1)
    for n in range(count):
        finish(n)
    expert_in[...] = rms_scale(mixed_out[...], moe_gain[...][None, :])

    def meta_arrived(i, carry):
        @pl.when(i != c)
        def _():
            landed(meta_all.at[i], meta_recv.at[i])

        return carry

    lax.fori_loop(0, total, meta_arrived, 0)
    copies.drain()

    def wq_drain(who, ways):
        for i, pred in enumerate(ways):
            pl.when(pred)(
                lambda i=i: remote(
                    wq.at[who], wq.at[who], wq_send.at[i, who], wq_recv.at[who], partner
                ).wait_send()
            )

    never = z < 0
    for j in range(2):
        wq_drain(4 * z + 2 * j + x, (upper, lower))
    for s in range(1, planes):
        for j in range(2):
            pl.when(z >= s)(
                lambda s=s, j=j: wq_drain(4 * (z - s) + 2 * j + x, (upper, never, always))
            )
            pl.when(z + s < planes)(
                lambda s=s, j=j: wq_drain(4 * (z + s) + 2 * j + x, (never, lower, always))
            )
    for n, (at, size) in enumerate(wo_spans):
        for j in range(2):
            i = 2 * j + x
            piece = wo.at[pl.ds(at, size), wo_rows(i)]
            for way, (where, pred) in enumerate(wo_ways()):
                pl.when(pred)(
                    lambda way=way, where=where: remote(
                        piece, piece, wo_send.at[way, i, n], wo_recv.at[i, n], where
                    ).wait_send()
                )


def front(tokens, lengths, attn_gain, w_query, w_key, w_value, sinks, w_out, moe_gain, routes, weights):
    bf16, f32 = jnp.bfloat16, jnp.float32
    rows, width = tokens.shape
    devices = lax.axis_size("ctx")
    planes = devices // 4
    seq = devices * rows
    quarter = w_query.shape[1] // 4
    heads = quarter // HD
    count = len(spans(width, 1024))
    place = np.arange(seq, dtype=np.float32)
    freqs = np.float32(THETA) ** (-np.arange(HD // 2, dtype=np.float32) / np.float32(HD // 2))
    angles = place[:, None] * freqs[None, :].astype(np.float32)
    cos, sin = np.cos(angles).astype(np.float32), np.sin(angles).astype(np.float32)
    tables = np.stack(
        [np.tile(cos, (1, 4)), np.tile(np.concatenate([-sin, sin], axis=1), (1, 2))]
    )
    meta_shape = (devices, rows)
    dma = pltpu.SemaphoreType.DMA
    vmem = pltpu.VMEM
    return pl.pallas_call(
        functools.partial(front_kernel, planes),
        out_shape=[
            jax.ShapeDtypeStruct((rows, width), bf16),
            jax.ShapeDtypeStruct((rows, width), bf16),
            jax.ShapeDtypeStruct((devices,) + meta_shape, f32),
        ],
        in_specs=[VMEM, SMEM, VMEM, ANY, ANY, ANY, SMEM, ANY, VMEM, ANY, VMEM, VMEM],
        out_specs=[VMEM] * 3,
        scratch_shapes=[
            vmem((rows, width), bf16),
            vmem((2, 4 * rows, 2 * HD), f32),
            vmem(meta_shape, f32),
            vmem((4, rows, width), bf16),
            vmem((devices, w_query.shape[0], quarter), bf16),
            vmem((2,) + w_key.shape, bf16),
            vmem((4, rows, 2 * HD), bf16),
            vmem((devices, rows, 2 * HD), bf16),
            vmem((devices, 4 * rows, w_query.shape[0]), bf16),
            vmem((4 * rows, quarter), f32),
            vmem((heads, 4 * rows, 2 * HD), bf16),
            vmem((seq, 2 * HD), bf16),
            vmem((seq, 2 * HD), bf16),
            vmem((4 * rows, 4 * rows), f32),
            vmem((4 * rows, 1), f32),
            vmem((4 * rows, 2 * HD), f32),
            vmem((heads // 2, 4 * rows, 2 * HD), bf16),
            vmem((width, 4 * rows), bf16),
            vmem((4 * rows, 1024), f32),
            vmem((2, rows, width), f32),
            vmem((2, rows, width), bf16),
            vmem((2, rows, width), bf16),
            vmem((rows, width), bf16),
            vmem((rows, width), bf16),
            dma((3,)),
            dma((devices,)), dma((4,)), dma((3, devices)),
            dma((4,)), dma((3,)),
            dma((devices,)), dma((planes, 4)),
            dma((devices,)), dma((devices,)),
            dma((4, count)), dma((count,)), dma((3, 4, count)),
            dma((count,)), dma((count,)), dma((count,)), dma((count,)),
        ],
        compiler_params=pltpu.CompilerParams(
            collective_id=4, has_side_effects=True, vmem_limit_bytes=LIMIT
        ),
    )(
        tokens.T, lengths, attn_gain, w_query, w_key, w_value, sinks, w_out.T,
        moe_gain, jnp.asarray(tables), routes.T, weights.T,
    )


def call(kernel, chips, out_shape, scratch, identity, *args, smem=(), hbm=()):
    single = not isinstance(out_shape, (list, tuple))
    return pl.pallas_call(
        functools.partial(kernel, chips),
        out_shape=out_shape,
        in_specs=[
            pl.BlockSpec(memory_space=pltpu.SMEM)
            if i in smem
            else pl.BlockSpec(memory_space=pl.ANY)
            if i in hbm
            else VMEM
            for i in range(len(args))
        ],
        out_specs=VMEM if single else [VMEM] * len(out_shape),
        scratch_shapes=scratch,
        compiler_params=pltpu.CompilerParams(
            collective_id=identity, has_side_effects=True, vmem_limit_bytes=LIMIT
        ),
    )(*args)


def ring_front(
    tokens, lengths, attn_gain, w_query, w_key, w_value, sinks, w_out, moe_gain, routes,
    route_weights,
):
    bf16, f32 = jnp.bfloat16, jnp.float32
    tok_rows, width = tokens.shape
    devices = lax.axis_size("ctx")
    chips = devices // 2
    me = lax.axis_index("ctx")
    q_cols = w_query.shape[1]
    num_heads = q_cols // HD
    kv_cols = w_key.shape[1]
    kv_heads = kv_cols // HD
    experts = chips
    member = routes[:, :, None] == jnp.arange(experts, dtype=jnp.int32)[None, None, :]
    named = jnp.any(member, axis=1)
    lower = jnp.tril(jnp.ones((tok_rows, tok_rows), bf16))
    slot = jnp.dot(lower, named.astype(bf16), preferred_element_type=f32) - 1.0
    slot = jnp.where(named, slot, -1.0)
    routed_weight = jnp.sum(jnp.where(member, route_weights[:, :, None], 0.0), axis=1)
    meta = jnp.concatenate([slot, routed_weight], axis=1).T

    positions = me * tok_rows + jnp.arange(tok_rows, dtype=jnp.int32)
    freqs = THETA ** (-jnp.arange(HD // 2, dtype=f32) / (HD // 2))
    angles = positions.astype(f32)[:, None] * freqs[None, :]
    cosine, sine = jnp.cos(angles)[:, None, :], jnp.sin(angles)[:, None, :]

    def rotate(values):
        first, second = values[..., : HD // 2], values[..., HD // 2 :]
        return jnp.concatenate(
            [first * cosine - second * sine, second * cosine + first * sine], axis=-1
        ).astype(bf16)

    normed = rms_scale(tokens, attn_gain)
    raw_key = jnp.dot(normed, w_key, preferred_element_type=f32)
    value = jnp.dot(normed, w_value, preferred_element_type=f32).astype(bf16)
    key = rotate(raw_key.reshape(tok_rows, kv_heads, HD)).reshape(tok_rows, kv_cols)
    kv = jnp.concatenate([key, value], axis=1)
    lhs = normed.reshape(tok_rows, devices, width // devices).transpose(1, 0, 2)
    raw_query, kv_all, meta_all = call(
        query_kernel,
        chips,
        [
            jax.ShapeDtypeStruct((tok_rows, q_cols), f32),
            jax.ShapeDtypeStruct((devices,) + kv.shape, bf16),
            jax.ShapeDtypeStruct((devices,) + meta.shape, f32),
        ],
        [pltpu.VMEM((devices,) + w_query.shape, bf16)] + gather_sems(5, chips),
        0,
        lhs, kv, meta, w_query,
    )
    cosine_pair = jnp.tile(cosine[:, 0, :], (1, 4))
    sine_pair = jnp.tile(jnp.concatenate([-sine[:, 0, :], sine[:, 0, :]], axis=1), (1, 2))
    doc_ends = jnp.dot(jnp.tril(jnp.ones((lengths.size,) * 2, jnp.int32)), lengths)
    start = jnp.max(
        jnp.where(positions[:, None] >= doc_ends[None, :], doc_ends[None, :], 0), axis=1
    )[:, None]
    mixed, expert_in = call(
        attend_kernel,
        chips,
        [jax.ShapeDtypeStruct((tok_rows, width), bf16)] * 2,
        [
            pltpu.VMEM((tok_rows, width), f32),
            pltpu.VMEM((devices,) + w_out.shape, bf16),
            pltpu.VMEM((tok_rows, devices * tok_rows), f32),
            pltpu.VMEM((num_heads, tok_rows, HD), bf16),
            pltpu.VMEM((kv_heads, devices * tok_rows, HD), bf16),
            pltpu.VMEM((kv_heads, devices * tok_rows, HD), bf16),
            pltpu.VMEM((devices, tok_rows, w_out.shape[0]), bf16),
        ]
        + gather_sems(3, chips),
        1,
        raw_query, kv_all, cosine_pair, sine_pair, sinks, start, w_out, tokens, moe_gain[None, :],
        smem=(4,),
    )
    return mixed, expert_in, meta_all


def per_device(
    tokens, lengths, attn_gain, w_query, w_key, w_value, sinks, w_out, moe_gain, routes,
    route_weights, w_gate, w_up, w_down,
):
    bf16, f32 = jnp.bfloat16, jnp.float32
    tok_rows, width = tokens.shape
    devices = lax.axis_size("ctx")
    chips = devices // 2
    me = lax.axis_index("ctx")
    experts = chips
    capacity = tok_rows * 4 * 17 // (16 * experts)
    padded = -(-capacity // 16) * 16

    square = lax.axis_size("groups") == 2 and devices == 16
    mixed, expert_in, meta_all = (front if square else ring_front)(
        tokens, lengths, attn_gain, w_query, w_key, w_value, sinks, w_out, moe_gain, routes,
        route_weights,
    )
    expert = me // 2
    slot_all = lax.dynamic_index_in_dim(meta_all, expert, 1, keepdims=False)
    weight_all = lax.dynamic_index_in_dim(meta_all, experts + expert, 1, keepdims=False)
    places = jnp.arange(padded, dtype=jnp.int32).astype(f32)
    select = (slot_all[:, None, :] == places[None, :, None]).astype(bf16)
    select_back = (slot_all[:, :, None] == places[None, None, :]).astype(bf16)
    partial = call(
        expert_kernel,
        chips,
        jax.ShapeDtypeStruct((devices, padded, width), bf16),
        [
            pltpu.VMEM((devices, tok_rows, width), bf16),
            pltpu.VMEM((4 * padded, width), bf16),
            pltpu.VMEM(w_gate.shape[1:], bf16),
            pltpu.VMEM(w_up.shape[1:], bf16),
            pltpu.VMEM(w_down.shape[:0:-1], bf16),
            pltpu.SemaphoreType.DMA((3,)),
        ]
        + gather_sems(2, chips),
        2,
        expert_in, select, w_gate[0], w_up[0], w_down[0].T,
        hbm=(2, 3, 4),
    )
    return call(
        combine_kernel,
        chips,
        jax.ShapeDtypeStruct((tok_rows, width), bf16),
        [pltpu.VMEM((chips, tok_rows, width), bf16)] * 2
        + [pltpu.VMEM((chips - 1, tok_rows, width), bf16)] * 2
        + ring_sems(2, chips),
        3,
        partial, select_back, weight_all[:, :, None], mixed,
    )


def solution(mesh):
    placed = (
        P(("groups", "ctx"), None),
        P("groups"),
        P(),
        P("ctx", None),
        P(),
        P(),
        P(),
        P("ctx", None),
        P(),
        P(("groups", "ctx"), None),
        P(("groups", "ctx"), None),
        P("ctx", None, None),
        P("ctx", None, None),
        P("ctx", None, None),
    )
    return jax.shard_map(
        per_device,
        mesh=mesh,
        in_specs=placed,
        out_specs=P(("groups", "ctx"), None),
        check_vma=False,
    )
```

```python
import functools

import jax
import jax.numpy as jnp
import numpy as np
from jax import lax
from jax.experimental import pallas as pl
from jax.experimental.pallas import tpu as pltpu
from jax.sharding import PartitionSpec as P

HD = 64
EPS = 1e-05
THETA = 150000.0
ALPHA = 1.702
SCALE = 0.125
NEGATIVE = -1e30
MESH = pl.DeviceIdType.MESH
VMEM = pl.BlockSpec(memory_space=pltpu.VMEM)
LIMIT = 63 * 1024 * 1024


def rms_scale(values, gain_vec):
    wide = values.astype(jnp.float32)
    inverse = lax.rsqrt(jnp.mean(wide * wide, axis=-1, keepdims=True) + EPS)
    return (wide * inverse * gain_vec).astype(jnp.bfloat16)


class Ring:
    def __init__(self, chips):
        self.chips = chips
        self.me = lax.axis_index("ctx")
        self.core = lax.rem(self.me, 2)
        chip = self.me // 2
        self.fold = chips == 8
        if self.fold:
            z, y = chip // 2, lax.rem(chip, 2)
            self.pos = z + y * (chips - 1 - 2 * z)
        else:
            self.pos = chip
        self.way = 1 - 2 * self.core
        self.partner = {"ctx": self.me + self.way}
        self.next = {"ctx": self.owner(-1)}
        self.prev = {"ctx": self.owner(1)}
        group = lax.axis_index("groups")
        self.parity = lax.rem(group, 2)
        self.peer = {"groups": group + 1 - 2 * self.parity}

    def index(self, pos, core):
        pos = lax.rem(pos + 2 * self.chips, self.chips)
        if self.fold:
            y = pos // (self.chips // 2)
            z = pos + y * (self.chips - 1 - 2 * pos)
            chip = z * 2 + y
        else:
            chip = pos
        return chip * 2 + core

    def owner(self, step):
        return self.index(self.pos - self.way * step, self.core)

    def partner_owner(self, step):
        return self.index(self.pos + self.way * step, 1 - self.core)

    def barrier(self, with_peer=False):
        sem = pltpu.get_barrier_semaphore()
        others = [self.next, self.prev, self.partner] + ([self.peer] if with_peer else [])
        for other in others:
            pl.semaphore_signal(sem, inc=1, device_id=other, device_id_type=MESH)
        pl.semaphore_wait(sem, len(others))


def gather_ring(ring, pieces, sems, setup, work):
    ring_send, ring_recv, part_send, part_recv, peer_send, peer_recv = sems
    chips = ring.chips
    ringed = [i for i, piece in enumerate(pieces) if piece[3] != "peer"]
    peered = [i for i, piece in enumerate(pieces) if piece[3] == "peer"]
    shared = [i for i, piece in enumerate(pieces) if piece[3] == "both"]
    lag = 2 if peered else 1

    def copy(i, step, target, send, recv, own=False):
        source, slots, view, _ = pieces[i]
        dst = view(slots.at[ring.owner(step)])
        return pltpu.make_async_remote_copy(
            src_ref=view(source) if own else dst,
            dst_ref=dst,
            send_sem=send,
            recv_sem=recv,
            device_id=target,
            device_id_type=MESH,
        )

    def onward(i, step, own=False):
        return copy(
            i, step, ring.next, ring_send.at[i, step], ring_recv.at[i, step + 1], own
        )

    def across(i, step, own=False):
        return copy(i, step, ring.partner, part_send.at[i, step], part_recv.at[i, step], own)

    def aside(i, step):
        return copy(i, step, ring.peer, peer_send.at[step], peer_recv.at[step])

    def arrived(i, sem, who):
        ref = pieces[i][2](pieces[i][1].at[who])
        pltpu.make_async_copy(ref, ref, sem).wait()

    ring.barrier(bool(peered))
    for i in ringed:
        onward(i, 0, True).start()
    for i in range(len(pieces)):
        across(i, 0, True).start()
    filled = []
    for source, slots, _, _ in pieces:
        if not any(slots is other for other in filled):
            slots[ring.me] = source[...]
            filled.append(slots)
    setup()

    def turn(t, carry):
        @pl.when(t < chips)
        def _():
            for i in ringed:
                arrived(i, ring_recv.at[i, t], ring.owner(t))

                @pl.when(t < chips - 1)
                def _():
                    onward(i, t).start()

                if i in shared:
                    aside(i, t).start()
                across(i, t).start()

        if peered:

            @pl.when((t > 1) & (t <= chips))
            def _():
                for i in peered:
                    arrived(i, peer_recv.at[t - 1], ring.owner(t - 1))
                    across(i, t - 1).start()

        @pl.when(t >= lag)
        def _():
            s = t - lag
            for i in range(len(pieces)):
                arrived(i, part_recv.at[i, s], ring.partner_owner(s))
            work(s)

        return carry

    lax.fori_loop(1, chips + lag, turn, 0)

    def drain(s, carry):
        for i in range(len(pieces)):
            across(i, s).wait_send()
        for i in ringed:

            @pl.when(s < chips - 1)
            def _():
                onward(i, s).wait_send()

        for i in shared:

            @pl.when(s > 0)
            def _():
                aside(i, s).wait_send()

        return carry

    lax.fori_loop(0, chips, drain, 0)


def ring_sems(count, chips):
    return [pltpu.SemaphoreType.DMA((count, chips))] * 4


def gather_sems(count, chips):
    return ring_sems(count, chips) + [pltpu.SemaphoreType.DMA((chips,))] * 2


def whole(ref):
    return ref


def cols(start, size):
    return lambda ref: ref.at[:, pl.ds(start, size)]


def rows(start, size):
    return lambda ref: ref.at[pl.ds(start, size), :]


def thirds(ring, source, slots):
    width = source.shape[1]
    third = width // 3 // 128 * 128
    mine = pl.multiple_of(ring.parity * third, 128)
    other = pl.multiple_of((1 - ring.parity) * third, 128)
    return [
        (source, slots, cols(mine, third), "both"),
        (source, slots, cols(2 * third, width - 2 * third), "ring"),
        (source, slots, cols(other, third), "peer"),
    ]


def query_kernel(chips, lhs, kv, meta, weight, out, kv_all, meta_all, slots, *sems):
    ring = Ring(chips)
    pieces = [(kv, kv_all, whole, "ring"), (meta, meta_all, whole, "ring")]
    pieces += thirds(ring, weight, slots)

    def setup():
        out[...] = jnp.zeros_like(out)

    def work(s):
        for who in (ring.owner(s), ring.partner_owner(s)):
            out[...] += jnp.dot(lhs[who], slots[who], preferred_element_type=jnp.float32)

    gather_ring(ring, pieces, sems, setup, work)


def attend_kernel(
    chips, raw, kv_all, cosine, sine, sinks, start, weight, tokens, gain,
    mixed_out, expert_in, out, slots, bias, query, key, value, attended, *sems
):
    ring = Ring(chips)
    blocks, tok_rows, width = attended.shape
    per_block = width // HD
    kv_heads, seq, _ = key.shape
    group = query.shape[0] // kv_heads
    pieces = thirds(ring, weight, slots)

    def setup():
        key_pos = lax.broadcasted_iota(jnp.int32, (tok_rows, seq), 1)
        row_pos = lax.broadcasted_iota(jnp.int32, (tok_rows, seq), 0) + ring.me * tok_rows
        allowed = (key_pos <= row_pos) & (key_pos >= start[...])
        bias[...] = jnp.where(allowed, 0.0, NEGATIVE)
        lane = lax.broadcasted_iota(jnp.int32, (tok_rows, 2 * HD), 1)
        first = lax.rem(lane, HD) < HD // 2

        def turn_pair(j, carry):
            pair = raw[:, pl.ds(pl.multiple_of(j * 2 * HD, 2 * HD), 2 * HD)]
            other = jnp.where(
                first, pltpu.roll(pair, 2 * HD - HD // 2, 1), pltpu.roll(pair, HD // 2, 1)
            )
            turned = ((pair * cosine[...] + other * sine[...]) * SCALE).astype(jnp.bfloat16)
            query[2 * j] = turned[:, :HD]
            query[2 * j + 1] = turned[:, HD:]
            return carry

        lax.fori_loop(0, query.shape[0] // 2, turn_pair, 0)

        def unpack(d, carry):
            at = pl.ds(pl.multiple_of(d * tok_rows, tok_rows), tok_rows)
            block = kv_all[d]
            for g in range(kv_heads):
                key[g, at, :] = block[:, g * HD : (g + 1) * HD]
                value[g, at, :] = block[:, (kv_heads + g) * HD : (kv_heads + g + 1) * HD]
            return carry

        lax.fori_loop(0, blocks, unpack, 0)

    def attend(who):
        heads = []
        for j in range(per_block):
            head = who * per_block + j
            kv_head = head // group
            scores = (
                lax.dot_general(
                    query[head],
                    key[kv_head],
                    (((1,), (1,)), ((), ())),
                    preferred_element_type=jnp.float32,
                )
                + bias[...]
            )
            sink = sinks[head]
            top = jnp.maximum(jnp.max(scores, axis=1, keepdims=True), sink)
            weights = jnp.exp(scores - top)
            total = jnp.sum(weights, axis=1, keepdims=True) + jnp.exp(sink - top)
            mixed = jnp.dot(
                weights.astype(jnp.bfloat16), value[kv_head], preferred_element_type=jnp.float32
            )
            heads.append(mixed / total)
        joined = heads[0] if per_block == 1 else jnp.concatenate(heads, axis=1)
        attended[who] = joined.astype(jnp.bfloat16)

    def work(s):
        attend(ring.owner(s))
        attend(ring.partner_owner(s))

    gather_ring(ring, pieces, sems, setup, work)
    out[...] = tokens[...].astype(jnp.float32)

    def project(d, carry):
        out[...] += jnp.dot(attended[d], slots[d], preferred_element_type=jnp.float32)
        return carry

    lax.fori_loop(0, blocks, project, 0)
    mixed_out[...] = out[...].astype(jnp.bfloat16)
    expert_in[...] = rms_scale(mixed_out[...], gain[...])


def chosen_rows(slot, padded, weight=None):
    place = lax.broadcasted_iota(jnp.int32, (padded, slot.shape[1]), 0).astype(jnp.float32)
    return jnp.where(place == slot, 1.0 if weight is None else weight, 0.0).astype(jnp.bfloat16)


def expert_kernel(
    chips, rows_in, slot_all, w_gate, w_up, w_down,
    out, slots, packed, hidden, gate, up, down, load_sem, *sems
):
    ring = Ring(chips)
    half = rows_in.shape[0] // 2
    padded = out.shape[1]
    pieces = [
        (rows_in, slots, rows(0, half), "ring"),
        (rows_in, slots, rows(half, half), "ring"),
    ]
    loads = [
        pltpu.make_async_copy(source, target, load_sem.at[i])
        for i, (source, target) in enumerate(((w_gate, gate), (w_up, up), (w_down, down)))
    ]
    for load in loads:
        load.start()

    def whose(s):
        return [
            ring.owner(s - 1), ring.partner_owner(s - 1), ring.owner(s), ring.partner_owner(s)
        ]

    def widen(s):
        for j, who in enumerate(whose(s)):
            packed[j * padded : (j + 1) * padded, :] = jnp.dot(
                chosen_rows(slot_all[who], padded), slots[who],
                preferred_element_type=jnp.float32,
            ).astype(jnp.bfloat16)
        gate_val = jnp.dot(packed[...], gate[...], preferred_element_type=jnp.float32)
        up_val = jnp.dot(packed[...], up[...], preferred_element_type=jnp.float32)
        turned = (up_val + 1.0) * gate_val * jax.nn.sigmoid(ALPHA * gate_val)
        hidden[...] = turned.astype(jnp.bfloat16)

    def narrow(s):
        partial = lax.dot_general(
            hidden[...], down[...], (((1,), (1,)), ((), ())), preferred_element_type=jnp.float32
        ).astype(jnp.bfloat16)
        for j, who in enumerate(whose(s)):
            out[who] = partial[j * padded : (j + 1) * padded, :]

    def work(s):
        @pl.when(s == 1)
        def _():
            for load in loads:
                load.wait()

        pl.when(lax.rem(s, 2) == 1)(lambda: widen(s))
        pl.when((lax.rem(s, 2) == 0) & (s > 0))(lambda: narrow(s - 1))

    gather_ring(ring, pieces, sems, lambda: None, work)
    narrow(chips - 1)


def combine_kernel(
    chips, partial, slot_all, weight_all, mixed, out, cross_out, cross_in, ring_out, ring_in,
    ring_send, ring_recv, part_send, part_recv,
):
    ring = Ring(chips)
    tok_rows = mixed.shape[0]
    half = tok_rows // 2
    ring.barrier()

    def share(who, h):
        at = slice(h * half, (h + 1) * half)
        chosen = chosen_rows(slot_all[who], partial.shape[1], weight_all[who])
        return lax.dot_general(
            chosen[:, at], partial[who], (((0,), (0,)), ((), ())),
            preferred_element_type=jnp.float32,
        )

    def crossing(s, h):
        at = pl.ds(h * half, half)
        return pltpu.make_async_remote_copy(
            src_ref=cross_out.at[s, at, :],
            dst_ref=cross_in.at[s, at, :],
            send_sem=part_send.at[h, s],
            recv_sem=part_recv.at[h, s],
            device_id=ring.partner,
            device_id_type=MESH,
        )

    def onward(s, h):
        at = pl.ds(h * half, half)
        return pltpu.make_async_remote_copy(
            src_ref=ring_out.at[s, at, :],
            dst_ref=ring_in.at[s, at, :],
            send_sem=ring_send.at[h, s],
            recv_sem=ring_recv.at[h, s],
            device_id=ring.next,
            device_id_type=MESH,
        )

    def give(s):
        who = ring.partner_owner(s + 1)
        for h in range(2):
            at = pl.ds(h * half, half)
            cross_out[s, at, :] = share(who, h).astype(jnp.bfloat16)
            crossing(s, h).start()

    def own(s, h):
        total = share(ring.owner(s + 1), h)
        crossing(s, h).wait_recv()
        return total + cross_in[s, pl.ds(h * half, half), :].astype(jnp.float32)

    give(0)
    for h in range(2):
        ring_out[0, pl.ds(h * half, half), :] = own(0, h).astype(jnp.bfloat16)
        onward(0, h).start()
    give(1)

    def step(s, carry):
        for h in range(2):
            at = pl.ds(h * half, half)
            total = own(s, h)
            onward(s - 1, h).wait_recv()
            total = total + ring_in[s - 1, at, :].astype(jnp.float32)
            ring_out[s, at, :] = total.astype(jnp.bfloat16)
            onward(s, h).start()
        give(s + 1)
        return carry

    lax.fori_loop(1, chips - 1, step, 0)
    last = chips - 1
    for h in range(2):
        at = pl.ds(h * half, half)
        total = own(last, h)
        onward(last - 1, h).wait_recv()
        total = total + ring_in[last - 1, at, :].astype(jnp.float32)
        out[at, :] = (mixed[at, :].astype(jnp.float32) + total).astype(jnp.bfloat16)

    def drain(s, carry):
        for h in range(2):
            crossing(s, h).wait_send()

            @pl.when(s < chips - 1)
            def _():
                onward(s, h).wait_send()

        return carry

    lax.fori_loop(0, chips, drain, 0)


LOG2E = 1.4426950408889634
ANY = pl.BlockSpec(memory_space=pl.ANY)
SMEM = pl.BlockSpec(memory_space=pltpu.SMEM)


class Copies:
    def __init__(self):
        self.made = []

    def send(self, make, pred=None):
        self.made.append((make, pred))
        if pred is None:
            make().start()
        else:
            pl.when(pred)(lambda: make().start())

    def drain(self):
        for make, pred in self.made:
            if pred is None:
                make().wait_send()
            else:
                pl.when(pred)(lambda make=make: make().wait_send())


def remote(src, dst, send_sem, recv_sem, where):
    return pltpu.make_async_remote_copy(
        src_ref=src, dst_ref=dst, send_sem=send_sem, recv_sem=recv_sem,
        device_id=where, device_id_type=MESH,
    )


def landed(ref, sem):
    pltpu.make_async_copy(ref, ref, sem).wait()


def spans(width, size):
    return [(at, min(size, width - at)) for at in range(0, width, size)]


def front_kernel(
    planes, tokens_t, lengths, attn_gain, w_query, w_key, w_value, sinks, w_out, moe_gain,
    angles, routes, weights_in, mixed_out, expert_in, meta_all,
    tokens, table, meta, normed, wq, wkv, kv_own, kv_all, lhs, raw, qx, kx, vx, bias, top, acc, attended, wo,
    part, held, k_out, k_in, y_out, y_in,
    load_sem, wq_recv, wq_plane, wq_send, norm_recv, norm_send, kv_recv, kv_send,
    meta_recv, meta_send, wo_recv, wo_plane, wo_send, k_recv, k_send, y_recv, y_send,
):
    f32, bf16 = jnp.float32, jnp.bfloat16
    x, c = lax.axis_index("groups"), lax.axis_index("ctx")
    z, y, k, d = c // 4, lax.rem(c // 2, 2), lax.rem(c, 2), lax.rem(c, 4)
    total = 4 * planes
    width, rows = tokens_t.shape
    wq_rows, qcols = wq.shape[1], wq.shape[2]
    heads = qx.shape[0]
    plane_rows = 4 * rows

    def head_of(place):
        return lax.rem(3 * place, 4)

    g = head_of(d)
    partner, across = {"ctx": c + 1 - 2 * k}, {"ctx": c + 2 - 4 * y}
    peer = {"groups": 1 - x}
    copies = Copies()

    loads = [
        pltpu.make_async_copy(w_key, wkv.at[0], load_sem.at[0]),
        pltpu.make_async_copy(w_value, wkv.at[1], load_sem.at[1]),
        pltpu.make_async_copy(
            angles.at[:, pl.ds(z * plane_rows, plane_rows), :], table, load_sem.at[2]
        ),
        pltpu.make_async_copy(w_query.at[:, pl.ds(g * qcols, qcols)], wq.at[c], wq_recv.at[c]),
    ]
    cosine, sine = table.at[0], table.at[1]
    for load in loads:
        load.start()

    barrier = pltpu.get_barrier_semaphore()
    for r in range(1, total):
        pl.semaphore_signal(
            barrier, inc=1, device_id={"ctx": lax.rem(c + r, total)}, device_id_type=MESH
        )
    pl.semaphore_signal(barrier, inc=1, device_id=peer, device_id_type=MESH)
    pl.semaphore_wait(barrier, total)

    for r in (2, 3, 1):
        other = jnp.bitwise_xor(d, r)
        copies.send(
            lambda r=r, other=other: remote(
                w_query.at[:, pl.ds(head_of(other) * qcols, qcols)], wq.at[c],
                wq_plane.at[r], wq_recv.at[c], {"ctx": 4 * z + other},
            )
        )
    tokens[...] = tokens_t[...].T
    normed[d] = rms_scale(tokens[...], attn_gain[...][None, :])
    copies.send(
        lambda: remote(normed.at[d], normed.at[d], norm_send.at[0], norm_recv.at[d], across)
    )
    copies.send(
        lambda: remote(normed.at[d], normed.at[d], norm_send.at[1], norm_recv.at[d], partner)
    )

    def wq_relay(who, right, left, side):
        landed(wq.at[who], wq_recv.at[who])
        for i, (where, pred) in enumerate(
            (({"ctx": c + 4}, right), ({"ctx": c - 4}, left), (peer, side))
        ):
            if pred is not None:
                copies_start(
                    lambda i=i, where=where: remote(
                        wq.at[who], wq.at[who], wq_send.at[i, who], wq_recv.at[who], where
                    ),
                    pred,
                )

    def copies_start(make, pred):
        pl.when(pred)(lambda: make().start())

    upper, lower = z < planes - 1, z > 0
    always = z >= 0
    wq_relay(4 * z + 2 * y + x, upper, lower, None)

    for load in loads[:3]:
        load.wait()
    own = normed[d]
    lane = lax.broadcasted_iota(jnp.int32, (rows, 2 * HD), 1)
    first = lax.rem(lane, HD) < HD // 2
    mine = pl.ds(pl.multiple_of(d * rows, rows), rows)
    turn_cos, turn_sin = cosine[mine, :], sine[mine, :]

    def turned(pair, cos, sin, low):
        other = jnp.where(
            low, pltpu.roll(pair, 2 * HD - HD // 2, 1), pltpu.roll(pair, HD // 2, 1)
        )
        return pair * cos + other * sin

    raw_key = jnp.dot(own, wkv[0], preferred_element_type=f32)
    raw_value = jnp.dot(own, wkv[1], preferred_element_type=f32)
    for j in range(2):
        at = slice(j * 2 * HD, (j + 1) * 2 * HD)
        keys = turned(raw_key[:, at], turn_cos, turn_sin, first)
        values = raw_value[:, at]
        kv_own[2 * j] = jnp.where(lane < HD, keys, pltpu.roll(values, HD, 1)).astype(bf16)
        kv_own[2 * j + 1] = jnp.where(lane < HD, pltpu.roll(keys, HD, 1), values).astype(bf16)
    kv_all[c] = kv_own[g]

    def kv_copy(dz, other):
        return lambda: remote(
            kv_own.at[head_of(other)], kv_all.at[c], kv_send.at[dz, other], kv_recv.at[c],
            {"ctx": 4 * (z + dz) + other},
        )

    wq_relay(4 * z + 2 * (1 - y) + x, upper, lower, None)
    for dz in range(planes):
        for other in range(4):
            pred = (z + dz < planes) if dz else (d != other)
            copies.send(kv_copy(dz, other), pred)
    experts = meta.shape[0] // 2
    expert = lax.broadcasted_iota(jnp.int32, (experts, rows), 0)
    named, chosen = jnp.zeros((experts, rows), f32), jnp.zeros((experts, rows), f32)
    for t in range(routes.shape[0]):
        same = routes[t : t + 1, :] == expert
        named += jnp.where(same, 1.0, 0.0)
        chosen += jnp.where(same, weights_in[t : t + 1, :], 0.0)
    tri = (rows, rows)
    upto = lax.broadcasted_iota(jnp.int32, tri, 0) <= lax.broadcasted_iota(jnp.int32, tri, 1)
    place = jnp.dot(
        named.astype(bf16), jnp.where(upto, 1.0, 0.0).astype(bf16), preferred_element_type=f32
    )
    meta[:experts, :] = jnp.where(named > 0.5, place - 1.0, -1.0)
    meta[experts:, :] = chosen
    meta_all[c] = meta[...]
    for r in range(1, total):
        copies.send(
            lambda r=r: remote(
                meta, meta_all.at[c], meta_send.at[r], meta_recv.at[c],
                {"ctx": lax.rem(c + r, total)},
            )
        )

    def wo_rows(i):
        return pl.ds(pl.multiple_of(i * rows, rows), rows)

    wo_spans = spans(width, 1024)

    def wo_hand(n):
        at, size = wo_spans[n]
        return remote(
            w_out.at[pl.ds(at, size), :], wo.at[pl.ds(at, size), wo_rows(d)],
            wo_plane.at[n], wo_recv.at[d, n], {"ctx": 4 * z + head_of(z)},
        )

    def wo_keep(n):
        at, size = wo_spans[n]
        return pltpu.make_async_copy(
            w_out.at[pl.ds(at, size), :], wo.at[pl.ds(at, size), wo_rows(d)], wo_recv.at[d, n]
        )

    for s in range(1, planes):
        for j in range(2):

            @pl.when(z >= s)
            def _(s=s, j=j):
                wq_relay(4 * (z - s) + 2 * j + x, upper, None, always)

            @pl.when(z + s < planes)
            def _(s=s, j=j):
                wq_relay(4 * (z + s) + 2 * j + x, None, lower, always)

        if s == 1:
            for n in range(len(wo_spans)):
                pl.when(g == z)(lambda n=n: wo_keep(n).start())
                copies.send(lambda n=n: wo_hand(n), g != z)
            opposite = jnp.bitwise_xor(d, 2)
            landed(normed.at[opposite], norm_recv.at[opposite])
            copies.send(
                lambda: remote(
                    normed.at[opposite], normed.at[opposite],
                    norm_send.at[2], norm_recv.at[opposite], partner,
                )
            )

    def wo_relay(n, j):
        at, size = wo_spans[n]
        i = 2 * j + x
        piece = wo.at[pl.ds(at, size), wo_rows(i)]
        landed(piece, wo_recv.at[i, n])
        for way, (where, pred) in enumerate(wo_ways()):
            copies_start(
                lambda way=way, where=where: remote(
                    piece, piece, wo_send.at[way, i, n], wo_recv.at[i, n], where
                ),
                pred,
            )

    def wo_ways():
        return (
            ({"ctx": c + 4}, upper & (z >= g)),
            ({"ctx": c - 4}, lower & (z <= g)),
            (peer, z != g),
        )

    def wo_stage(stage):
        for n in range(len(wo_spans)):
            for j in range(2):
                jj = jnp.bitwise_xor(j, y)
                if stage == 0:
                    pl.when(z == g)(lambda n=n, jj=jj: wo_relay(n, jj))
                for away in range(1, planes):
                    if stage == n + away:
                        pl.when(jnp.abs(z - g) == away)(lambda n=n, jj=jj: wo_relay(n, jj))

    for r in (1, 3):
        other = jnp.bitwise_xor(d, r)
        landed(normed.at[other], norm_recv.at[other])
    for t in range(4):
        block = normed[t]
        for j in range(total):
            lhs[j, t * rows : (t + 1) * rows, :] = block[:, j * wq_rows : (j + 1) * wq_rows]

    wo_stage(0)
    raw[...] = jnp.zeros_like(raw)

    def query_rows(plane):
        for i in range(4):
            who = 4 * plane + i
            raw[...] += jnp.dot(lhs[who], wq[who], preferred_element_type=f32)

    query_rows_wait = lambda plane, i: landed(wq.at[4 * plane + i], wq_recv.at[4 * plane + i])
    for i in range(2):
        query_rows_wait(z, 2 * i + 1 - x)
    query_rows(z)
    for s in range(1, planes):
        for step in (-s, s):

            @pl.when((z + step >= 0) & (z + step < planes))
            def _(step=step):
                for i in range(2):
                    query_rows_wait(z + step, 2 * i + 1 - x)
                query_rows(z + step)

    ends = [lengths[0]]
    for i in range(1, lengths.shape[0]):
        ends.append(ends[-1] + lengths[i])

    def segment(start, shape):
        place = start + lax.broadcasted_iota(jnp.int32, shape, 0)
        found = jnp.zeros(shape, jnp.int32)
        for end in ends:
            found += (place >= end).astype(jnp.int32)
        return found

    wide = (plane_rows, 2 * HD)
    wide_lane = lax.broadcasted_iota(jnp.int32, wide, 1)
    mark = jnp.where(
        (wide_lane - HD == segment(z * plane_rows, wide)) & (wide_lane >= HD), 1.0, 0.0
    )
    wide_first = lax.rem(wide_lane, HD) < HD // 2

    for j in range(heads // 2):
        pair = turned(
            raw[:, j * 2 * HD : (j + 1) * 2 * HD], cosine[...], sine[...], wide_first
        ) * (SCALE * LOG2E)
        qx[2 * j] = jnp.where(wide_lane < HD, pair, mark).astype(bf16)
        qx[2 * j + 1] = jnp.where(wide_lane < HD, pltpu.roll(pair, HD, 1), mark).astype(bf16)

    def unpack(i, carry):
        @pl.when(i != c)
        def _():
            landed(kv_all.at[i], kv_recv.at[i])

        both = kv_all[i].astype(f32)
        apart = jnp.where(
            (lane - HD == segment(i * rows, lane.shape)) | (lane >= HD + len(ends)), 0.0, NEGATIVE
        )
        at = pl.ds(pl.multiple_of(i * rows, rows), rows)
        kx[:, at] = jnp.where(lane < HD, both, apart).T.astype(bf16)
        ones = jnp.where(lane == HD, 1.0, 0.0)
        vx[at, :] = jnp.where(lane < HD, pltpu.roll(both, HD, 1), ones).astype(bf16)
        return carry

    lax.fori_loop(0, 4 * (z + 1), unpack, 0)
    square = (plane_rows, plane_rows)
    bias[...] = jnp.where(
        lax.broadcasted_iota(jnp.int32, square, 1) <= lax.broadcasted_iota(jnp.int32, square, 0),
        0.0, NEGATIVE,
    )

    wo_stage(1)

    def attend(h):
        for e in range(2):
            top[e] = jnp.full(top.shape[1:], sinks[g * heads + h + e] * LOG2E, f32)
            acc[e] = jnp.where(wide_lane == HD, 1.0, 0.0)

        def block(b, last):
            at = pl.ds(pl.multiple_of(b * plane_rows, plane_rows), plane_rows)
            scores = [
                jnp.dot(qx[h + e], kx[:, at], preferred_element_type=f32) for e in range(2)
            ]
            for e in range(2):
                score = scores[e] + bias[...] if last else scores[e]
                old = top[e]
                new = jnp.maximum(old, jnp.max(score, axis=1, keepdims=True))
                weights = jnp.exp2(score - new).astype(bf16)
                acc[e] = acc[e] * jnp.exp2(old - new) + jnp.dot(
                    weights, vx[at, :], preferred_element_type=f32
                )
                top[e] = new

        def body(b, carry):
            block(b, False)
            return carry

        lax.fori_loop(0, z, body, 0)
        block(z, True)
        return [acc[e] / acc[e, :, HD : HD + 1] for e in range(2)]

    def pair_of_heads(j, carry):
        for stage in range(1, heads // 2):
            pl.when(j == stage)(lambda stage=stage: wo_stage(stage + 1))
        even, odd = attend(2 * j)
        attended[j] = jnp.where(wide_lane < HD, even, pltpu.roll(odd, HD, 1)).astype(bf16)
        return carry

    lax.fori_loop(0, heads // 2, pair_of_heads, 0)
    wo_stage(5)

    lhs_out = jnp.concatenate([attended[j] for j in range(heads // 2)], axis=1)
    give, keep = 1 - k, k

    def k_copy(n):
        at, size = wo_spans[n]
        return remote(
            k_out.at[:, :, pl.ds(at, size)], k_in.at[:, :, pl.ds(at, size)],
            k_send.at[n], k_recv.at[n], partner,
        )

    def y_copy(n):
        at, size = wo_spans[n]
        return remote(
            y_out.at[:, pl.ds(at, size)], y_in.at[:, pl.ds(at, size)],
            y_send.at[n], y_recv.at[n], across,
        )

    def project(n):
        at, size = wo_spans[n]
        cols = pl.ds(at, size)
        for j in range(2):
            i = 2 * j + 1 - x
            landed(wo.at[cols, wo_rows(i)], wo_recv.at[i, n])
        part[:, :size] = lax.dot_general(
            lhs_out, wo[cols, :], (((1,), (1,)), ((), ())), preferred_element_type=f32
        )
        for j in range(2):
            k_out[j, :, cols] = part[wo_rows(2 * j + give), :size].astype(bf16)
            held[j, :, cols] = part[wo_rows(2 * j + keep), :size]
        copies.send(lambda: k_copy(n))

    def fold(n):
        at, size = wo_spans[n]
        cols = pl.ds(at, size)
        k_copy(n).wait_recv()
        y_out[:, cols] = (held[1 - y, :, cols] + k_in[1 - y, :, cols].astype(f32)).astype(bf16)
        copies.send(lambda: y_copy(n))

    def finish(n):
        at, size = wo_spans[n]
        cols = pl.ds(at, size)
        mine = held[y, :, cols] + k_in[y, :, cols].astype(f32) + tokens[:, cols].astype(f32)
        y_copy(n).wait_recv()
        mixed_out[:, cols] = (mine + y_in[:, cols].astype(f32)).astype(bf16)

    count = len(wo_spans)
    for n in range(count):
        project(n)
        fold(n)
    for n in range(count):
        finish(n)
    expert_in[...] = rms_scale(mixed_out[...], moe_gain[...][None, :])

    def meta_arrived(i, carry):
        @pl.when(i != c)
        def _():
            landed(meta_all.at[i], meta_recv.at[i])

        return carry

    lax.fori_loop(0, total, meta_arrived, 0)
    copies.drain()

    def wq_drain(who, ways):
        for i, pred in enumerate(ways):
            pl.when(pred)(
                lambda i=i: remote(
                    wq.at[who], wq.at[who], wq_send.at[i, who], wq_recv.at[who], partner
                ).wait_send()
            )

    never = z < 0
    for j in range(2):
        wq_drain(4 * z + 2 * j + x, (upper, lower))
    for s in range(1, planes):
        for j in range(2):
            pl.when(z >= s)(
                lambda s=s, j=j: wq_drain(4 * (z - s) + 2 * j + x, (upper, never, always))
            )
            pl.when(z + s < planes)(
                lambda s=s, j=j: wq_drain(4 * (z + s) + 2 * j + x, (never, lower, always))
            )
    for n, (at, size) in enumerate(wo_spans):
        for j in range(2):
            i = 2 * j + x
            piece = wo.at[pl.ds(at, size), wo_rows(i)]
            for way, (where, pred) in enumerate(wo_ways()):
                pl.when(pred)(
                    lambda way=way, where=where: remote(
                        piece, piece, wo_send.at[way, i, n], wo_recv.at[i, n], where
                    ).wait_send()
                )


def front(tokens, lengths, attn_gain, w_query, w_key, w_value, sinks, w_out, moe_gain, routes, weights):
    bf16, f32 = jnp.bfloat16, jnp.float32
    rows, width = tokens.shape
    devices = lax.axis_size("ctx")
    planes = devices // 4
    seq = devices * rows
    quarter = w_query.shape[1] // 4
    heads = quarter // HD
    count = len(spans(width, 1024))
    place = np.arange(seq, dtype=np.float32)
    freqs = np.float32(THETA) ** (-np.arange(HD // 2, dtype=np.float32) / np.float32(HD // 2))
    angles = place[:, None] * freqs[None, :].astype(np.float32)
    cos, sin = np.cos(angles).astype(np.float32), np.sin(angles).astype(np.float32)
    tables = np.stack(
        [np.tile(cos, (1, 4)), np.tile(np.concatenate([-sin, sin], axis=1), (1, 2))]
    )
    meta_shape = (devices, rows)
    dma = pltpu.SemaphoreType.DMA
    vmem = pltpu.VMEM
    return pl.pallas_call(
        functools.partial(front_kernel, planes),
        out_shape=[
            jax.ShapeDtypeStruct((rows, width), bf16),
            jax.ShapeDtypeStruct((rows, width), bf16),
            jax.ShapeDtypeStruct((devices,) + meta_shape, f32),
        ],
        in_specs=[VMEM, SMEM, VMEM, ANY, ANY, ANY, SMEM, ANY, VMEM, ANY, VMEM, VMEM],
        out_specs=[VMEM] * 3,
        scratch_shapes=[
            vmem((rows, width), bf16),
            vmem((2, 4 * rows, 2 * HD), f32),
            vmem(meta_shape, f32),
            vmem((4, rows, width), bf16),
            vmem((devices, w_query.shape[0], quarter), bf16),
            vmem((2,) + w_key.shape, bf16),
            vmem((4, rows, 2 * HD), bf16),
            vmem((devices, rows, 2 * HD), bf16),
            vmem((devices, 4 * rows, w_query.shape[0]), bf16),
            vmem((4 * rows, quarter), f32),
            vmem((heads, 4 * rows, 2 * HD), bf16),
            vmem((2 * HD, seq), bf16),
            vmem((seq, 2 * HD), bf16),
            vmem((4 * rows, 4 * rows), f32),
            vmem((2, 4 * rows, 1), f32),
            vmem((2, 4 * rows, 2 * HD), f32),
            vmem((heads // 2, 4 * rows, 2 * HD), bf16),
            vmem((width, 4 * rows), bf16),
            vmem((4 * rows, 1024), f32),
            vmem((2, rows, width), f32),
            vmem((2, rows, width), bf16),
            vmem((2, rows, width), bf16),
            vmem((rows, width), bf16),
            vmem((rows, width), bf16),
            dma((3,)),
            dma((devices,)), dma((4,)), dma((3, devices)),
            dma((4,)), dma((3,)),
            dma((devices,)), dma((planes, 4)),
            dma((devices,)), dma((devices,)),
            dma((4, count)), dma((count,)), dma((3, 4, count)),
            dma((count,)), dma((count,)), dma((count,)), dma((count,)),
        ],
        compiler_params=pltpu.CompilerParams(
            collective_id=4, has_side_effects=True, vmem_limit_bytes=LIMIT
        ),
    )(
        tokens.T, lengths, attn_gain, w_query, w_key, w_value, sinks, w_out.T,
        moe_gain, jnp.asarray(tables), routes.T, weights.T,
    )


def call(kernel, chips, out_shape, scratch, identity, *args, smem=(), hbm=()):
    single = not isinstance(out_shape, (list, tuple))
    return pl.pallas_call(
        functools.partial(kernel, chips),
        out_shape=out_shape,
        in_specs=[
            pl.BlockSpec(memory_space=pltpu.SMEM)
            if i in smem
            else pl.BlockSpec(memory_space=pl.ANY)
            if i in hbm
            else VMEM
            for i in range(len(args))
        ],
        out_specs=VMEM if single else [VMEM] * len(out_shape),
        scratch_shapes=scratch,
        compiler_params=pltpu.CompilerParams(
            collective_id=identity, has_side_effects=True, vmem_limit_bytes=LIMIT
        ),
    )(*args)


def ring_front(
    tokens, lengths, attn_gain, w_query, w_key, w_value, sinks, w_out, moe_gain, routes,
    route_weights,
):
    bf16, f32 = jnp.bfloat16, jnp.float32
    tok_rows, width = tokens.shape
    devices = lax.axis_size("ctx")
    chips = devices // 2
    me = lax.axis_index("ctx")
    q_cols = w_query.shape[1]
    num_heads = q_cols // HD
    kv_cols = w_key.shape[1]
    kv_heads = kv_cols // HD
    experts = chips
    member = routes[:, :, None] == jnp.arange(experts, dtype=jnp.int32)[None, None, :]
    named = jnp.any(member, axis=1)
    lower = jnp.tril(jnp.ones((tok_rows, tok_rows), bf16))
    slot = jnp.dot(lower, named.astype(bf16), preferred_element_type=f32) - 1.0
    slot = jnp.where(named, slot, -1.0)
    routed_weight = jnp.sum(jnp.where(member, route_weights[:, :, None], 0.0), axis=1)
    meta = jnp.concatenate([slot, routed_weight], axis=1).T

    positions = me * tok_rows + jnp.arange(tok_rows, dtype=jnp.int32)
    freqs = THETA ** (-jnp.arange(HD // 2, dtype=f32) / (HD // 2))
    angles = positions.astype(f32)[:, None] * freqs[None, :]
    cosine, sine = jnp.cos(angles)[:, None, :], jnp.sin(angles)[:, None, :]

    def rotate(values):
        first, second = values[..., : HD // 2], values[..., HD // 2 :]
        return jnp.concatenate(
            [first * cosine - second * sine, second * cosine + first * sine], axis=-1
        ).astype(bf16)

    normed = rms_scale(tokens, attn_gain)
    raw_key = jnp.dot(normed, w_key, preferred_element_type=f32)
    value = jnp.dot(normed, w_value, preferred_element_type=f32).astype(bf16)
    key = rotate(raw_key.reshape(tok_rows, kv_heads, HD)).reshape(tok_rows, kv_cols)
    kv = jnp.concatenate([key, value], axis=1)
    lhs = normed.reshape(tok_rows, devices, width // devices).transpose(1, 0, 2)
    raw_query, kv_all, meta_all = call(
        query_kernel,
        chips,
        [
            jax.ShapeDtypeStruct((tok_rows, q_cols), f32),
            jax.ShapeDtypeStruct((devices,) + kv.shape, bf16),
            jax.ShapeDtypeStruct((devices,) + meta.shape, f32),
        ],
        [pltpu.VMEM((devices,) + w_query.shape, bf16)] + gather_sems(5, chips),
        0,
        lhs, kv, meta, w_query,
    )
    cosine_pair = jnp.tile(cosine[:, 0, :], (1, 4))
    sine_pair = jnp.tile(jnp.concatenate([-sine[:, 0, :], sine[:, 0, :]], axis=1), (1, 2))
    doc_ends = jnp.dot(jnp.tril(jnp.ones((lengths.size,) * 2, jnp.int32)), lengths)
    start = jnp.max(
        jnp.where(positions[:, None] >= doc_ends[None, :], doc_ends[None, :], 0), axis=1
    )[:, None]
    mixed, expert_in = call(
        attend_kernel,
        chips,
        [jax.ShapeDtypeStruct((tok_rows, width), bf16)] * 2,
        [
            pltpu.VMEM((tok_rows, width), f32),
            pltpu.VMEM((devices,) + w_out.shape, bf16),
            pltpu.VMEM((tok_rows, devices * tok_rows), f32),
            pltpu.VMEM((num_heads, tok_rows, HD), bf16),
            pltpu.VMEM((kv_heads, devices * tok_rows, HD), bf16),
            pltpu.VMEM((kv_heads, devices * tok_rows, HD), bf16),
            pltpu.VMEM((devices, tok_rows, w_out.shape[0]), bf16),
        ]
        + gather_sems(3, chips),
        1,
        raw_query, kv_all, cosine_pair, sine_pair, sinks, start, w_out, tokens, moe_gain[None, :],
        smem=(4,),
    )
    return mixed, expert_in, meta_all


def per_device(
    tokens, lengths, attn_gain, w_query, w_key, w_value, sinks, w_out, moe_gain, routes,
    route_weights, w_gate, w_up, w_down,
):
    bf16, f32 = jnp.bfloat16, jnp.float32
    tok_rows, width = tokens.shape
    devices = lax.axis_size("ctx")
    chips = devices // 2
    me = lax.axis_index("ctx")
    experts = chips
    capacity = tok_rows * 4 * 17 // (16 * experts)
    padded = -(-capacity // 16) * 16

    square = lax.axis_size("groups") == 2 and devices == 16
    mixed, expert_in, meta_all = (front if square else ring_front)(
        tokens, lengths, attn_gain, w_query, w_key, w_value, sinks, w_out, moe_gain, routes,
        route_weights,
    )
    expert = me // 2
    slot_all = lax.dynamic_slice_in_dim(meta_all, expert, 1, 1)
    weight_all = lax.dynamic_slice_in_dim(meta_all, experts + expert, 1, 1)
    partial = call(
        expert_kernel,
        chips,
        jax.ShapeDtypeStruct((devices, padded, width), bf16),
        [
            pltpu.VMEM((devices, tok_rows, width), bf16),
            pltpu.VMEM((4 * padded, width), bf16),
            pltpu.VMEM((4 * padded, w_gate.shape[2]), bf16),
            pltpu.VMEM(w_gate.shape[1:], bf16),
            pltpu.VMEM(w_up.shape[1:], bf16),
            pltpu.VMEM(w_down.shape[:0:-1], bf16),
            pltpu.SemaphoreType.DMA((3,)),
        ]
        + gather_sems(2, chips),
        2,
        expert_in, slot_all, w_gate[0], w_up[0], w_down[0].T,
        hbm=(2, 3, 4),
    )
    return call(
        combine_kernel,
        chips,
        jax.ShapeDtypeStruct((tok_rows, width), bf16),
        [pltpu.VMEM((chips, tok_rows, width), bf16)] * 2
        + [pltpu.VMEM((chips - 1, tok_rows, width), bf16)] * 2
        + ring_sems(2, chips),
        3,
        partial, slot_all, weight_all, mixed,
    )


def solution(mesh):
    placed = (
        P(("groups", "ctx"), None),
        P("groups"),
        P(),
        P("ctx", None),
        P(),
        P(),
        P(),
        P("ctx", None),
        P(),
        P(("groups", "ctx"), None),
        P(("groups", "ctx"), None),
        P("ctx", None, None),
        P("ctx", None, None),
        P("ctx", None, None),
    )
    return jax.shard_map(
        per_device,
        mesh=mesh,
        in_specs=placed,
        out_specs=P(("groups", "ctx"), None),
        check_vma=False,
    )
```

```python
import functools

import jax
import jax.numpy as jnp
import numpy as np
from jax import lax
from jax.experimental import pallas as pl
from jax.experimental.pallas import tpu as pltpu
from jax.sharding import PartitionSpec as P

HD = 64
EPS = 1e-05
THETA = 150000.0
ALPHA = 1.702
SCALE = 0.125
NEGATIVE = -1e30
MESH = pl.DeviceIdType.MESH
VMEM = pl.BlockSpec(memory_space=pltpu.VMEM)
LIMIT = 63 * 1024 * 1024


def rms_scale(values, gain_vec):
    wide = values.astype(jnp.float32)
    inverse = lax.rsqrt(jnp.mean(wide * wide, axis=-1, keepdims=True) + EPS)
    return (wide * inverse * gain_vec).astype(jnp.bfloat16)


class Ring:
    def __init__(self, chips):
        self.chips = chips
        self.me = lax.axis_index("ctx")
        self.core = lax.rem(self.me, 2)
        chip = self.me // 2
        self.fold = chips == 8
        if self.fold:
            z, y = chip // 2, lax.rem(chip, 2)
            self.pos = z + y * (chips - 1 - 2 * z)
        else:
            self.pos = chip
        self.way = 1 - 2 * self.core
        self.partner = {"ctx": self.me + self.way}
        self.next = {"ctx": self.owner(-1)}
        self.prev = {"ctx": self.owner(1)}
        group = lax.axis_index("groups")
        self.parity = lax.rem(group, 2)
        self.peer = {"groups": group + 1 - 2 * self.parity}

    def index(self, pos, core):
        pos = lax.rem(pos + 2 * self.chips, self.chips)
        if self.fold:
            y = pos // (self.chips // 2)
            z = pos + y * (self.chips - 1 - 2 * pos)
            chip = z * 2 + y
        else:
            chip = pos
        return chip * 2 + core

    def owner(self, step):
        return self.index(self.pos - self.way * step, self.core)

    def partner_owner(self, step):
        return self.index(self.pos + self.way * step, 1 - self.core)

    def barrier(self, with_peer=False):
        sem = pltpu.get_barrier_semaphore()
        others = [self.next, self.prev, self.partner] + ([self.peer] if with_peer else [])
        for other in others:
            pl.semaphore_signal(sem, inc=1, device_id=other, device_id_type=MESH)
        pl.semaphore_wait(sem, len(others))


def gather_ring(ring, pieces, sems, setup, work):
    ring_send, ring_recv, part_send, part_recv, peer_send, peer_recv = sems
    chips = ring.chips
    ringed = [i for i, piece in enumerate(pieces) if piece[3] != "peer"]
    peered = [i for i, piece in enumerate(pieces) if piece[3] == "peer"]
    shared = [i for i, piece in enumerate(pieces) if piece[3] == "both"]
    lag = 2 if peered else 1

    def copy(i, step, target, send, recv, own=False):
        source, slots, view, _ = pieces[i]
        dst = view(slots.at[ring.owner(step)])
        return pltpu.make_async_remote_copy(
            src_ref=view(source) if own else dst,
            dst_ref=dst,
            send_sem=send,
            recv_sem=recv,
            device_id=target,
            device_id_type=MESH,
        )

    def onward(i, step, own=False):
        return copy(
            i, step, ring.next, ring_send.at[i, step], ring_recv.at[i, step + 1], own
        )

    def across(i, step, own=False):
        return copy(i, step, ring.partner, part_send.at[i, step], part_recv.at[i, step], own)

    def aside(i, step):
        return copy(i, step, ring.peer, peer_send.at[step], peer_recv.at[step])

    def arrived(i, sem, who):
        ref = pieces[i][2](pieces[i][1].at[who])
        pltpu.make_async_copy(ref, ref, sem).wait()

    ring.barrier(bool(peered))
    for i in ringed:
        onward(i, 0, True).start()
    for i in range(len(pieces)):
        across(i, 0, True).start()
    filled = []
    for source, slots, _, _ in pieces:
        if not any(slots is other for other in filled):
            slots[ring.me] = source[...]
            filled.append(slots)
    setup()

    def turn(t, carry):
        @pl.when(t < chips)
        def _():
            for i in ringed:
                arrived(i, ring_recv.at[i, t], ring.owner(t))

                @pl.when(t < chips - 1)
                def _():
                    onward(i, t).start()

                if i in shared:
                    aside(i, t).start()
                across(i, t).start()

        if peered:

            @pl.when((t > 1) & (t <= chips))
            def _():
                for i in peered:
                    arrived(i, peer_recv.at[t - 1], ring.owner(t - 1))
                    across(i, t - 1).start()

        @pl.when(t >= lag)
        def _():
            s = t - lag
            for i in range(len(pieces)):
                arrived(i, part_recv.at[i, s], ring.partner_owner(s))
            work(s)

        return carry

    lax.fori_loop(1, chips + lag, turn, 0)

    def drain(s, carry):
        for i in range(len(pieces)):
            across(i, s).wait_send()
        for i in ringed:

            @pl.when(s < chips - 1)
            def _():
                onward(i, s).wait_send()

        for i in shared:

            @pl.when(s > 0)
            def _():
                aside(i, s).wait_send()

        return carry

    lax.fori_loop(0, chips, drain, 0)


def ring_sems(count, chips):
    return [pltpu.SemaphoreType.DMA((count, chips))] * 4


def gather_sems(count, chips):
    return ring_sems(count, chips) + [pltpu.SemaphoreType.DMA((chips,))] * 2


def whole(ref):
    return ref


def cols(start, size):
    return lambda ref: ref.at[:, pl.ds(start, size)]


def rows(start, size):
    return lambda ref: ref.at[pl.ds(start, size), :]


def thirds(ring, source, slots):
    width = source.shape[1]
    third = width // 3 // 128 * 128
    mine = pl.multiple_of(ring.parity * third, 128)
    other = pl.multiple_of((1 - ring.parity) * third, 128)
    return [
        (source, slots, cols(mine, third), "both"),
        (source, slots, cols(2 * third, width - 2 * third), "ring"),
        (source, slots, cols(other, third), "peer"),
    ]


def query_kernel(chips, lhs, kv, meta, weight, out, kv_all, meta_all, slots, *sems):
    ring = Ring(chips)
    pieces = [(kv, kv_all, whole, "ring"), (meta, meta_all, whole, "ring")]
    pieces += thirds(ring, weight, slots)

    def setup():
        out[...] = jnp.zeros_like(out)

    def work(s):
        for who in (ring.owner(s), ring.partner_owner(s)):
            out[...] += jnp.dot(lhs[who], slots[who], preferred_element_type=jnp.float32)

    gather_ring(ring, pieces, sems, setup, work)


def attend_kernel(
    chips, raw, kv_all, cosine, sine, sinks, start, weight, tokens, gain,
    mixed_out, expert_in, out, slots, bias, query, key, value, attended, *sems
):
    ring = Ring(chips)
    blocks, tok_rows, width = attended.shape
    per_block = width // HD
    kv_heads, seq, _ = key.shape
    group = query.shape[0] // kv_heads
    pieces = thirds(ring, weight, slots)

    def setup():
        key_pos = lax.broadcasted_iota(jnp.int32, (tok_rows, seq), 1)
        row_pos = lax.broadcasted_iota(jnp.int32, (tok_rows, seq), 0) + ring.me * tok_rows
        allowed = (key_pos <= row_pos) & (key_pos >= start[...])
        bias[...] = jnp.where(allowed, 0.0, NEGATIVE)
        lane = lax.broadcasted_iota(jnp.int32, (tok_rows, 2 * HD), 1)
        first = lax.rem(lane, HD) < HD // 2

        def turn_pair(j, carry):
            pair = raw[:, pl.ds(pl.multiple_of(j * 2 * HD, 2 * HD), 2 * HD)]
            other = jnp.where(
                first, pltpu.roll(pair, 2 * HD - HD // 2, 1), pltpu.roll(pair, HD // 2, 1)
            )
            turned = ((pair * cosine[...] + other * sine[...]) * SCALE).astype(jnp.bfloat16)
            query[2 * j] = turned[:, :HD]
            query[2 * j + 1] = turned[:, HD:]
            return carry

        lax.fori_loop(0, query.shape[0] // 2, turn_pair, 0)

        def unpack(d, carry):
            at = pl.ds(pl.multiple_of(d * tok_rows, tok_rows), tok_rows)
            block = kv_all[d]
            for g in range(kv_heads):
                key[g, at, :] = block[:, g * HD : (g + 1) * HD]
                value[g, at, :] = block[:, (kv_heads + g) * HD : (kv_heads + g + 1) * HD]
            return carry

        lax.fori_loop(0, blocks, unpack, 0)

    def attend(who):
        heads = []
        for j in range(per_block):
            head = who * per_block + j
            kv_head = head // group
            scores = (
                lax.dot_general(
                    query[head],
                    key[kv_head],
                    (((1,), (1,)), ((), ())),
                    preferred_element_type=jnp.float32,
                )
                + bias[...]
            )
            sink = sinks[head]
            top = jnp.maximum(jnp.max(scores, axis=1, keepdims=True), sink)
            weights = jnp.exp(scores - top)
            total = jnp.sum(weights, axis=1, keepdims=True) + jnp.exp(sink - top)
            mixed = jnp.dot(
                weights.astype(jnp.bfloat16), value[kv_head], preferred_element_type=jnp.float32
            )
            heads.append(mixed / total)
        joined = heads[0] if per_block == 1 else jnp.concatenate(heads, axis=1)
        attended[who] = joined.astype(jnp.bfloat16)

    def work(s):
        attend(ring.owner(s))
        attend(ring.partner_owner(s))

    gather_ring(ring, pieces, sems, setup, work)
    out[...] = tokens[...].astype(jnp.float32)

    def project(d, carry):
        out[...] += jnp.dot(attended[d], slots[d], preferred_element_type=jnp.float32)
        return carry

    lax.fori_loop(0, blocks, project, 0)
    mixed_out[...] = out[...].astype(jnp.bfloat16)
    expert_in[...] = rms_scale(mixed_out[...], gain[...])


def chosen_rows(slot, padded, weight=None):
    place = lax.broadcasted_iota(jnp.int32, (padded, slot.shape[1]), 0).astype(jnp.float32)
    return jnp.where(place == slot, 1.0 if weight is None else weight, 0.0).astype(jnp.bfloat16)


def expert_kernel(
    chips, rows_in, slot_all, w_gate, w_up, w_down,
    out, slots, packed, hidden, gate, up, down, load_sem, *sems
):
    ring = Ring(chips)
    half = rows_in.shape[0] // 2
    padded = out.shape[1]
    pieces = [
        (rows_in, slots, rows(0, half), "ring"),
        (rows_in, slots, rows(half, half), "ring"),
    ]
    loads = [
        pltpu.make_async_copy(source, target, load_sem.at[i])
        for i, (source, target) in enumerate(((w_gate, gate), (w_up, up), (w_down, down)))
    ]
    for load in loads:
        load.start()

    def whose(s):
        return [
            ring.owner(s - 1), ring.partner_owner(s - 1), ring.owner(s), ring.partner_owner(s)
        ]

    def widen(s):
        for j, who in enumerate(whose(s)):
            packed[j * padded : (j + 1) * padded, :] = jnp.dot(
                chosen_rows(slot_all[who], padded), slots[who],
                preferred_element_type=jnp.float32,
            ).astype(jnp.bfloat16)
        gate_val = jnp.dot(packed[...], gate[...], preferred_element_type=jnp.float32)
        up_val = jnp.dot(packed[...], up[...], preferred_element_type=jnp.float32)
        turned = (up_val + 1.0) * gate_val * jax.nn.sigmoid(ALPHA * gate_val)
        hidden[...] = turned.astype(jnp.bfloat16)

    def narrow(s):
        partial = lax.dot_general(
            hidden[...], down[...], (((1,), (1,)), ((), ())), preferred_element_type=jnp.float32
        ).astype(jnp.bfloat16)
        for j, who in enumerate(whose(s)):
            out[who] = partial[j * padded : (j + 1) * padded, :]

    def work(s):
        @pl.when(s == 1)
        def _():
            for load in loads:
                load.wait()

        pl.when(lax.rem(s, 2) == 1)(lambda: widen(s))
        pl.when((lax.rem(s, 2) == 0) & (s > 0))(lambda: narrow(s - 1))

    gather_ring(ring, pieces, sems, lambda: None, work)
    narrow(chips - 1)


def combine_kernel(
    chips, partial, slot_all, weight_all, mixed, out, cross_out, cross_in, ring_out, ring_in,
    ring_send, ring_recv, part_send, part_recv,
):
    ring = Ring(chips)
    tok_rows = mixed.shape[0]
    half = tok_rows // 2
    ring.barrier()

    def share(who, h):
        at = slice(h * half, (h + 1) * half)
        chosen = chosen_rows(slot_all[who], partial.shape[1], weight_all[who])
        return lax.dot_general(
            chosen[:, at], partial[who], (((0,), (0,)), ((), ())),
            preferred_element_type=jnp.float32,
        )

    def crossing(s, h):
        at = pl.ds(h * half, half)
        return pltpu.make_async_remote_copy(
            src_ref=cross_out.at[s, at, :],
            dst_ref=cross_in.at[s, at, :],
            send_sem=part_send.at[h, s],
            recv_sem=part_recv.at[h, s],
            device_id=ring.partner,
            device_id_type=MESH,
        )

    def onward(s, h):
        at = pl.ds(h * half, half)
        return pltpu.make_async_remote_copy(
            src_ref=ring_out.at[s, at, :],
            dst_ref=ring_in.at[s, at, :],
            send_sem=ring_send.at[h, s],
            recv_sem=ring_recv.at[h, s],
            device_id=ring.next,
            device_id_type=MESH,
        )

    def give(s):
        who = ring.partner_owner(s + 1)
        for h in range(2):
            at = pl.ds(h * half, half)
            cross_out[s, at, :] = share(who, h).astype(jnp.bfloat16)
            crossing(s, h).start()

    def own(s, h):
        total = share(ring.owner(s + 1), h)
        crossing(s, h).wait_recv()
        return total + cross_in[s, pl.ds(h * half, half), :].astype(jnp.float32)

    give(0)
    for h in range(2):
        ring_out[0, pl.ds(h * half, half), :] = own(0, h).astype(jnp.bfloat16)
        onward(0, h).start()
    give(1)

    def step(s, carry):
        for h in range(2):
            at = pl.ds(h * half, half)
            total = own(s, h)
            onward(s - 1, h).wait_recv()
            total = total + ring_in[s - 1, at, :].astype(jnp.float32)
            ring_out[s, at, :] = total.astype(jnp.bfloat16)
            onward(s, h).start()
        give(s + 1)
        return carry

    lax.fori_loop(1, chips - 1, step, 0)
    last = chips - 1
    for h in range(2):
        at = pl.ds(h * half, half)
        total = own(last, h)
        onward(last - 1, h).wait_recv()
        total = total + ring_in[last - 1, at, :].astype(jnp.float32)
        out[at, :] = (mixed[at, :].astype(jnp.float32) + total).astype(jnp.bfloat16)

    def drain(s, carry):
        for h in range(2):
            crossing(s, h).wait_send()

            @pl.when(s < chips - 1)
            def _():
                onward(s, h).wait_send()

        return carry

    lax.fori_loop(0, chips, drain, 0)


LOG2E = 1.4426950408889634
ANY = pl.BlockSpec(memory_space=pl.ANY)
SMEM = pl.BlockSpec(memory_space=pltpu.SMEM)


class Copies:
    def __init__(self):
        self.made = []

    def send(self, make, pred=None):
        self.made.append((make, pred))
        if pred is None:
            make().start()
        else:
            pl.when(pred)(lambda: make().start())

    def drain(self):
        for make, pred in self.made:
            if pred is None:
                make().wait_send()
            else:
                pl.when(pred)(lambda make=make: make().wait_send())


def remote(src, dst, send_sem, recv_sem, where):
    return pltpu.make_async_remote_copy(
        src_ref=src, dst_ref=dst, send_sem=send_sem, recv_sem=recv_sem,
        device_id=where, device_id_type=MESH,
    )


def landed(ref, sem):
    pltpu.make_async_copy(ref, ref, sem).wait()


def spans(width, size):
    return [(at, min(size, width - at)) for at in range(0, width, size)]


def front_kernel(
    planes, tokens_t, lengths, attn_gain, w_query, w_key, w_value, sinks, w_out, moe_gain,
    angles, routes, weights_in, mixed_out, expert_in, meta_all,
    tokens, table, meta, normed, wq, wkv, kv_own, kv_all, lhs, raw, qx, kx, vx, bias, top, acc, attended, wo,
    part, held, k_out, k_in, y_out, y_in,
    load_sem, wq_recv, wq_plane, wq_send, norm_recv, norm_send, kv_recv, kv_send,
    meta_recv, meta_send, wo_recv, wo_plane, wo_send, k_recv, k_send, y_recv, y_send,
):
    f32, bf16 = jnp.float32, jnp.bfloat16
    x, c = lax.axis_index("groups"), lax.axis_index("ctx")
    z, y, k, d = c // 4, lax.rem(c // 2, 2), lax.rem(c, 2), lax.rem(c, 4)
    total = 4 * planes
    width, rows = tokens_t.shape
    wq_rows, qcols = wq.shape[1], wq.shape[2]
    heads = qx.shape[0]
    plane_rows = 4 * rows

    def head_of(place):
        return lax.rem(3 * place, 4)

    g = head_of(d)
    partner, across = {"ctx": c + 1 - 2 * k}, {"ctx": c + 2 - 4 * y}
    peer = {"groups": 1 - x}
    copies = Copies()

    loads = [
        pltpu.make_async_copy(w_key, wkv.at[0], load_sem.at[0]),
        pltpu.make_async_copy(w_value, wkv.at[1], load_sem.at[1]),
        pltpu.make_async_copy(
            angles.at[:, pl.ds(z * plane_rows, plane_rows), :], table, load_sem.at[2]
        ),
        pltpu.make_async_copy(w_query.at[:, pl.ds(g * qcols, qcols)], wq.at[c], wq_recv.at[c]),
    ]
    cosine, sine = table.at[0], table.at[1]
    for load in loads:
        load.start()

    barrier = pltpu.get_barrier_semaphore()
    for r in range(1, total):
        pl.semaphore_signal(
            barrier, inc=1, device_id={"ctx": lax.rem(c + r, total)}, device_id_type=MESH
        )
    pl.semaphore_signal(barrier, inc=1, device_id=peer, device_id_type=MESH)
    pl.semaphore_wait(barrier, total)

    for r in (2, 3, 1):
        other = jnp.bitwise_xor(d, r)
        copies.send(
            lambda r=r, other=other: remote(
                w_query.at[:, pl.ds(head_of(other) * qcols, qcols)], wq.at[c],
                wq_plane.at[r], wq_recv.at[c], {"ctx": 4 * z + other},
            )
        )
    tokens[...] = tokens_t[...].T
    normed[d] = rms_scale(tokens[...], attn_gain[...][None, :])
    copies.send(
        lambda: remote(normed.at[d], normed.at[d], norm_send.at[0], norm_recv.at[d], across)
    )
    copies.send(
        lambda: remote(normed.at[d], normed.at[d], norm_send.at[1], norm_recv.at[d], partner)
    )

    def wq_relay(who, right, left, side):
        landed(wq.at[who], wq_recv.at[who])
        for i, (where, pred) in enumerate(
            (({"ctx": c + 4}, right), ({"ctx": c - 4}, left), (peer, side))
        ):
            if pred is not None:
                copies_start(
                    lambda i=i, where=where: remote(
                        wq.at[who], wq.at[who], wq_send.at[i, who], wq_recv.at[who], where
                    ),
                    pred,
                )

    def copies_start(make, pred):
        pl.when(pred)(lambda: make().start())

    upper, lower = z < planes - 1, z > 0
    always = z >= 0
    wq_relay(4 * z + 2 * y + x, upper, lower, None)

    for load in loads[:3]:
        load.wait()
    own = normed[d]
    lane = lax.broadcasted_iota(jnp.int32, (rows, 2 * HD), 1)
    first = lax.rem(lane, HD) < HD // 2
    mine = pl.ds(pl.multiple_of(d * rows, rows), rows)
    turn_cos, turn_sin = cosine[mine, :], sine[mine, :]

    def turned(pair, cos, sin, low):
        other = jnp.where(
            low, pltpu.roll(pair, 2 * HD - HD // 2, 1), pltpu.roll(pair, HD // 2, 1)
        )
        return pair * cos + other * sin

    raw_key = jnp.dot(own, wkv[0], preferred_element_type=f32)
    raw_value = jnp.dot(own, wkv[1], preferred_element_type=f32)
    for j in range(2):
        at = slice(j * 2 * HD, (j + 1) * 2 * HD)
        keys = turned(raw_key[:, at], turn_cos, turn_sin, first)
        values = raw_value[:, at]
        kv_own[2 * j] = jnp.where(lane < HD, keys, pltpu.roll(values, HD, 1)).astype(bf16)
        kv_own[2 * j + 1] = jnp.where(lane < HD, pltpu.roll(keys, HD, 1), values).astype(bf16)
    kv_all[c] = kv_own[g]

    def kv_copy(dz, other):
        return lambda: remote(
            kv_own.at[head_of(other)], kv_all.at[c], kv_send.at[dz, other], kv_recv.at[c],
            {"ctx": 4 * (z + dz) + other},
        )

    wq_relay(4 * z + 2 * (1 - y) + x, upper, lower, None)
    for dz in range(planes):
        for other in range(4):
            pred = (z + dz < planes) if dz else (d != other)
            copies.send(kv_copy(dz, other), pred)
    experts = meta.shape[0] // 2
    expert = lax.broadcasted_iota(jnp.int32, (experts, rows), 0)
    named, chosen = jnp.zeros((experts, rows), f32), jnp.zeros((experts, rows), f32)
    for t in range(routes.shape[0]):
        same = routes[t : t + 1, :] == expert
        named += jnp.where(same, 1.0, 0.0)
        chosen += jnp.where(same, weights_in[t : t + 1, :], 0.0)
    tri = (rows, rows)
    upto = lax.broadcasted_iota(jnp.int32, tri, 0) <= lax.broadcasted_iota(jnp.int32, tri, 1)
    place = jnp.dot(
        named.astype(bf16), jnp.where(upto, 1.0, 0.0).astype(bf16), preferred_element_type=f32
    )
    meta[:experts, :] = jnp.where(named > 0.5, place - 1.0, -1.0)
    meta[experts:, :] = chosen
    meta_all[c] = meta[...]
    for r in range(1, total):
        copies.send(
            lambda r=r: remote(
                meta, meta_all.at[c], meta_send.at[r], meta_recv.at[c],
                {"ctx": lax.rem(c + r, total)},
            )
        )

    def wo_rows(i):
        return pl.ds(pl.multiple_of(i * rows, rows), rows)

    wo_spans = spans(width, 1024)

    def wo_hand(n):
        at, size = wo_spans[n]
        return remote(
            w_out.at[pl.ds(at, size), :], wo.at[pl.ds(at, size), wo_rows(d)],
            wo_plane.at[n], wo_recv.at[d, n], {"ctx": 4 * z + head_of(z)},
        )

    def wo_keep(n):
        at, size = wo_spans[n]
        return pltpu.make_async_copy(
            w_out.at[pl.ds(at, size), :], wo.at[pl.ds(at, size), wo_rows(d)], wo_recv.at[d, n]
        )

    for s in range(1, planes):
        for j in range(2):

            @pl.when(z >= s)
            def _(s=s, j=j):
                wq_relay(4 * (z - s) + 2 * j + x, upper, None, always)

            @pl.when(z + s < planes)
            def _(s=s, j=j):
                wq_relay(4 * (z + s) + 2 * j + x, None, lower, always)

        if s == 1:
            for n in range(len(wo_spans)):
                pl.when(g == z)(lambda n=n: wo_keep(n).start())
                copies.send(lambda n=n: wo_hand(n), g != z)
            opposite = jnp.bitwise_xor(d, 2)
            landed(normed.at[opposite], norm_recv.at[opposite])
            copies.send(
                lambda: remote(
                    normed.at[opposite], normed.at[opposite],
                    norm_send.at[2], norm_recv.at[opposite], partner,
                )
            )

    def wo_relay(n, j):
        at, size = wo_spans[n]
        i = 2 * j + x
        piece = wo.at[pl.ds(at, size), wo_rows(i)]
        landed(piece, wo_recv.at[i, n])
        for way, (where, pred) in enumerate(wo_ways()):
            copies_start(
                lambda way=way, where=where: remote(
                    piece, piece, wo_send.at[way, i, n], wo_recv.at[i, n], where
                ),
                pred,
            )

    def wo_ways():
        return (
            ({"ctx": c + 4}, upper & (z >= g)),
            ({"ctx": c - 4}, lower & (z <= g)),
            (peer, z != g),
        )

    def wo_stage(stage):
        for n in range(len(wo_spans)):
            for j in range(2):
                jj = jnp.bitwise_xor(j, y)
                if stage == 0:
                    pl.when(z == g)(lambda n=n, jj=jj: wo_relay(n, jj))
                for away in range(1, planes):
                    if stage == n + away:
                        pl.when(jnp.abs(z - g) == away)(lambda n=n, jj=jj: wo_relay(n, jj))

    for r in (1, 3):
        other = jnp.bitwise_xor(d, r)
        landed(normed.at[other], norm_recv.at[other])
    for t in range(4):
        block = normed[t]
        for j in range(total):
            lhs[j, t * rows : (t + 1) * rows, :] = block[:, j * wq_rows : (j + 1) * wq_rows]

    wo_stage(0)
    raw[...] = jnp.zeros_like(raw)

    def query_rows(plane):
        for i in range(4):
            who = 4 * plane + i
            raw[...] += jnp.dot(lhs[who], wq[who], preferred_element_type=f32)

    query_rows_wait = lambda plane, i: landed(wq.at[4 * plane + i], wq_recv.at[4 * plane + i])
    for i in range(2):
        query_rows_wait(z, 2 * i + 1 - x)
    query_rows(z)
    for s in range(1, planes):
        for step in (-s, s):

            @pl.when((z + step >= 0) & (z + step < planes))
            def _(step=step):
                for i in range(2):
                    query_rows_wait(z + step, 2 * i + 1 - x)
                query_rows(z + step)

    ends = [lengths[0]]
    for i in range(1, lengths.shape[0]):
        ends.append(ends[-1] + lengths[i])

    def segment(start, shape):
        place = start + lax.broadcasted_iota(jnp.int32, shape, 0)
        found = jnp.zeros(shape, jnp.int32)
        for end in ends:
            found += (place >= end).astype(jnp.int32)
        return found

    wide = (plane_rows, 2 * HD)
    wide_lane = lax.broadcasted_iota(jnp.int32, wide, 1)
    mark = jnp.where(
        (wide_lane - HD == segment(z * plane_rows, wide)) & (wide_lane >= HD), 1.0, 0.0
    )
    wide_first = lax.rem(wide_lane, HD) < HD // 2

    for j in range(heads // 2):
        pair = turned(
            raw[:, j * 2 * HD : (j + 1) * 2 * HD], cosine[...], sine[...], wide_first
        ) * (SCALE * LOG2E)
        qx[2 * j] = jnp.where(wide_lane < HD, pair, mark).T.astype(bf16)
        qx[2 * j + 1] = jnp.where(wide_lane < HD, pltpu.roll(pair, HD, 1), mark).T.astype(bf16)

    def unpack(i, carry):
        @pl.when(i != c)
        def _():
            landed(kv_all.at[i], kv_recv.at[i])

        both = kv_all[i].astype(f32)
        apart = jnp.where(
            (lane - HD == segment(i * rows, lane.shape)) | (lane >= HD + len(ends)), 0.0, NEGATIVE
        )
        at = pl.ds(pl.multiple_of(i * rows, rows), rows)
        kx[at, :] = jnp.where(lane < HD, both, apart).astype(bf16)
        ones = jnp.where(lane == HD, 1.0, 0.0)
        vx[:, at] = jnp.where(lane < HD, pltpu.roll(both, HD, 1), ones).T[: vx.shape[0]].astype(bf16)
        return carry

    lax.fori_loop(0, 4 * (z + 1), unpack, 0)
    square = (plane_rows, plane_rows)
    bias[...] = jnp.where(
        lax.broadcasted_iota(jnp.int32, square, 0) <= lax.broadcasted_iota(jnp.int32, square, 1),
        0.0, NEGATIVE,
    )

    wo_stage(1)

    def attend(h):
        count_row = lax.broadcasted_iota(jnp.int32, acc.shape[1:], 0) == HD
        for e in range(2):
            top[e] = jnp.full(top.shape[1:], sinks[g * heads + h + e] * LOG2E, f32)
            acc[e] = jnp.where(count_row, 1.0, 0.0)

        def block(b, last):
            at = pl.ds(pl.multiple_of(b * plane_rows, plane_rows), plane_rows)
            scores = [
                jnp.dot(kx[at, :], qx[h + e], preferred_element_type=f32) for e in range(2)
            ]
            for e in range(2):
                score = scores[e] + bias[...] if last else scores[e]
                old = top[e]
                new = jnp.maximum(old, jnp.max(score, axis=0, keepdims=True))
                weights = jnp.exp2(score - new).astype(bf16)
                acc[e] = acc[e] * jnp.exp2(old - new) + jnp.dot(
                    vx[:, at], weights, preferred_element_type=f32
                )
                top[e] = new

        def body(b, carry):
            block(b, False)
            return carry

        lax.fori_loop(0, z, body, 0)
        block(z, True)
        for e in range(2):
            at = pl.ds(pl.multiple_of((h + e) * HD, HD), HD)
            attended[at, :] = (acc[e, :HD, :] / acc[e, HD : HD + 1, :]).astype(bf16)

    def pair_of_heads(j, carry):
        for stage in range(1, heads // 2):
            pl.when(j == stage)(lambda stage=stage: wo_stage(stage + 1))
        attend(2 * j)
        return carry

    lax.fori_loop(0, heads // 2, pair_of_heads, 0)
    wo_stage(5)

    lhs_out = attended[...].T
    give, keep = 1 - k, k

    def k_copy(n):
        at, size = wo_spans[n]
        return remote(
            k_out.at[:, :, pl.ds(at, size)], k_in.at[:, :, pl.ds(at, size)],
            k_send.at[n], k_recv.at[n], partner,
        )

    def y_copy(n):
        at, size = wo_spans[n]
        return remote(
            y_out.at[:, pl.ds(at, size)], y_in.at[:, pl.ds(at, size)],
            y_send.at[n], y_recv.at[n], across,
        )

    def project(n):
        at, size = wo_spans[n]
        cols = pl.ds(at, size)
        for j in range(2):
            i = 2 * j + 1 - x
            landed(wo.at[cols, wo_rows(i)], wo_recv.at[i, n])
        part[:, :size] = lax.dot_general(
            lhs_out, wo[cols, :], (((1,), (1,)), ((), ())), preferred_element_type=f32
        )
        for j in range(2):
            k_out[j, :, cols] = part[wo_rows(2 * j + give), :size].astype(bf16)
            held[j, :, cols] = part[wo_rows(2 * j + keep), :size]
        copies.send(lambda: k_copy(n))

    def fold(n):
        at, size = wo_spans[n]
        cols = pl.ds(at, size)
        k_copy(n).wait_recv()
        y_out[:, cols] = (held[1 - y, :, cols] + k_in[1 - y, :, cols].astype(f32)).astype(bf16)
        copies.send(lambda: y_copy(n))

    def finish(n):
        at, size = wo_spans[n]
        cols = pl.ds(at, size)
        mine = held[y, :, cols] + k_in[y, :, cols].astype(f32) + tokens[:, cols].astype(f32)
        y_copy(n).wait_recv()
        mixed_out[:, cols] = (mine + y_in[:, cols].astype(f32)).astype(bf16)

    count = len(wo_spans)
    for n in range(count):
        project(n)
        fold(n)
    for n in range(count):
        finish(n)
    expert_in[...] = rms_scale(mixed_out[...], moe_gain[...][None, :])

    def meta_arrived(i, carry):
        @pl.when(i != c)
        def _():
            landed(meta_all.at[i], meta_recv.at[i])

        return carry

    lax.fori_loop(0, total, meta_arrived, 0)
    copies.drain()

    def wq_drain(who, ways):
        for i, pred in enumerate(ways):
            pl.when(pred)(
                lambda i=i: remote(
                    wq.at[who], wq.at[who], wq_send.at[i, who], wq_recv.at[who], partner
                ).wait_send()
            )

    never = z < 0
    for j in range(2):
        wq_drain(4 * z + 2 * j + x, (upper, lower))
    for s in range(1, planes):
        for j in range(2):
            pl.when(z >= s)(
                lambda s=s, j=j: wq_drain(4 * (z - s) + 2 * j + x, (upper, never, always))
            )
            pl.when(z + s < planes)(
                lambda s=s, j=j: wq_drain(4 * (z + s) + 2 * j + x, (never, lower, always))
            )
    for n, (at, size) in enumerate(wo_spans):
        for j in range(2):
            i = 2 * j + x
            piece = wo.at[pl.ds(at, size), wo_rows(i)]
            for way, (where, pred) in enumerate(wo_ways()):
                pl.when(pred)(
                    lambda way=way, where=where: remote(
                        piece, piece, wo_send.at[way, i, n], wo_recv.at[i, n], where
                    ).wait_send()
                )


def front(tokens, lengths, attn_gain, w_query, w_key, w_value, sinks, w_out, moe_gain, routes, weights):
    bf16, f32 = jnp.bfloat16, jnp.float32
    rows, width = tokens.shape
    devices = lax.axis_size("ctx")
    planes = devices // 4
    seq = devices * rows
    quarter = w_query.shape[1] // 4
    heads = quarter // HD
    count = len(spans(width, 1024))
    place = np.arange(seq, dtype=np.float32)
    freqs = np.float32(THETA) ** (-np.arange(HD // 2, dtype=np.float32) / np.float32(HD // 2))
    angles = place[:, None] * freqs[None, :].astype(np.float32)
    cos, sin = np.cos(angles).astype(np.float32), np.sin(angles).astype(np.float32)
    tables = np.stack(
        [np.tile(cos, (1, 4)), np.tile(np.concatenate([-sin, sin], axis=1), (1, 2))]
    )
    meta_shape = (devices, rows)
    dma = pltpu.SemaphoreType.DMA
    vmem = pltpu.VMEM
    return pl.pallas_call(
        functools.partial(front_kernel, planes),
        out_shape=[
            jax.ShapeDtypeStruct((rows, width), bf16),
            jax.ShapeDtypeStruct((rows, width), bf16),
            jax.ShapeDtypeStruct((devices,) + meta_shape, f32),
        ],
        in_specs=[VMEM, SMEM, VMEM, ANY, ANY, ANY, SMEM, ANY, VMEM, ANY, VMEM, VMEM],
        out_specs=[VMEM] * 3,
        scratch_shapes=[
            vmem((rows, width), bf16),
            vmem((2, 4 * rows, 2 * HD), f32),
            vmem(meta_shape, f32),
            vmem((4, rows, width), bf16),
            vmem((devices, w_query.shape[0], quarter), bf16),
            vmem((2,) + w_key.shape, bf16),
            vmem((4, rows, 2 * HD), bf16),
            vmem((devices, rows, 2 * HD), bf16),
            vmem((devices, 4 * rows, w_query.shape[0]), bf16),
            vmem((4 * rows, quarter), f32),
            vmem((heads, 2 * HD, 4 * rows), bf16),
            vmem((seq, 2 * HD), bf16),
            vmem((HD + 16, seq), bf16),
            vmem((4 * rows, 4 * rows), f32),
            vmem((2, 1, 4 * rows), f32),
            vmem((2, HD + 16, 4 * rows), f32),
            vmem((quarter, 4 * rows), bf16),
            vmem((width, 4 * rows), bf16),
            vmem((4 * rows, 1024), f32),
            vmem((2, rows, width), f32),
            vmem((2, rows, width), bf16),
            vmem((2, rows, width), bf16),
            vmem((rows, width), bf16),
            vmem((rows, width), bf16),
            dma((3,)),
            dma((devices,)), dma((4,)), dma((3, devices)),
            dma((4,)), dma((3,)),
            dma((devices,)), dma((planes, 4)),
            dma((devices,)), dma((devices,)),
            dma((4, count)), dma((count,)), dma((3, 4, count)),
            dma((count,)), dma((count,)), dma((count,)), dma((count,)),
        ],
        compiler_params=pltpu.CompilerParams(
            collective_id=4, has_side_effects=True, vmem_limit_bytes=LIMIT
        ),
    )(
        tokens.T, lengths, attn_gain, w_query, w_key, w_value, sinks, w_out.T,
        moe_gain, jnp.asarray(tables), routes.T, weights.T,
    )


def call(kernel, chips, out_shape, scratch, identity, *args, smem=(), hbm=()):
    single = not isinstance(out_shape, (list, tuple))
    return pl.pallas_call(
        functools.partial(kernel, chips),
        out_shape=out_shape,
        in_specs=[
            pl.BlockSpec(memory_space=pltpu.SMEM)
            if i in smem
            else pl.BlockSpec(memory_space=pl.ANY)
            if i in hbm
            else VMEM
            for i in range(len(args))
        ],
        out_specs=VMEM if single else [VMEM] * len(out_shape),
        scratch_shapes=scratch,
        compiler_params=pltpu.CompilerParams(
            collective_id=identity, has_side_effects=True, vmem_limit_bytes=LIMIT
        ),
    )(*args)


def ring_front(
    tokens, lengths, attn_gain, w_query, w_key, w_value, sinks, w_out, moe_gain, routes,
    route_weights,
):
    bf16, f32 = jnp.bfloat16, jnp.float32
    tok_rows, width = tokens.shape
    devices = lax.axis_size("ctx")
    chips = devices // 2
    me = lax.axis_index("ctx")
    q_cols = w_query.shape[1]
    num_heads = q_cols // HD
    kv_cols = w_key.shape[1]
    kv_heads = kv_cols // HD
    experts = chips
    member = routes[:, :, None] == jnp.arange(experts, dtype=jnp.int32)[None, None, :]
    named = jnp.any(member, axis=1)
    lower = jnp.tril(jnp.ones((tok_rows, tok_rows), bf16))
    slot = jnp.dot(lower, named.astype(bf16), preferred_element_type=f32) - 1.0
    slot = jnp.where(named, slot, -1.0)
    routed_weight = jnp.sum(jnp.where(member, route_weights[:, :, None], 0.0), axis=1)
    meta = jnp.concatenate([slot, routed_weight], axis=1).T

    positions = me * tok_rows + jnp.arange(tok_rows, dtype=jnp.int32)
    freqs = THETA ** (-jnp.arange(HD // 2, dtype=f32) / (HD // 2))
    angles = positions.astype(f32)[:, None] * freqs[None, :]
    cosine, sine = jnp.cos(angles)[:, None, :], jnp.sin(angles)[:, None, :]

    def rotate(values):
        first, second = values[..., : HD // 2], values[..., HD // 2 :]
        return jnp.concatenate(
            [first * cosine - second * sine, second * cosine + first * sine], axis=-1
        ).astype(bf16)

    normed = rms_scale(tokens, attn_gain)
    raw_key = jnp.dot(normed, w_key, preferred_element_type=f32)
    value = jnp.dot(normed, w_value, preferred_element_type=f32).astype(bf16)
    key = rotate(raw_key.reshape(tok_rows, kv_heads, HD)).reshape(tok_rows, kv_cols)
    kv = jnp.concatenate([key, value], axis=1)
    lhs = normed.reshape(tok_rows, devices, width // devices).transpose(1, 0, 2)
    raw_query, kv_all, meta_all = call(
        query_kernel,
        chips,
        [
            jax.ShapeDtypeStruct((tok_rows, q_cols), f32),
            jax.ShapeDtypeStruct((devices,) + kv.shape, bf16),
            jax.ShapeDtypeStruct((devices,) + meta.shape, f32),
        ],
        [pltpu.VMEM((devices,) + w_query.shape, bf16)] + gather_sems(5, chips),
        0,
        lhs, kv, meta, w_query,
    )
    cosine_pair = jnp.tile(cosine[:, 0, :], (1, 4))
    sine_pair = jnp.tile(jnp.concatenate([-sine[:, 0, :], sine[:, 0, :]], axis=1), (1, 2))
    doc_ends = jnp.dot(jnp.tril(jnp.ones((lengths.size,) * 2, jnp.int32)), lengths)
    start = jnp.max(
        jnp.where(positions[:, None] >= doc_ends[None, :], doc_ends[None, :], 0), axis=1
    )[:, None]
    mixed, expert_in = call(
        attend_kernel,
        chips,
        [jax.ShapeDtypeStruct((tok_rows, width), bf16)] * 2,
        [
            pltpu.VMEM((tok_rows, width), f32),
            pltpu.VMEM((devices,) + w_out.shape, bf16),
            pltpu.VMEM((tok_rows, devices * tok_rows), f32),
            pltpu.VMEM((num_heads, tok_rows, HD), bf16),
            pltpu.VMEM((kv_heads, devices * tok_rows, HD), bf16),
            pltpu.VMEM((kv_heads, devices * tok_rows, HD), bf16),
            pltpu.VMEM((devices, tok_rows, w_out.shape[0]), bf16),
        ]
        + gather_sems(3, chips),
        1,
        raw_query, kv_all, cosine_pair, sine_pair, sinks, start, w_out, tokens, moe_gain[None, :],
        smem=(4,),
    )
    return mixed, expert_in, meta_all


def per_device(
    tokens, lengths, attn_gain, w_query, w_key, w_value, sinks, w_out, moe_gain, routes,
    route_weights, w_gate, w_up, w_down,
):
    bf16, f32 = jnp.bfloat16, jnp.float32
    tok_rows, width = tokens.shape
    devices = lax.axis_size("ctx")
    chips = devices // 2
    me = lax.axis_index("ctx")
    experts = chips
    capacity = tok_rows * 4 * 17 // (16 * experts)
    padded = -(-capacity // 16) * 16

    square = lax.axis_size("groups") == 2 and devices == 16
    mixed, expert_in, meta_all = (front if square else ring_front)(
        tokens, lengths, attn_gain, w_query, w_key, w_value, sinks, w_out, moe_gain, routes,
        route_weights,
    )
    expert = me // 2
    slot_all = lax.dynamic_slice_in_dim(meta_all, expert, 1, 1)
    weight_all = lax.dynamic_slice_in_dim(meta_all, experts + expert, 1, 1)
    partial = call(
        expert_kernel,
        chips,
        jax.ShapeDtypeStruct((devices, padded, width), bf16),
        [
            pltpu.VMEM((devices, tok_rows, width), bf16),
            pltpu.VMEM((4 * padded, width), bf16),
            pltpu.VMEM((4 * padded, w_gate.shape[2]), bf16),
            pltpu.VMEM(w_gate.shape[1:], bf16),
            pltpu.VMEM(w_up.shape[1:], bf16),
            pltpu.VMEM(w_down.shape[:0:-1], bf16),
            pltpu.SemaphoreType.DMA((3,)),
        ]
        + gather_sems(2, chips),
        2,
        expert_in, slot_all, w_gate[0], w_up[0], w_down[0].T,
        hbm=(2, 3, 4),
    )
    return call(
        combine_kernel,
        chips,
        jax.ShapeDtypeStruct((tok_rows, width), bf16),
        [pltpu.VMEM((chips, tok_rows, width), bf16)] * 2
        + [pltpu.VMEM((chips - 1, tok_rows, width), bf16)] * 2
        + ring_sems(2, chips),
        3,
        partial, slot_all, weight_all, mixed,
    )


def solution(mesh):
    placed = (
        P(("groups", "ctx"), None),
        P("groups"),
        P(),
        P("ctx", None),
        P(),
        P(),
        P(),
        P("ctx", None),
        P(),
        P(("groups", "ctx"), None),
        P(("groups", "ctx"), None),
        P("ctx", None, None),
        P("ctx", None, None),
        P("ctx", None, None),
    )
    return jax.shard_map(
        per_device,
        mesh=mesh,
        in_specs=placed,
        out_specs=P(("groups", "ctx"), None),
        check_vma=False,
    )
```

```python
import functools

import jax
import jax.numpy as jnp
import numpy as np
from jax import lax
from jax.experimental import pallas as pl
from jax.experimental.pallas import tpu as pltpu
from jax.sharding import PartitionSpec as P

HD = 64
EPS = 1e-05
THETA = 150000.0
ALPHA = 1.702
SCALE = 0.125
NEGATIVE = -1e30
MESH = pl.DeviceIdType.MESH
VMEM = pl.BlockSpec(memory_space=pltpu.VMEM)
LIMIT = 63 * 1024 * 1024


def rms_scale(values, gain_vec):
    wide = values.astype(jnp.float32)
    inverse = lax.rsqrt(jnp.mean(wide * wide, axis=-1, keepdims=True) + EPS)
    return (wide * inverse * gain_vec).astype(jnp.bfloat16)


class Ring:
    def __init__(self, chips):
        self.chips = chips
        self.me = lax.axis_index("ctx")
        self.core = lax.rem(self.me, 2)
        chip = self.me // 2
        self.fold = chips == 8
        if self.fold:
            z, y = chip // 2, lax.rem(chip, 2)
            self.pos = z + y * (chips - 1 - 2 * z)
        else:
            self.pos = chip
        self.way = 1 - 2 * self.core
        self.partner = {"ctx": self.me + self.way}
        self.next = {"ctx": self.owner(-1)}
        self.prev = {"ctx": self.owner(1)}
        group = lax.axis_index("groups")
        self.parity = lax.rem(group, 2)
        self.peer = {"groups": group + 1 - 2 * self.parity}

    def index(self, pos, core):
        pos = lax.rem(pos + 2 * self.chips, self.chips)
        if self.fold:
            y = pos // (self.chips // 2)
            z = pos + y * (self.chips - 1 - 2 * pos)
            chip = z * 2 + y
        else:
            chip = pos
        return chip * 2 + core

    def owner(self, step):
        return self.index(self.pos - self.way * step, self.core)

    def partner_owner(self, step):
        return self.index(self.pos + self.way * step, 1 - self.core)

    def barrier(self, with_peer=False):
        sem = pltpu.get_barrier_semaphore()
        others = [self.next, self.prev, self.partner] + ([self.peer] if with_peer else [])
        for other in others:
            pl.semaphore_signal(sem, inc=1, device_id=other, device_id_type=MESH)
        pl.semaphore_wait(sem, len(others))


def gather_ring(ring, pieces, sems, setup, work):
    ring_send, ring_recv, part_send, part_recv, peer_send, peer_recv = sems
    chips = ring.chips
    ringed = [i for i, piece in enumerate(pieces) if piece[3] != "peer"]
    peered = [i for i, piece in enumerate(pieces) if piece[3] == "peer"]
    shared = [i for i, piece in enumerate(pieces) if piece[3] == "both"]
    lag = 2 if peered else 1

    def copy(i, step, target, send, recv, own=False):
        source, slots, view, _ = pieces[i]
        dst = view(slots.at[ring.owner(step)])
        return pltpu.make_async_remote_copy(
            src_ref=view(source) if own else dst,
            dst_ref=dst,
            send_sem=send,
            recv_sem=recv,
            device_id=target,
            device_id_type=MESH,
        )

    def onward(i, step, own=False):
        return copy(
            i, step, ring.next, ring_send.at[i, step], ring_recv.at[i, step + 1], own
        )

    def across(i, step, own=False):
        return copy(i, step, ring.partner, part_send.at[i, step], part_recv.at[i, step], own)

    def aside(i, step):
        return copy(i, step, ring.peer, peer_send.at[step], peer_recv.at[step])

    def arrived(i, sem, who):
        ref = pieces[i][2](pieces[i][1].at[who])
        pltpu.make_async_copy(ref, ref, sem).wait()

    ring.barrier(bool(peered))
    for i in ringed:
        onward(i, 0, True).start()
    for i in range(len(pieces)):
        across(i, 0, True).start()
    filled = []
    for source, slots, _, _ in pieces:
        if not any(slots is other for other in filled):
            slots[ring.me] = source[...]
            filled.append(slots)
    setup()

    def turn(t, carry):
        @pl.when(t < chips)
        def _():
            for i in ringed:
                arrived(i, ring_recv.at[i, t], ring.owner(t))

                @pl.when(t < chips - 1)
                def _():
                    onward(i, t).start()

                if i in shared:
                    aside(i, t).start()
                across(i, t).start()

        if peered:

            @pl.when((t > 1) & (t <= chips))
            def _():
                for i in peered:
                    arrived(i, peer_recv.at[t - 1], ring.owner(t - 1))
                    across(i, t - 1).start()

        @pl.when(t >= lag)
        def _():
            s = t - lag
            for i in range(len(pieces)):
                arrived(i, part_recv.at[i, s], ring.partner_owner(s))
            work(s)

        return carry

    lax.fori_loop(1, chips + lag, turn, 0)

    def drain(s, carry):
        for i in range(len(pieces)):
            across(i, s).wait_send()
        for i in ringed:

            @pl.when(s < chips - 1)
            def _():
                onward(i, s).wait_send()

        for i in shared:

            @pl.when(s > 0)
            def _():
                aside(i, s).wait_send()

        return carry

    lax.fori_loop(0, chips, drain, 0)


def ring_sems(count, chips):
    return [pltpu.SemaphoreType.DMA((count, chips))] * 4


def gather_sems(count, chips):
    return ring_sems(count, chips) + [pltpu.SemaphoreType.DMA((chips,))] * 2


def whole(ref):
    return ref


def cols(start, size):
    return lambda ref: ref.at[:, pl.ds(start, size)]


def rows(start, size):
    return lambda ref: ref.at[pl.ds(start, size), :]


def thirds(ring, source, slots):
    width = source.shape[1]
    third = width // 3 // 128 * 128
    mine = pl.multiple_of(ring.parity * third, 128)
    other = pl.multiple_of((1 - ring.parity) * third, 128)
    return [
        (source, slots, cols(mine, third), "both"),
        (source, slots, cols(2 * third, width - 2 * third), "ring"),
        (source, slots, cols(other, third), "peer"),
    ]


def query_kernel(chips, lhs, kv, meta, weight, out, kv_all, meta_all, slots, *sems):
    ring = Ring(chips)
    pieces = [(kv, kv_all, whole, "ring"), (meta, meta_all, whole, "ring")]
    pieces += thirds(ring, weight, slots)

    def setup():
        out[...] = jnp.zeros_like(out)

    def work(s):
        for who in (ring.owner(s), ring.partner_owner(s)):
            out[...] += jnp.dot(lhs[who], slots[who], preferred_element_type=jnp.float32)

    gather_ring(ring, pieces, sems, setup, work)


def attend_kernel(
    chips, raw, kv_all, cosine, sine, sinks, start, weight, tokens, gain,
    mixed_out, expert_in, out, slots, bias, query, key, value, attended, *sems
):
    ring = Ring(chips)
    blocks, tok_rows, width = attended.shape
    per_block = width // HD
    kv_heads, seq, _ = key.shape
    group = query.shape[0] // kv_heads
    pieces = thirds(ring, weight, slots)

    def setup():
        key_pos = lax.broadcasted_iota(jnp.int32, (tok_rows, seq), 1)
        row_pos = lax.broadcasted_iota(jnp.int32, (tok_rows, seq), 0) + ring.me * tok_rows
        allowed = (key_pos <= row_pos) & (key_pos >= start[...])
        bias[...] = jnp.where(allowed, 0.0, NEGATIVE)
        lane = lax.broadcasted_iota(jnp.int32, (tok_rows, 2 * HD), 1)
        first = lax.rem(lane, HD) < HD // 2

        def turn_pair(j, carry):
            pair = raw[:, pl.ds(pl.multiple_of(j * 2 * HD, 2 * HD), 2 * HD)]
            other = jnp.where(
                first, pltpu.roll(pair, 2 * HD - HD // 2, 1), pltpu.roll(pair, HD // 2, 1)
            )
            turned = ((pair * cosine[...] + other * sine[...]) * SCALE).astype(jnp.bfloat16)
            query[2 * j] = turned[:, :HD]
            query[2 * j + 1] = turned[:, HD:]
            return carry

        lax.fori_loop(0, query.shape[0] // 2, turn_pair, 0)

        def unpack(d, carry):
            at = pl.ds(pl.multiple_of(d * tok_rows, tok_rows), tok_rows)
            block = kv_all[d]
            for g in range(kv_heads):
                key[g, at, :] = block[:, g * HD : (g + 1) * HD]
                value[g, at, :] = block[:, (kv_heads + g) * HD : (kv_heads + g + 1) * HD]
            return carry

        lax.fori_loop(0, blocks, unpack, 0)

    def attend(who):
        heads = []
        for j in range(per_block):
            head = who * per_block + j
            kv_head = head // group
            scores = (
                lax.dot_general(
                    query[head],
                    key[kv_head],
                    (((1,), (1,)), ((), ())),
                    preferred_element_type=jnp.float32,
                )
                + bias[...]
            )
            sink = sinks[head]
            top = jnp.maximum(jnp.max(scores, axis=1, keepdims=True), sink)
            weights = jnp.exp(scores - top)
            total = jnp.sum(weights, axis=1, keepdims=True) + jnp.exp(sink - top)
            mixed = jnp.dot(
                weights.astype(jnp.bfloat16), value[kv_head], preferred_element_type=jnp.float32
            )
            heads.append(mixed / total)
        joined = heads[0] if per_block == 1 else jnp.concatenate(heads, axis=1)
        attended[who] = joined.astype(jnp.bfloat16)

    def work(s):
        attend(ring.owner(s))
        attend(ring.partner_owner(s))

    gather_ring(ring, pieces, sems, setup, work)
    out[...] = tokens[...].astype(jnp.float32)

    def project(d, carry):
        out[...] += jnp.dot(attended[d], slots[d], preferred_element_type=jnp.float32)
        return carry

    lax.fori_loop(0, blocks, project, 0)
    mixed_out[...] = out[...].astype(jnp.bfloat16)
    expert_in[...] = rms_scale(mixed_out[...], gain[...])


def chosen_rows(slot, padded, weight=None):
    place = lax.broadcasted_iota(jnp.int32, (padded, slot.shape[1]), 0).astype(jnp.float32)
    return jnp.where(place == slot, 1.0 if weight is None else weight, 0.0).astype(jnp.bfloat16)


def expert_kernel(
    chips, rows_in, meta_all, w_gate, w_up, w_down,
    out, slots, packed, hidden, gate, up, down, load_sem, *sems
):
    ring = Ring(chips)
    half = rows_in.shape[0] // 2
    padded = out.shape[1]
    pieces = [
        (rows_in, slots, rows(0, half), "ring"),
        (rows_in, slots, rows(half, half), "ring"),
    ]
    loads = [
        pltpu.make_async_copy(source, target, load_sem.at[i])
        for i, (source, target) in enumerate(((w_gate, gate), (w_up, up), (w_down, down)))
    ]
    for load in loads:
        load.start()

    def whose(s):
        return [
            ring.owner(s - 1), ring.partner_owner(s - 1), ring.owner(s), ring.partner_owner(s)
        ]

    def widen(s):
        for j, who in enumerate(whose(s)):
            packed[j * padded : (j + 1) * padded, :] = jnp.dot(
                chosen_rows(meta_all[who, pl.ds(ring.me // 2, 1), :], padded), slots[who],
                preferred_element_type=jnp.float32,
            ).astype(jnp.bfloat16)
        gate_val = jnp.dot(packed[...], gate[...], preferred_element_type=jnp.float32)
        up_val = jnp.dot(packed[...], up[...], preferred_element_type=jnp.float32)
        turned = (up_val + 1.0) * gate_val * jax.nn.sigmoid(ALPHA * gate_val)
        hidden[...] = turned.astype(jnp.bfloat16)

    def narrow(s):
        partial = lax.dot_general(
            hidden[...], down[...], (((1,), (1,)), ((), ())), preferred_element_type=jnp.float32
        ).astype(jnp.bfloat16)
        for j, who in enumerate(whose(s)):
            out[who] = partial[j * padded : (j + 1) * padded, :]

    def work(s):
        @pl.when(s == 1)
        def _():
            for load in loads:
                load.wait()

        pl.when(lax.rem(s, 2) == 1)(lambda: widen(s))
        pl.when((lax.rem(s, 2) == 0) & (s > 0))(lambda: narrow(s - 1))

    gather_ring(ring, pieces, sems, lambda: None, work)
    narrow(chips - 1)


def combine_kernel(
    chips, partial, meta_all, mixed, out, cross_out, cross_in, ring_out, ring_in,
    ring_send, ring_recv, part_send, part_recv,
):
    ring = Ring(chips)
    tok_rows = mixed.shape[0]
    half = tok_rows // 2
    ring.barrier()

    def share(who, h):
        at = slice(h * half, (h + 1) * half)
        expert = ring.me // 2
        chosen = chosen_rows(
            meta_all[who, pl.ds(expert, 1), :], partial.shape[1],
            meta_all[who, pl.ds(chips + expert, 1), :],
        )
        return lax.dot_general(
            chosen[:, at], partial[who], (((0,), (0,)), ((), ())),
            preferred_element_type=jnp.float32,
        )

    def crossing(s, h):
        at = pl.ds(h * half, half)
        return pltpu.make_async_remote_copy(
            src_ref=cross_out.at[s, at, :],
            dst_ref=cross_in.at[s, at, :],
            send_sem=part_send.at[h, s],
            recv_sem=part_recv.at[h, s],
            device_id=ring.partner,
            device_id_type=MESH,
        )

    def onward(s, h):
        at = pl.ds(h * half, half)
        return pltpu.make_async_remote_copy(
            src_ref=ring_out.at[s, at, :],
            dst_ref=ring_in.at[s, at, :],
            send_sem=ring_send.at[h, s],
            recv_sem=ring_recv.at[h, s],
            device_id=ring.next,
            device_id_type=MESH,
        )

    def give(s):
        who = ring.partner_owner(s + 1)
        for h in range(2):
            at = pl.ds(h * half, half)
            cross_out[s, at, :] = share(who, h).astype(jnp.bfloat16)
            crossing(s, h).start()

    def own(s, h):
        total = share(ring.owner(s + 1), h)
        crossing(s, h).wait_recv()
        return total + cross_in[s, pl.ds(h * half, half), :].astype(jnp.float32)

    give(0)
    for h in range(2):
        ring_out[0, pl.ds(h * half, half), :] = own(0, h).astype(jnp.bfloat16)
        onward(0, h).start()
    give(1)

    def step(s, carry):
        for h in range(2):
            at = pl.ds(h * half, half)
            total = own(s, h)
            onward(s - 1, h).wait_recv()
            total = total + ring_in[s - 1, at, :].astype(jnp.float32)
            ring_out[s, at, :] = total.astype(jnp.bfloat16)
            onward(s, h).start()
        give(s + 1)
        return carry

    lax.fori_loop(1, chips - 1, step, 0)
    last = chips - 1
    for h in range(2):
        at = pl.ds(h * half, half)
        total = own(last, h)
        onward(last - 1, h).wait_recv()
        total = total + ring_in[last - 1, at, :].astype(jnp.float32)
        out[at, :] = (mixed[at, :].astype(jnp.float32) + total).astype(jnp.bfloat16)

    def drain(s, carry):
        for h in range(2):
            crossing(s, h).wait_send()

            @pl.when(s < chips - 1)
            def _():
                onward(s, h).wait_send()

        return carry

    lax.fori_loop(0, chips, drain, 0)


LOG2E = 1.4426950408889634
ANY = pl.BlockSpec(memory_space=pl.ANY)
SMEM = pl.BlockSpec(memory_space=pltpu.SMEM)


class Copies:
    def __init__(self):
        self.made = []

    def send(self, make, pred=None):
        self.made.append((make, pred))
        if pred is None:
            make().start()
        else:
            pl.when(pred)(lambda: make().start())

    def drain(self):
        for make, pred in self.made:
            if pred is None:
                make().wait_send()
            else:
                pl.when(pred)(lambda make=make: make().wait_send())


def remote(src, dst, send_sem, recv_sem, where):
    return pltpu.make_async_remote_copy(
        src_ref=src, dst_ref=dst, send_sem=send_sem, recv_sem=recv_sem,
        device_id=where, device_id_type=MESH,
    )


def landed(ref, sem):
    pltpu.make_async_copy(ref, ref, sem).wait()


def spans(width, size):
    return [(at, min(size, width - at)) for at in range(0, width, size)]


def front_kernel(
    planes, tokens_t, lengths, attn_gain, w_query, w_key, w_value, sinks, w_out, moe_gain,
    angles, routes, weights_in, mixed_out, expert_in, meta_all,
    tokens, table, meta, normed, wq, wkv, kv_own, kv_all, lhs, raw, qx, kx, vx, bias, top, acc, attended, wo,
    part, held, k_out, k_in, y_out, y_in,
    load_sem, wq_recv, wq_plane, wq_send, norm_recv, norm_send, kv_recv, kv_send,
    meta_recv, meta_send, wo_recv, wo_plane, wo_send, k_recv, k_send, y_recv, y_send,
):
    f32, bf16 = jnp.float32, jnp.bfloat16
    x, c = lax.axis_index("groups"), lax.axis_index("ctx")
    z, y, k, d = c // 4, lax.rem(c // 2, 2), lax.rem(c, 2), lax.rem(c, 4)
    total = 4 * planes
    width, rows = tokens_t.shape
    wq_rows, qcols = wq.shape[1], wq.shape[2]
    heads = qx.shape[0]
    plane_rows = 4 * rows

    def head_of(place):
        return lax.rem(3 * place, 4)

    g = head_of(d)
    partner, across = {"ctx": c + 1 - 2 * k}, {"ctx": c + 2 - 4 * y}
    peer = {"groups": 1 - x}
    copies = Copies()

    loads = [
        pltpu.make_async_copy(w_key, wkv.at[0], load_sem.at[0]),
        pltpu.make_async_copy(w_value, wkv.at[1], load_sem.at[1]),
        pltpu.make_async_copy(
            angles.at[:, pl.ds(z * plane_rows, plane_rows), :], table, load_sem.at[2]
        ),
        pltpu.make_async_copy(w_query.at[:, pl.ds(g * qcols, qcols)], wq.at[c], wq_recv.at[c]),
    ]
    cosine, sine = table.at[0], table.at[1]
    for load in loads:
        load.start()

    barrier = pltpu.get_barrier_semaphore()
    for r in range(1, total):
        pl.semaphore_signal(
            barrier, inc=1, device_id={"ctx": lax.rem(c + r, total)}, device_id_type=MESH
        )
    pl.semaphore_signal(barrier, inc=1, device_id=peer, device_id_type=MESH)
    pl.semaphore_wait(barrier, total)

    for r in (2, 3, 1):
        other = jnp.bitwise_xor(d, r)
        copies.send(
            lambda r=r, other=other: remote(
                w_query.at[:, pl.ds(head_of(other) * qcols, qcols)], wq.at[c],
                wq_plane.at[r], wq_recv.at[c], {"ctx": 4 * z + other},
            )
        )
    tokens[...] = tokens_t[...].T
    normed[d] = rms_scale(tokens[...], attn_gain[...][None, :])
    copies.send(
        lambda: remote(normed.at[d], normed.at[d], norm_send.at[0], norm_recv.at[d], across)
    )
    copies.send(
        lambda: remote(normed.at[d], normed.at[d], norm_send.at[1], norm_recv.at[d], partner)
    )

    def wq_relay(who, right, left, side):
        landed(wq.at[who], wq_recv.at[who])
        for i, (where, pred) in enumerate(
            (({"ctx": c + 4}, right), ({"ctx": c - 4}, left), (peer, side))
        ):
            if pred is not None:
                copies_start(
                    lambda i=i, where=where: remote(
                        wq.at[who], wq.at[who], wq_send.at[i, who], wq_recv.at[who], where
                    ),
                    pred,
                )

    def copies_start(make, pred):
        pl.when(pred)(lambda: make().start())

    upper, lower = z < planes - 1, z > 0
    always = z >= 0
    wq_relay(4 * z + 2 * y + x, upper, lower, None)

    for load in loads[:3]:
        load.wait()
    own = normed[d]
    lane = lax.broadcasted_iota(jnp.int32, (rows, 2 * HD), 1)
    first = lax.rem(lane, HD) < HD // 2
    mine = pl.ds(pl.multiple_of(d * rows, rows), rows)
    turn_cos, turn_sin = cosine[mine, :], sine[mine, :]

    def turned(pair, cos, sin, low):
        other = jnp.where(
            low, pltpu.roll(pair, 2 * HD - HD // 2, 1), pltpu.roll(pair, HD // 2, 1)
        )
        return pair * cos + other * sin

    raw_key = jnp.dot(own, wkv[0], preferred_element_type=f32)
    raw_value = jnp.dot(own, wkv[1], preferred_element_type=f32)
    for j in range(2):
        at = slice(j * 2 * HD, (j + 1) * 2 * HD)
        keys = turned(raw_key[:, at], turn_cos, turn_sin, first)
        values = raw_value[:, at]
        kv_own[2 * j] = jnp.where(lane < HD, keys, pltpu.roll(values, HD, 1)).astype(bf16)
        kv_own[2 * j + 1] = jnp.where(lane < HD, pltpu.roll(keys, HD, 1), values).astype(bf16)
    kv_all[c] = kv_own[g]

    def kv_copy(dz, other):
        return lambda: remote(
            kv_own.at[head_of(other)], kv_all.at[c], kv_send.at[dz, other], kv_recv.at[c],
            {"ctx": 4 * (z + dz) + other},
        )

    wq_relay(4 * z + 2 * (1 - y) + x, upper, lower, None)
    for dz in range(planes):
        for other in range(4):
            pred = (z + dz < planes) if dz else (d != other)
            copies.send(kv_copy(dz, other), pred)
    experts = meta.shape[0] // 2
    expert = lax.broadcasted_iota(jnp.int32, (experts, rows), 0)
    named, chosen = jnp.zeros((experts, rows), f32), jnp.zeros((experts, rows), f32)
    for t in range(routes.shape[0]):
        same = routes[t : t + 1, :] == expert
        named += jnp.where(same, 1.0, 0.0)
        chosen += jnp.where(same, weights_in[t : t + 1, :], 0.0)
    tri = (rows, rows)
    upto = lax.broadcasted_iota(jnp.int32, tri, 0) <= lax.broadcasted_iota(jnp.int32, tri, 1)
    place = jnp.dot(
        named.astype(bf16), jnp.where(upto, 1.0, 0.0).astype(bf16), preferred_element_type=f32
    )
    meta[:experts, :] = jnp.where(named > 0.5, place - 1.0, -1.0)
    meta[experts:, :] = chosen
    meta_all[c] = meta[...]
    for r in range(1, total):
        copies.send(
            lambda r=r: remote(
                meta, meta_all.at[c], meta_send.at[r], meta_recv.at[c],
                {"ctx": lax.rem(c + r, total)},
            )
        )

    def wo_rows(i):
        return pl.ds(pl.multiple_of(i * rows, rows), rows)

    wo_spans = spans(width, 640)

    def wo_hand(n):
        at, size = wo_spans[n]
        return remote(
            w_out.at[pl.ds(at, size), :], wo.at[pl.ds(at, size), wo_rows(d)],
            wo_plane.at[n], wo_recv.at[d, n], {"ctx": 4 * z + head_of(z)},
        )

    def wo_keep(n):
        at, size = wo_spans[n]
        return pltpu.make_async_copy(
            w_out.at[pl.ds(at, size), :], wo.at[pl.ds(at, size), wo_rows(d)], wo_recv.at[d, n]
        )

    for s in range(1, planes):
        for j in range(2):

            @pl.when(z >= s)
            def _(s=s, j=j):
                wq_relay(4 * (z - s) + 2 * j + x, upper, None, always)

            @pl.when(z + s < planes)
            def _(s=s, j=j):
                wq_relay(4 * (z + s) + 2 * j + x, None, lower, always)

        if s == 1:
            for n in range(len(wo_spans)):
                pl.when(g == z)(lambda n=n: wo_keep(n).start())
                copies.send(lambda n=n: wo_hand(n), g != z)

        if s == 2:
            opposite = jnp.bitwise_xor(d, 2)
            landed(normed.at[opposite], norm_recv.at[opposite])
            copies.send(
                lambda: remote(
                    normed.at[opposite], normed.at[opposite],
                    norm_send.at[2], norm_recv.at[opposite], partner,
                )
            )

    def wo_relay(n, j):
        at, size = wo_spans[n]
        i = 2 * j + x
        piece = wo.at[pl.ds(at, size), wo_rows(i)]
        landed(piece, wo_recv.at[i, n])
        for way, (where, pred) in enumerate(wo_ways()):
            copies_start(
                lambda way=way, where=where: remote(
                    piece, piece, wo_send.at[way, i, n], wo_recv.at[i, n], where
                ),
                pred,
            )

    def wo_ways():
        return (
            ({"ctx": c + 4}, upper & (z >= g)),
            ({"ctx": c - 4}, lower & (z <= g)),
            (peer, z != g),
        )

    def wo_stage(stage):
        for n in range(len(wo_spans)):
            for j in range(2):
                jj = jnp.bitwise_xor(j, y)
                if stage == 0:
                    pl.when(z == g)(lambda n=n, jj=jj: wo_relay(n, jj))
                for away in range(1, planes):
                    if stage == min(n + away, 5):
                        pl.when(jnp.abs(z - g) == away)(lambda n=n, jj=jj: wo_relay(n, jj))

    for r in (1, 3):
        other = jnp.bitwise_xor(d, r)
        landed(normed.at[other], norm_recv.at[other])
    for t in range(4):
        block = normed[t]
        for j in range(total):
            lhs[j, t * rows : (t + 1) * rows, :] = block[:, j * wq_rows : (j + 1) * wq_rows]

    wo_stage(0)
    raw[...] = jnp.zeros_like(raw)

    def query_rows(plane):
        for i in range(4):
            who = 4 * plane + i
            raw[...] += jnp.dot(lhs[who], wq[who], preferred_element_type=f32)

    query_rows_wait = lambda plane, i: landed(wq.at[4 * plane + i], wq_recv.at[4 * plane + i])
    for i in range(2):
        query_rows_wait(z, 2 * i + 1 - x)
    query_rows(z)
    for s in range(1, planes):
        for step in (-s, s):

            @pl.when((z + step >= 0) & (z + step < planes))
            def _(step=step):
                for i in range(2):
                    query_rows_wait(z + step, 2 * i + 1 - x)
                query_rows(z + step)

    ends = [lengths[0]]
    for i in range(1, lengths.shape[0]):
        ends.append(ends[-1] + lengths[i])

    def segment(start, shape):
        place = start + lax.broadcasted_iota(jnp.int32, shape, 0)
        found = jnp.zeros(shape, jnp.int32)
        for end in ends:
            found += (place >= end).astype(jnp.int32)
        return found

    wide = (plane_rows, 2 * HD)
    wide_lane = lax.broadcasted_iota(jnp.int32, wide, 1)
    mark = jnp.where(
        (wide_lane - HD == segment(z * plane_rows, wide)) & (wide_lane >= HD), 1.0, 0.0
    )
    wide_first = lax.rem(wide_lane, HD) < HD // 2

    for j in range(heads // 2):
        pair = turned(
            raw[:, j * 2 * HD : (j + 1) * 2 * HD], cosine[...], sine[...], wide_first
        ) * (SCALE * LOG2E)
        qx[2 * j] = jnp.where(wide_lane < HD, pair, mark).T.astype(bf16)
        qx[2 * j + 1] = jnp.where(wide_lane < HD, pltpu.roll(pair, HD, 1), mark).T.astype(bf16)

    def unpack(i, carry):
        @pl.when(i != c)
        def _():
            landed(kv_all.at[i], kv_recv.at[i])

        both = kv_all[i].astype(f32)
        apart = jnp.where(
            (lane - HD == segment(i * rows, lane.shape)) | (lane >= HD + len(ends)), 0.0, NEGATIVE
        )
        at = pl.ds(pl.multiple_of(i * rows, rows), rows)
        kx[at, :] = jnp.where(lane < HD, both, apart).astype(bf16)
        ones = jnp.where(lane == HD, 1.0, 0.0)
        vx[:, at] = jnp.where(lane < HD, pltpu.roll(both, HD, 1), ones).T[: vx.shape[0]].astype(bf16)
        return carry

    lax.fori_loop(0, 4 * (z + 1), unpack, 0)
    square = (plane_rows, plane_rows)
    bias[...] = jnp.where(
        lax.broadcasted_iota(jnp.int32, square, 0) <= lax.broadcasted_iota(jnp.int32, square, 1),
        0.0, NEGATIVE,
    )

    wo_stage(1)

    def attend(h):
        count_row = lax.broadcasted_iota(jnp.int32, acc.shape[1:], 0) == HD
        for e in range(2):
            top[e] = jnp.full(top.shape[1:], sinks[g * heads + h + e] * LOG2E, f32)
            acc[e] = jnp.where(count_row, 1.0, 0.0)

        def block(b, last):
            at = pl.ds(pl.multiple_of(b * plane_rows, plane_rows), plane_rows)
            scores = [
                jnp.dot(kx[at, :], qx[h + e], preferred_element_type=f32) for e in range(2)
            ]
            for e in range(2):
                score = scores[e] + bias[...] if last else scores[e]
                old = top[e]
                new = jnp.maximum(old, jnp.max(score, axis=0, keepdims=True))
                weights = jnp.exp2(score - new).astype(bf16)
                acc[e] = acc[e] * jnp.exp2(old - new) + jnp.dot(
                    vx[:, at], weights, preferred_element_type=f32
                )
                top[e] = new

        def body(b, carry):
            block(b, False)
            return carry

        lax.fori_loop(0, z, body, 0)
        block(z, True)
        for e in range(2):
            at = pl.ds(pl.multiple_of((h + e) * HD, HD), HD)
            attended[at, :] = (acc[e, :HD, :] / acc[e, HD : HD + 1, :]).astype(bf16)

    def pair_of_heads(j, carry):
        for stage in range(1, heads // 2):
            pl.when(j == stage)(lambda stage=stage: wo_stage(stage + 1))
        attend(2 * j)
        return carry

    lax.fori_loop(0, heads // 2, pair_of_heads, 0)
    wo_stage(5)

    lhs_out = attended[...].T
    give, keep = 1 - k, k

    def k_copy(n):
        at, size = wo_spans[n]
        return remote(
            k_out.at[:, :, pl.ds(at, size)], k_in.at[:, :, pl.ds(at, size)],
            k_send.at[n], k_recv.at[n], partner,
        )

    def y_copy(n):
        at, size = wo_spans[n]
        return remote(
            y_out.at[:, pl.ds(at, size)], y_in.at[:, pl.ds(at, size)],
            y_send.at[n], y_recv.at[n], across,
        )

    def project(n):
        at, size = wo_spans[n]
        cols = pl.ds(at, size)
        for j in range(2):
            i = 2 * j + 1 - x
            landed(wo.at[cols, wo_rows(i)], wo_recv.at[i, n])
        part[:, :size] = lax.dot_general(
            lhs_out, wo[cols, :], (((1,), (1,)), ((), ())), preferred_element_type=f32
        )
        for j in range(2):
            k_out[j, :, cols] = part[wo_rows(2 * j + give), :size].astype(bf16)
            held[j, :, cols] = part[wo_rows(2 * j + keep), :size]
        copies.send(lambda: k_copy(n))

    def fold(n):
        at, size = wo_spans[n]
        cols = pl.ds(at, size)
        k_copy(n).wait_recv()
        y_out[:, cols] = (held[1 - y, :, cols] + k_in[1 - y, :, cols].astype(f32)).astype(bf16)
        copies.send(lambda: y_copy(n))

    def finish(n):
        at, size = wo_spans[n]
        cols = pl.ds(at, size)
        mine = held[y, :, cols] + k_in[y, :, cols].astype(f32) + tokens[:, cols].astype(f32)
        y_copy(n).wait_recv()
        mixed_out[:, cols] = (mine + y_in[:, cols].astype(f32)).astype(bf16)

    count = len(wo_spans)
    for n in range(count):
        project(n)
        fold(n)
    for n in range(count):
        finish(n)
    expert_in[...] = rms_scale(mixed_out[...], moe_gain[...][None, :])

    def meta_arrived(i, carry):
        @pl.when(i != c)
        def _():
            landed(meta_all.at[i], meta_recv.at[i])

        return carry

    lax.fori_loop(0, total, meta_arrived, 0)
    copies.drain()

    def wq_drain(who, ways):
        for i, pred in enumerate(ways):
            pl.when(pred)(
                lambda i=i: remote(
                    wq.at[who], wq.at[who], wq_send.at[i, who], wq_recv.at[who], partner
                ).wait_send()
            )

    never = z < 0
    for j in range(2):
        wq_drain(4 * z + 2 * j + x, (upper, lower))
    for s in range(1, planes):
        for j in range(2):
            pl.when(z >= s)(
                lambda s=s, j=j: wq_drain(4 * (z - s) + 2 * j + x, (upper, never, always))
            )
            pl.when(z + s < planes)(
                lambda s=s, j=j: wq_drain(4 * (z + s) + 2 * j + x, (never, lower, always))
            )
    for n, (at, size) in enumerate(wo_spans):
        for j in range(2):
            i = 2 * j + x
            piece = wo.at[pl.ds(at, size), wo_rows(i)]
            for way, (where, pred) in enumerate(wo_ways()):
                pl.when(pred)(
                    lambda way=way, where=where: remote(
                        piece, piece, wo_send.at[way, i, n], wo_recv.at[i, n], where
                    ).wait_send()
                )


def front(tokens, lengths, attn_gain, w_query, w_key, w_value, sinks, w_out, moe_gain, routes, weights):
    bf16, f32 = jnp.bfloat16, jnp.float32
    rows, width = tokens.shape
    devices = lax.axis_size("ctx")
    planes = devices // 4
    seq = devices * rows
    quarter = w_query.shape[1] // 4
    heads = quarter // HD
    count = len(spans(width, 640))
    place = np.arange(seq, dtype=np.float32)
    freqs = np.float32(THETA) ** (-np.arange(HD // 2, dtype=np.float32) / np.float32(HD // 2))
    angles = place[:, None] * freqs[None, :].astype(np.float32)
    cos, sin = np.cos(angles).astype(np.float32), np.sin(angles).astype(np.float32)
    tables = np.stack(
        [np.tile(cos, (1, 4)), np.tile(np.concatenate([-sin, sin], axis=1), (1, 2))]
    )
    meta_shape = (devices, rows)
    dma = pltpu.SemaphoreType.DMA
    vmem = pltpu.VMEM
    return pl.pallas_call(
        functools.partial(front_kernel, planes),
        out_shape=[
            jax.ShapeDtypeStruct((rows, width), bf16),
            jax.ShapeDtypeStruct((rows, width), bf16),
            jax.ShapeDtypeStruct((devices,) + meta_shape, f32),
        ],
        in_specs=[VMEM, SMEM, VMEM, ANY, ANY, ANY, SMEM, ANY, VMEM, ANY, VMEM, VMEM],
        out_specs=[VMEM] * 3,
        scratch_shapes=[
            vmem((rows, width), bf16),
            vmem((2, 4 * rows, 2 * HD), f32),
            vmem(meta_shape, f32),
            vmem((4, rows, width), bf16),
            vmem((devices, w_query.shape[0], quarter), bf16),
            vmem((2,) + w_key.shape, bf16),
            vmem((4, rows, 2 * HD), bf16),
            vmem((devices, rows, 2 * HD), bf16),
            vmem((devices, 4 * rows, w_query.shape[0]), bf16),
            vmem((4 * rows, quarter), f32),
            vmem((heads, 2 * HD, 4 * rows), bf16),
            vmem((seq, 2 * HD), bf16),
            vmem((HD + 16, seq), bf16),
            vmem((4 * rows, 4 * rows), f32),
            vmem((2, 1, 4 * rows), f32),
            vmem((2, HD + 16, 4 * rows), f32),
            vmem((quarter, 4 * rows), bf16),
            vmem((width, 4 * rows), bf16),
            vmem((4 * rows, 1024), f32),
            vmem((2, rows, width), f32),
            vmem((2, rows, width), bf16),
            vmem((2, rows, width), bf16),
            vmem((rows, width), bf16),
            vmem((rows, width), bf16),
            dma((3,)),
            dma((devices,)), dma((4,)), dma((3, devices)),
            dma((4,)), dma((3,)),
            dma((devices,)), dma((planes, 4)),
            dma((devices,)), dma((devices,)),
            dma((4, count)), dma((count,)), dma((3, 4, count)),
            dma((count,)), dma((count,)), dma((count,)), dma((count,)),
        ],
        compiler_params=pltpu.CompilerParams(
            collective_id=4, has_side_effects=True, vmem_limit_bytes=LIMIT
        ),
    )(
        tokens.T, lengths, attn_gain, w_query, w_key, w_value, sinks, w_out.T,
        moe_gain, jnp.asarray(tables), routes.T, weights.T,
    )


def call(kernel, chips, out_shape, scratch, identity, *args, smem=(), hbm=()):
    single = not isinstance(out_shape, (list, tuple))
    return pl.pallas_call(
        functools.partial(kernel, chips),
        out_shape=out_shape,
        in_specs=[
            pl.BlockSpec(memory_space=pltpu.SMEM)
            if i in smem
            else pl.BlockSpec(memory_space=pl.ANY)
            if i in hbm
            else VMEM
            for i in range(len(args))
        ],
        out_specs=VMEM if single else [VMEM] * len(out_shape),
        scratch_shapes=scratch,
        compiler_params=pltpu.CompilerParams(
            collective_id=identity, has_side_effects=True, vmem_limit_bytes=LIMIT
        ),
    )(*args)


def ring_front(
    tokens, lengths, attn_gain, w_query, w_key, w_value, sinks, w_out, moe_gain, routes,
    route_weights,
):
    bf16, f32 = jnp.bfloat16, jnp.float32
    tok_rows, width = tokens.shape
    devices = lax.axis_size("ctx")
    chips = devices // 2
    me = lax.axis_index("ctx")
    q_cols = w_query.shape[1]
    num_heads = q_cols // HD
    kv_cols = w_key.shape[1]
    kv_heads = kv_cols // HD
    experts = chips
    member = routes[:, :, None] == jnp.arange(experts, dtype=jnp.int32)[None, None, :]
    named = jnp.any(member, axis=1)
    lower = jnp.tril(jnp.ones((tok_rows, tok_rows), bf16))
    slot = jnp.dot(lower, named.astype(bf16), preferred_element_type=f32) - 1.0
    slot = jnp.where(named, slot, -1.0)
    routed_weight = jnp.sum(jnp.where(member, route_weights[:, :, None], 0.0), axis=1)
    meta = jnp.concatenate([slot, routed_weight], axis=1).T

    positions = me * tok_rows + jnp.arange(tok_rows, dtype=jnp.int32)
    freqs = THETA ** (-jnp.arange(HD // 2, dtype=f32) / (HD // 2))
    angles = positions.astype(f32)[:, None] * freqs[None, :]
    cosine, sine = jnp.cos(angles)[:, None, :], jnp.sin(angles)[:, None, :]

    def rotate(values):
        first, second = values[..., : HD // 2], values[..., HD // 2 :]
        return jnp.concatenate(
            [first * cosine - second * sine, second * cosine + first * sine], axis=-1
        ).astype(bf16)

    normed = rms_scale(tokens, attn_gain)
    raw_key = jnp.dot(normed, w_key, preferred_element_type=f32)
    value = jnp.dot(normed, w_value, preferred_element_type=f32).astype(bf16)
    key = rotate(raw_key.reshape(tok_rows, kv_heads, HD)).reshape(tok_rows, kv_cols)
    kv = jnp.concatenate([key, value], axis=1)
    lhs = normed.reshape(tok_rows, devices, width // devices).transpose(1, 0, 2)
    raw_query, kv_all, meta_all = call(
        query_kernel,
        chips,
        [
            jax.ShapeDtypeStruct((tok_rows, q_cols), f32),
            jax.ShapeDtypeStruct((devices,) + kv.shape, bf16),
            jax.ShapeDtypeStruct((devices,) + meta.shape, f32),
        ],
        [pltpu.VMEM((devices,) + w_query.shape, bf16)] + gather_sems(5, chips),
        0,
        lhs, kv, meta, w_query,
    )
    cosine_pair = jnp.tile(cosine[:, 0, :], (1, 4))
    sine_pair = jnp.tile(jnp.concatenate([-sine[:, 0, :], sine[:, 0, :]], axis=1), (1, 2))
    doc_ends = jnp.dot(jnp.tril(jnp.ones((lengths.size,) * 2, jnp.int32)), lengths)
    start = jnp.max(
        jnp.where(positions[:, None] >= doc_ends[None, :], doc_ends[None, :], 0), axis=1
    )[:, None]
    mixed, expert_in = call(
        attend_kernel,
        chips,
        [jax.ShapeDtypeStruct((tok_rows, width), bf16)] * 2,
        [
            pltpu.VMEM((tok_rows, width), f32),
            pltpu.VMEM((devices,) + w_out.shape, bf16),
            pltpu.VMEM((tok_rows, devices * tok_rows), f32),
            pltpu.VMEM((num_heads, tok_rows, HD), bf16),
            pltpu.VMEM((kv_heads, devices * tok_rows, HD), bf16),
            pltpu.VMEM((kv_heads, devices * tok_rows, HD), bf16),
            pltpu.VMEM((devices, tok_rows, w_out.shape[0]), bf16),
        ]
        + gather_sems(3, chips),
        1,
        raw_query, kv_all, cosine_pair, sine_pair, sinks, start, w_out, tokens, moe_gain[None, :],
        smem=(4,),
    )
    return mixed, expert_in, meta_all


def per_device(
    tokens, lengths, attn_gain, w_query, w_key, w_value, sinks, w_out, moe_gain, routes,
    route_weights, w_gate, w_up, w_down,
):
    bf16, f32 = jnp.bfloat16, jnp.float32
    tok_rows, width = tokens.shape
    devices = lax.axis_size("ctx")
    chips = devices // 2
    me = lax.axis_index("ctx")
    experts = chips
    capacity = tok_rows * 4 * 17 // (16 * experts)
    padded = -(-capacity // 16) * 16

    square = lax.axis_size("groups") == 2 and devices == 16
    mixed, expert_in, meta_all = (front if square else ring_front)(
        tokens, lengths, attn_gain, w_query, w_key, w_value, sinks, w_out, moe_gain, routes,
        route_weights,
    )
    partial = call(
        expert_kernel,
        chips,
        jax.ShapeDtypeStruct((devices, padded, width), bf16),
        [
            pltpu.VMEM((devices, tok_rows, width), bf16),
            pltpu.VMEM((4 * padded, width), bf16),
            pltpu.VMEM((4 * padded, w_gate.shape[2]), bf16),
            pltpu.VMEM(w_gate.shape[1:], bf16),
            pltpu.VMEM(w_up.shape[1:], bf16),
            pltpu.VMEM(w_down.shape[:0:-1], bf16),
            pltpu.SemaphoreType.DMA((3,)),
        ]
        + gather_sems(2, chips),
        2,
        expert_in, meta_all, w_gate[0], w_up[0], w_down[0].T,
        hbm=(2, 3, 4),
    )
    return call(
        combine_kernel,
        chips,
        jax.ShapeDtypeStruct((tok_rows, width), bf16),
        [pltpu.VMEM((chips, tok_rows, width), bf16)] * 2
        + [pltpu.VMEM((chips - 1, tok_rows, width), bf16)] * 2
        + ring_sems(2, chips),
        3,
        partial, meta_all, mixed,
    )


def solution(mesh):
    placed = (
        P(("groups", "ctx"), None),
        P("groups"),
        P(),
        P("ctx", None),
        P(),
        P(),
        P(),
        P("ctx", None),
        P(),
        P(("groups", "ctx"), None),
        P(("groups", "ctx"), None),
        P("ctx", None, None),
        P("ctx", None, None),
        P("ctx", None, None),
    )
    return jax.shard_map(
        per_device,
        mesh=mesh,
        in_specs=placed,
        out_specs=P(("groups", "ctx"), None),
        check_vma=False,
    )
```
